256 devices in a mesh: segment: 4 (over x), shard: 64 (over y, z, core).
Axes of the slice: x: 4, y: 4, z: 8, core: 2. Of those that a mesh axis runs over, the one named last changes fastest.
Arguments:
- tokens: bfloat16 [3, 128, 3072], P(None, 'shard'), may hold values from -6 to 6
- norm_gain: float32 [4, 3072], P('segment'), may hold values from 0.5 to 1.5
- w_gate: bfloat16 [4, 3072, 32768], P('segment', None, 'shard'), may hold values from -0.109375 to 0.109375
- w_up: bfloat16 [4, 3072, 32768], P('segment', None, 'shard'), may hold values from -0.109375 to 0.109375
- w_down: bfloat16 [4, 32768, 3072], P('segment', 'shard'), may hold values from -0.046875 to 0.046875
- block_counts: int32 [4], P('segment'), may hold values from 1 to 2
- gate_prob: float32 [4, 3, 128], P('segment', None, 'shard'), may hold values from 0.1 to 1
Outputs:
- section_outputs: bfloat16 [4, 3, 128, 3072], P('segment', None, 'shard')
The draws below stay inside these ranges and needn't reach their ends.
All inputs are finite; a program needn't handle non-finite values.
Results may differ from the reference program's by a relative error of at most 0.009.
Values may be sent and summed in bfloat16 or wider, within the bound.
A program may use at most 64 MiB of HBM per device.

```python
import math
import jax
import jax.numpy as jnp
from jax import lax

D = 3072
FF = 16384
EXPERTS = 2
BLOCK_ROWS = 128
BLOCKS = 3
SECTIONS = 4


def draw_block_counts(key, part):
    key_base, key_order = jax.random.split(key)
    drawn = jax.random.randint(key_base, (SECTIONS,), 1, BLOCKS)
    order = jax.random.permutation(key_order, SECTIONS)
    drawn = jnp.where(order == 0, 1, drawn)
    drawn = jnp.where(order == 1, BLOCKS - 1, drawn)
    return drawn.astype(jnp.int32)


def levels(rng, shape, pieces, least, top_value):
    def one(position, parts):
        draws = jax.random.uniform(jax.random.fold_in(jax.random.fold_in(rng, 6), position), (parts,), jnp.float32, least / len(pieces), top_value / len(pieces))
        return jnp.repeat(jnp.exp(draws), shape[position] // parts).reshape((-1,) + (1,) * (len(shape) - position - 1))

    factor_of = one(*pieces[0])
    for cut in pieces[1:]:
        factor_of = factor_of * one(*cut)
    return factor_of


def noise(stream_key, extent, spread, most, cuts=(), kind=jnp.bfloat16):
    level = levels(stream_key, extent, cuts, -0.22, 0.18) if cuts else 1.0
    array = jax.random.normal(stream_key, extent, jnp.float32) * spread * level
    return jnp.minimum(jnp.maximum(array, -most), most).astype(kind)


def setup_inputs(seed: int = 0) -> dict:
    arg_keys = jax.random.split(jax.random.key(seed), 8)
    tokens = noise(arg_keys[0], (BLOCKS, BLOCK_ROWS, D), 1.0, 6.0, ((1, 64),))
    norm_gain = jnp.clip(1.0 + 0.1 * jax.random.normal(arg_keys[1], (SECTIONS, D), jnp.float32), 0.5, 1.5)
    w_gate = noise(arg_keys[2], (SECTIONS, D, EXPERTS * FF), D ** -0.5, 0.109375, ((0, 4), (2, 64)))
    w_up = noise(arg_keys[3], (SECTIONS, D, EXPERTS * FF), D ** -0.5, 0.109375, ((0, 4), (2, 64)))
    w_down = noise(arg_keys[4], (SECTIONS, EXPERTS * FF, D), FF ** -0.5, 0.046875, ((0, 4), (1, 64)))
    block_counts = draw_block_counts(jax.random.fold_in(arg_keys[7], 71), 0)
    gate_prob = jnp.clip(jnp.exp(math.log(1.0) - 2.3025851 * jax.random.uniform(arg_keys[6], (SECTIONS, BLOCKS, BLOCK_ROWS), jnp.float32) ** levels(arg_keys[6], (SECTIONS, BLOCKS, BLOCK_ROWS), ((0, 4), (2, 64)), -0.2, 0.2)), 0.1, 1.0)
    return dict(tokens=tokens, norm_gain=norm_gain, w_gate=w_gate, w_up=w_up, w_down=w_down, block_counts=block_counts, gate_prob=gate_prob)


def normalize(values, row_gain):
    scale = jax.lax.rsqrt(lax.optimization_barrier(jnp.mean(values * values, axis=-1, keepdims=True)) + 1e-05)
    return (values * scale * row_gain).astype(jnp.bfloat16)

def reference(tokens, norm_gain, w_gate, w_up, w_down, block_counts, gate_prob):
    carried = tokens
    results = []
    block_ids = jnp.arange(BLOCKS, dtype=jnp.int32)
    for section in range(SECTIONS):
        values = carried.astype(jnp.float32)
        normed = normalize(values, norm_gain[section]).reshape(BLOCKS * BLOCK_ROWS, D)
        outputs = []
        for expert in range(EXPERTS):
            gate_val = jnp.dot(normed, w_gate[section, :, expert * FF:(expert + 1) * FF], preferred_element_type=jnp.float32)
            up_val = jnp.dot(normed, w_up[section, :, expert * FF:(expert + 1) * FF], preferred_element_type=jnp.float32)
            hidden = (jax.nn.silu(gate_val) * up_val).astype(jnp.bfloat16)
            outputs.append(jnp.dot(hidden, w_down[section, expert * FF:(expert + 1) * FF, :], preferred_element_type=jnp.float32).reshape(BLOCKS, BLOCK_ROWS, D))
        first_expert = (block_ids < block_counts[section])[:, None, None]
        expert_out = jnp.where(first_expert, outputs[0], outputs[1])
        updated = (values + gate_prob[section][:, :, None] * expert_out).astype(jnp.bfloat16)
        results.append(updated)
        carried = updated
    return jnp.stack(results)
```

```python
import functools

import jax
import jax.numpy as jnp
from jax import lax
from jax.experimental import pallas as pl
from jax.experimental.pallas import tpu as pltpu
from jax.sharding import PartitionSpec as P

FF = 16384
LANES = 128


def shifted(value, axis, steps):
    count = lax.axis_size(axis)
    initial, last = (max(0, -steps), min(count, count - steps))
    return lax.ppermute(value, axis, [(source, source + steps) for source in range(initial, last)])


def normalize(rows, row_gain):
    values = rows.astype(jnp.float32)
    scale = lax.rsqrt(jnp.mean(values * values, axis=-1, keepdims=True) + 1e-05)
    return (values * scale * row_gain).astype(jnp.bfloat16)


def exchange_kernel(count, per_expert, x_ref, o_ref, send_sem, recv_sem):
    me = lax.axis_index("shard")
    segment = lax.axis_index("segment")

    def source(dest):
        return x_ref.at[dest // per_expert] if per_expert else x_ref.at[dest]

    def copy_to(dest):
        return pltpu.make_async_remote_copy(
            src_ref=source(dest),
            dst_ref=o_ref.at[me],
            send_sem=send_sem.at[dest],
            recv_sem=recv_sem.at[me],
            device_id=(segment, dest),
            device_id_type=pl.DeviceIdType.MESH,
        )

    def start(step, carry):
        copy_to(lax.rem(me + step, count)).start()
        return carry

    lax.fori_loop(1, count, start, 0)
    o_ref[me] = source(me)[...]

    def finish(step, carry):
        copy_to(lax.rem(me + step, count)).wait_send()
        origin = lax.rem(me + count - step, count)
        pltpu.make_async_remote_copy(
            src_ref=source(origin),
            dst_ref=o_ref.at[origin],
            send_sem=send_sem.at[origin],
            recv_sem=recv_sem.at[origin],
            device_id=(segment, origin),
            device_id_type=pl.DeviceIdType.MESH,
        ).wait_recv()
        return carry

    lax.fori_loop(1, count, finish, 0)


def exchange(pieces, count, per_expert):
    rows, lanes = pieces.shape[1], pieces.shape[2]
    return pl.pallas_call(
        functools.partial(exchange_kernel, count, per_expert),
        out_shape=jax.ShapeDtypeStruct((count, rows, lanes), pieces.dtype),
        in_specs=[pl.BlockSpec(memory_space=pltpu.VMEM)],
        out_specs=pl.BlockSpec(memory_space=pltpu.VMEM),
        scratch_shapes=[pltpu.SemaphoreType.DMA((count,)), pltpu.SemaphoreType.DMA((count,))],
        compiler_params=pltpu.CompilerParams(has_side_effects=True),
    )(pieces)


def shards(tokens, norm_gain, w_gate, w_up, w_down, block_counts, gate_prob):
    segment_index = lax.axis_index("segment")
    segment_count = lax.axis_size("segment")
    shard_count = lax.axis_size("shard")
    hidden_count = w_gate.shape[2]
    per_expert = FF // hidden_count
    zero_blocks = block_counts[0]
    row_gain = norm_gain[0]
    gate_part = w_gate[0]
    up_part = w_up[0]
    down_part = w_down[0]
    probs = gate_prob[0]
    local_rows = tokens.shape[1]
    width = tokens.shape[2]
    piece_rows = 2 * local_rows * width // LANES
    carried = tokens
    stored = jnp.zeros_like(tokens)
    for tick in range(segment_count):
        normed = normalize(carried, row_gain)
        pieces = jnp.stack([normed[0:2], normed[1:3]]).reshape(2, piece_rows, LANES)
        gathered = exchange(pieces, shard_count, per_expert)
        block_rows = gathered.reshape(shard_count * 2 * local_rows, width)
        gate_val = jnp.dot(block_rows, gate_part, preferred_element_type=jnp.float32)
        up_val = jnp.dot(block_rows, up_part, preferred_element_type=jnp.float32)
        hidden = (jax.nn.silu(gate_val) * up_val).astype(jnp.bfloat16)
        partial_sum = jnp.dot(hidden, down_part, preferred_element_type=jnp.float32)
        received = exchange(partial_sum.reshape(shard_count, piece_rows, LANES), shard_count, 0)
        received = received.reshape(2, shard_count // 2, 2, local_rows, width)
        first, second = jnp.sum(received[0], axis=0), jnp.sum(received[1], axis=0)
        middle = jnp.where(zero_blocks >= 2, first[1], second[0])
        mixed = jnp.stack([first[0], middle, second[1]])
        updated = (carried.astype(jnp.float32) + probs[:, :, None] * mixed).astype(jnp.bfloat16)
        stored = jnp.where(segment_index == tick, updated, stored)
        if tick + 1 < segment_count:
            carried = shifted(updated, "segment", 1)
    return stored[None]


def solution(mesh):
    placed = (
        P(None, "shard", None),
        P("segment", None),
        P("segment", None, "shard"),
        P("segment", None, "shard"),
        P("segment", "shard", None),
        P("segment"),
        P("segment", None, "shard"),
    )
    return jax.shard_map(
        shards,
        mesh=mesh,
        in_specs=placed,
        out_specs=P("segment", None, "shard", None),
        check_vma=False,
    )
```

```python
import functools

import jax
import jax.numpy as jnp
from jax import lax
from jax.experimental import pallas as pl
from jax.experimental.pallas import tpu as pltpu
from jax.sharding import PartitionSpec as P

FF = 16384
LANES = 128


def shifted(value, axis, steps):
    count = lax.axis_size(axis)
    initial, last = (max(0, -steps), min(count, count - steps))
    return lax.ppermute(value, axis, [(source, source + steps) for source in range(initial, last)])


def normalize(rows, row_gain):
    values = rows.astype(jnp.float32)
    scale = lax.rsqrt(jnp.mean(values * values, axis=-1, keepdims=True) + 1e-05)
    return (values * scale * row_gain).astype(jnp.bfloat16)


def chip_exchange_kernel(chips, per_expert, x_ref, o_ref, send_sem, recv_sem):
    me = lax.axis_index("shard")
    segment = lax.axis_index("segment")
    core = lax.rem(me, 2)
    chip = me // 2

    def source(dest_chip):
        return x_ref.at[dest_chip // per_expert] if per_expert else x_ref.at[dest_chip]

    def copy_of(dest_chip, slot):
        return pltpu.make_async_remote_copy(
            src_ref=source(dest_chip),
            dst_ref=o_ref.at[slot],
            send_sem=send_sem.at[dest_chip],
            recv_sem=recv_sem.at[slot],
            device_id=(segment, dest_chip * 2 + core),
            device_id_type=pl.DeviceIdType.MESH,
        )

    def start(step, carry):
        copy_of(lax.rem(chip + step, chips), chip).start()
        return carry

    lax.fori_loop(1, chips, start, 0)
    o_ref[chip] = source(chip)[...]

    def finish(step, carry):
        copy_of(lax.rem(chip + step, chips), chip).wait_send()
        copy_of(lax.rem(chip + chips - step, chips), lax.rem(chip + chips - step, chips)).wait_recv()
        return carry

    lax.fori_loop(1, chips, finish, 0)


def chip_exchange(pieces, chips, per_expert):
    rows, lanes = pieces.shape[1], pieces.shape[2]
    return pl.pallas_call(
        functools.partial(chip_exchange_kernel, chips, per_expert),
        out_shape=jax.ShapeDtypeStruct((chips, rows, lanes), pieces.dtype),
        in_specs=[pl.BlockSpec(memory_space=pltpu.VMEM)],
        out_specs=pl.BlockSpec(memory_space=pltpu.VMEM),
        scratch_shapes=[pltpu.SemaphoreType.DMA((chips,)), pltpu.SemaphoreType.DMA((chips,))],
        compiler_params=pltpu.CompilerParams(has_side_effects=True),
    )(pieces)


def pair_exchange_kernel(x_ref, o_ref, send_sem, recv_sem):
    me = lax.axis_index("shard")
    segment = lax.axis_index("segment")
    copy = pltpu.make_async_remote_copy(
        src_ref=x_ref,
        dst_ref=o_ref,
        send_sem=send_sem,
        recv_sem=recv_sem,
        device_id=(segment, me + 1 - 2 * lax.rem(me, 2)),
        device_id_type=pl.DeviceIdType.MESH,
    )
    copy.start()
    copy.wait()


def pair_exchange(value):
    return pl.pallas_call(
        pair_exchange_kernel,
        out_shape=jax.ShapeDtypeStruct(value.shape, value.dtype),
        in_specs=[pl.BlockSpec(memory_space=pltpu.VMEM)],
        out_specs=pl.BlockSpec(memory_space=pltpu.VMEM),
        scratch_shapes=[pltpu.SemaphoreType.DMA(()), pltpu.SemaphoreType.DMA(())],
        compiler_params=pltpu.CompilerParams(has_side_effects=True),
    )(value)


def shards(tokens, norm_gain, w_gate, w_up, w_down, block_counts, gate_prob):
    segment_index = lax.axis_index("segment")
    segment_count = lax.axis_size("segment")
    shard_count = lax.axis_size("shard")
    hidden_count = w_gate.shape[2]
    per_expert = FF // hidden_count
    zero_blocks = block_counts[0]
    row_gain = norm_gain[0]
    gate_part = w_gate[0]
    up_part = w_up[0]
    down_part = w_down[0]
    probs = gate_prob[0]
    local_rows = tokens.shape[1]
    width = tokens.shape[2]
    piece_rows = 2 * local_rows * width // LANES
    chips = shard_count // 2
    carried = tokens
    stored = jnp.zeros_like(tokens)
    for tick in range(segment_count):
        normed = normalize(carried, row_gain)
        pieces = jnp.stack([normed[0:2], normed[1:3]]).reshape(2, piece_rows, LANES)
        own_core = chip_exchange(pieces, chips, per_expert // 2)
        other_core = pair_exchange(own_core)
        block_rows = jnp.concatenate([own_core, other_core]).reshape(shard_count * 2 * local_rows, width)
        gate_val = jnp.dot(block_rows, gate_part, preferred_element_type=jnp.float32)
        up_val = jnp.dot(block_rows, up_part, preferred_element_type=jnp.float32)
        hidden = (jax.nn.silu(gate_val) * up_val).astype(jnp.bfloat16)
        partial_sum = jnp.dot(hidden, down_part, preferred_element_type=jnp.float32)
        partial_sum = partial_sum.reshape(2, chips, piece_rows, LANES)
        chip_sum = partial_sum[0] + pair_exchange(partial_sum[1])
        received = chip_exchange(chip_sum.astype(jnp.bfloat16), chips, 0).astype(jnp.float32)
        received = received.reshape(2, chips // 2, 2, local_rows, width)
        first, second = jnp.sum(received[0], axis=0), jnp.sum(received[1], axis=0)
        middle = jnp.where(zero_blocks >= 2, first[1], second[0])
        mixed = jnp.stack([first[0], middle, second[1]])
        updated = (carried.astype(jnp.float32) + probs[:, :, None] * mixed).astype(jnp.bfloat16)
        stored = jnp.where(segment_index == tick, updated, stored)
        if tick + 1 < segment_count:
            carried = shifted(updated, "segment", 1)
    return stored[None]


def solution(mesh):
    placed = (
        P(None, "shard", None),
        P("segment", None),
        P("segment", None, "shard"),
        P("segment", None, "shard"),
        P("segment", "shard", None),
        P("segment"),
        P("segment", None, "shard"),
    )
    return jax.shard_map(
        shards,
        mesh=mesh,
        in_specs=placed,
        out_specs=P("segment", None, "shard", None),
        check_vma=False,
    )
```

```python
import functools

import jax
import jax.numpy as jnp
from jax import lax
from jax.experimental import pallas as pl
from jax.experimental.pallas import tpu as pltpu
from jax.sharding import PartitionSpec as P

FF = 16384
LANES = 128


def shifted(value, axis, steps):
    count = lax.axis_size(axis)
    initial, last = (max(0, -steps), min(count, count - steps))
    return lax.ppermute(value, axis, [(source, source + steps) for source in range(initial, last)])


def normalize(rows, row_gain):
    values = rows.astype(jnp.float32)
    scale = lax.rsqrt(jnp.mean(values * values, axis=-1, keepdims=True) + 1e-05)
    return (values * scale * row_gain).astype(jnp.bfloat16)


def chip_exchange_kernel(chips, per_expert, x_ref, o_ref, send_sem, recv_sem):
    me = lax.axis_index("shard")
    segment = lax.axis_index("segment")
    core = lax.rem(me, 2)
    chip = me // 2
    barrier = pltpu.get_barrier_semaphore()

    def greet(step, carry):
        dest = lax.rem(chip + step, chips) * 2 + core
        pl.semaphore_signal(barrier, 1, device_id=(segment, dest), device_id_type=pl.DeviceIdType.MESH)
        return carry

    lax.fori_loop(1, chips, greet, 0)
    pl.semaphore_wait(barrier, chips - 1)

    def source(dest_chip):
        return x_ref.at[dest_chip // per_expert] if per_expert else x_ref.at[dest_chip]

    def copy_of(dest_chip, slot):
        return pltpu.make_async_remote_copy(
            src_ref=source(dest_chip),
            dst_ref=o_ref.at[slot],
            send_sem=send_sem.at[dest_chip],
            recv_sem=recv_sem.at[slot],
            device_id=(segment, dest_chip * 2 + core),
            device_id_type=pl.DeviceIdType.MESH,
        )

    def start(step, carry):
        copy_of(lax.rem(chip + step, chips), chip).start()
        return carry

    lax.fori_loop(1, chips, start, 0)
    o_ref[chip] = source(chip)[...]

    def finish(step, carry):
        copy_of(lax.rem(chip + step, chips), chip).wait_send()
        copy_of(lax.rem(chip + chips - step, chips), lax.rem(chip + chips - step, chips)).wait_recv()
        return carry

    lax.fori_loop(1, chips, finish, 0)


def chip_exchange(pieces, chips, per_expert, collective):
    rows, lanes = pieces.shape[1], pieces.shape[2]
    return pl.pallas_call(
        functools.partial(chip_exchange_kernel, chips, per_expert),
        out_shape=jax.ShapeDtypeStruct((chips, rows, lanes), pieces.dtype),
        in_specs=[pl.BlockSpec(memory_space=pltpu.VMEM)],
        out_specs=pl.BlockSpec(memory_space=pltpu.VMEM),
        scratch_shapes=[pltpu.SemaphoreType.DMA((chips,)), pltpu.SemaphoreType.DMA((chips,))],
        compiler_params=pltpu.CompilerParams(collective_id=collective, has_side_effects=True),
    )(pieces)


def pair_exchange_kernel(x_ref, o_ref, send_sem, recv_sem):
    me = lax.axis_index("shard")
    segment = lax.axis_index("segment")
    partner = (segment, me + 1 - 2 * lax.rem(me, 2))
    barrier = pltpu.get_barrier_semaphore()
    pl.semaphore_signal(barrier, 1, device_id=partner, device_id_type=pl.DeviceIdType.MESH)
    pl.semaphore_wait(barrier, 1)
    copy = pltpu.make_async_remote_copy(
        src_ref=x_ref,
        dst_ref=o_ref,
        send_sem=send_sem,
        recv_sem=recv_sem,
        device_id=partner,
        device_id_type=pl.DeviceIdType.MESH,
    )
    copy.start()
    copy.wait()


def pair_exchange(value, collective):
    return pl.pallas_call(
        pair_exchange_kernel,
        out_shape=jax.ShapeDtypeStruct(value.shape, value.dtype),
        in_specs=[pl.BlockSpec(memory_space=pltpu.VMEM)],
        out_specs=pl.BlockSpec(memory_space=pltpu.VMEM),
        scratch_shapes=[pltpu.SemaphoreType.DMA(()), pltpu.SemaphoreType.DMA(())],
        compiler_params=pltpu.CompilerParams(collective_id=collective, has_side_effects=True),
    )(value)


def shards(tokens, norm_gain, w_gate, w_up, w_down, block_counts, gate_prob):
    segment_index = lax.axis_index("segment")
    segment_count = lax.axis_size("segment")
    shard_count = lax.axis_size("shard")
    hidden_count = w_gate.shape[2]
    per_expert = FF // hidden_count
    zero_blocks = block_counts[0]
    row_gain = norm_gain[0]
    gate_part = w_gate[0]
    up_part = w_up[0]
    down_part = w_down[0]
    probs = gate_prob[0]
    local_rows = tokens.shape[1]
    width = tokens.shape[2]
    piece_rows = 2 * local_rows * width // LANES
    chips = shard_count // 2
    carried = tokens
    stored = jnp.zeros_like(tokens)
    for tick in range(segment_count):
        normed = normalize(carried, row_gain)
        pieces = jnp.stack([normed[0:2], normed[1:3]]).reshape(2, piece_rows, LANES)
        own_core = chip_exchange(pieces, chips, per_expert // 2, 0)
        other_core = pair_exchange(own_core, 1)
        block_rows = jnp.concatenate([own_core, other_core]).reshape(shard_count * 2 * local_rows, width)
        gate_val = jnp.dot(block_rows, gate_part, preferred_element_type=jnp.float32)
        up_val = jnp.dot(block_rows, up_part, preferred_element_type=jnp.float32)
        hidden = (jax.nn.silu(gate_val) * up_val).astype(jnp.bfloat16)
        partial_sum = jnp.dot(hidden, down_part, preferred_element_type=jnp.float32)
        partial_sum = partial_sum.reshape(2, chips, piece_rows, LANES)
        chip_sum = partial_sum[0] + pair_exchange(partial_sum[1], 2)
        received = chip_exchange(chip_sum.astype(jnp.bfloat16), chips, 0, 3).astype(jnp.float32)
        received = received.reshape(2, chips // 2, 2, local_rows, width)
        first, second = jnp.sum(received[0], axis=0), jnp.sum(received[1], axis=0)
        middle = jnp.where(zero_blocks >= 2, first[1], second[0])
        mixed = jnp.stack([first[0], middle, second[1]])
        updated = (carried.astype(jnp.float32) + probs[:, :, None] * mixed).astype(jnp.bfloat16)
        stored = jnp.where(segment_index == tick, updated, stored)
        if tick + 1 < segment_count:
            carried = shifted(updated, "segment", 1)
    return stored[None]


def solution(mesh):
    placed = (
        P(None, "shard", None),
        P("segment", None),
        P("segment", None, "shard"),
        P("segment", None, "shard"),
        P("segment", "shard", None),
        P("segment"),
        P("segment", None, "shard"),
    )
    return jax.shard_map(
        shards,
        mesh=mesh,
        in_specs=placed,
        out_specs=P("segment", None, "shard", None),
        check_vma=False,
    )
```

```python
import functools

import jax
import jax.numpy as jnp
from jax import lax
from jax.experimental import pallas as pl
from jax.experimental.pallas import tpu as pltpu
from jax.sharding import PartitionSpec as P

FF = 16384
LANES = 128


def shifted(value, axis, steps):
    count = lax.axis_size(axis)
    initial, last = (max(0, -steps), min(count, count - steps))
    return lax.ppermute(value, axis, [(source, source + steps) for source in range(initial, last)])


def normalize(rows, row_gain):
    values = rows.astype(jnp.float32)
    scale = lax.rsqrt(jnp.mean(values * values, axis=-1, keepdims=True) + 1e-05)
    return (values * scale * row_gain).astype(jnp.bfloat16)


def signed(index):
    return (index + 1) // 2 * (2 * lax.rem(index, 2) - 1)


def chip_exchange_kernel(ring_y, ring_z, per_expert, x_ref, o_ref, send_sem, recv_sem):
    me = lax.axis_index("shard")
    segment = lax.axis_index("segment")
    core = lax.rem(me, 2)
    chip = me // 2
    y, z = chip // ring_z, lax.rem(chip, ring_z)
    chips = ring_y * ring_z

    def peer(step, sign):
        z_index = lax.rem(step, ring_z)
        y_index = lax.rem(step // ring_z + z_index, ring_y)
        peer_y = lax.rem(y + sign * signed(y_index) + ring_y, ring_y)
        peer_z = lax.rem(z + sign * signed(z_index) + ring_z, ring_z)
        return peer_y * ring_z + peer_z

    def source(dest_chip):
        return x_ref.at[dest_chip // per_expert] if per_expert else x_ref.at[dest_chip]

    def copy_of(dest_chip, slot):
        return pltpu.make_async_remote_copy(
            src_ref=source(dest_chip),
            dst_ref=o_ref.at[slot],
            send_sem=send_sem.at[dest_chip],
            recv_sem=recv_sem.at[slot],
            device_id=(segment, dest_chip * 2 + core),
            device_id_type=pl.DeviceIdType.MESH,
        )

    barrier = pltpu.get_barrier_semaphore()

    def greet(step, carry):
        dest = peer(step, 1) * 2 + core
        pl.semaphore_signal(barrier, 1, device_id=(segment, dest), device_id_type=pl.DeviceIdType.MESH)
        return carry

    lax.fori_loop(1, chips, greet, 0)
    pl.semaphore_wait(barrier, chips - 1)

    def start(step, carry):
        copy_of(peer(step, 1), chip).start()
        return carry

    lax.fori_loop(1, chips, start, 0)
    o_ref[chip] = source(chip)[...]

    def finish(step, carry):
        copy_of(peer(step, 1), chip).wait_send()
        origin = peer(step, -1)
        copy_of(origin, origin).wait_recv()
        return carry

    lax.fori_loop(1, chips, finish, 0)


def chip_exchange(pieces, ring_y, ring_z, per_expert, collective):
    rows, lanes = pieces.shape[1], pieces.shape[2]
    chips = ring_y * ring_z
    return pl.pallas_call(
        functools.partial(chip_exchange_kernel, ring_y, ring_z, per_expert),
        out_shape=jax.ShapeDtypeStruct((chips, rows, lanes), pieces.dtype),
        in_specs=[pl.BlockSpec(memory_space=pltpu.VMEM)],
        out_specs=pl.BlockSpec(memory_space=pltpu.VMEM),
        scratch_shapes=[pltpu.SemaphoreType.DMA((chips,)), pltpu.SemaphoreType.DMA((chips,))],
        compiler_params=pltpu.CompilerParams(collective_id=collective, has_side_effects=True),
    )(pieces)


def pair_barrier():
    me = lax.axis_index("shard")
    partner = (lax.axis_index("segment"), me + 1 - 2 * lax.rem(me, 2))
    barrier = pltpu.get_barrier_semaphore()
    pl.semaphore_signal(barrier, 1, device_id=partner, device_id_type=pl.DeviceIdType.MESH)
    pl.semaphore_wait(barrier, 1)
    return partner


def pair_gather_kernel(x_ref, o_ref, send_sem, recv_sem, local_sem):
    partner = pair_barrier()
    copy = pltpu.make_async_remote_copy(
        src_ref=x_ref,
        dst_ref=o_ref.at[1],
        send_sem=send_sem,
        recv_sem=recv_sem,
        device_id=partner,
        device_id_type=pl.DeviceIdType.MESH,
    )
    copy.start()
    local = pltpu.make_async_copy(x_ref, o_ref.at[0], local_sem)
    local.start()
    local.wait()
    copy.wait()


def pair_gather(value, collective):
    return pl.pallas_call(
        pair_gather_kernel,
        out_shape=jax.ShapeDtypeStruct((2,) + value.shape, value.dtype),
        in_specs=[pl.BlockSpec(memory_space=pltpu.VMEM)],
        out_specs=pl.BlockSpec(memory_space=pltpu.VMEM),
        scratch_shapes=[pltpu.SemaphoreType.DMA(()), pltpu.SemaphoreType.DMA(()), pltpu.SemaphoreType.DMA(())],
        compiler_params=pltpu.CompilerParams(collective_id=collective, has_side_effects=True),
    )(value)


def pair_send_kernel(x_ref, o_ref, send_sem, recv_sem):
    partner = pair_barrier()
    rows = o_ref.shape[0]
    copy = pltpu.make_async_remote_copy(
        src_ref=x_ref.at[pl.ds(rows, rows)],
        dst_ref=o_ref,
        send_sem=send_sem,
        recv_sem=recv_sem,
        device_id=partner,
        device_id_type=pl.DeviceIdType.MESH,
    )
    copy.start()
    copy.wait()


def pair_send(value, collective):
    return pl.pallas_call(
        pair_send_kernel,
        out_shape=jax.ShapeDtypeStruct((value.shape[0] // 2, value.shape[1]), value.dtype),
        in_specs=[pl.BlockSpec(memory_space=pltpu.VMEM)],
        out_specs=pl.BlockSpec(memory_space=pltpu.VMEM),
        scratch_shapes=[pltpu.SemaphoreType.DMA(()), pltpu.SemaphoreType.DMA(())],
        compiler_params=pltpu.CompilerParams(collective_id=collective, has_side_effects=True),
    )(value)


def shards(tokens, norm_gain, w_gate, w_up, w_down, block_counts, gate_prob):
    segment_index = lax.axis_index("segment")
    segment_count = lax.axis_size("segment")
    shard_count = lax.axis_size("shard")
    hidden_count = w_gate.shape[2]
    per_expert = FF // hidden_count
    zero_blocks = block_counts[0]
    row_gain = norm_gain[0]
    gate_part = w_gate[0]
    up_part = w_up[0]
    down_part = w_down[0]
    probs = gate_prob[0]
    local_rows = tokens.shape[1]
    width = tokens.shape[2]
    piece_rows = 2 * local_rows * width // LANES
    chips = shard_count // 2
    ring_z = 8
    ring_y = chips // ring_z
    carried = tokens
    stored = jnp.zeros_like(tokens)
    for tick in range(segment_count):
        normed = normalize(carried, row_gain)
        pieces = jnp.stack([normed[0:2], normed[1:3]]).reshape(2, piece_rows, LANES)
        own_core = chip_exchange(pieces, ring_y, ring_z, per_expert // 2, 0)
        block_rows = pair_gather(own_core, 1).reshape(shard_count * 2 * local_rows, width)
        gate_val = jnp.dot(block_rows, gate_part, preferred_element_type=jnp.float32)
        up_val = jnp.dot(block_rows, up_part, preferred_element_type=jnp.float32)
        hidden = (jax.nn.silu(gate_val) * up_val).astype(jnp.bfloat16)
        partial_sum = jnp.dot(hidden, down_part, preferred_element_type=jnp.float32)
        half = partial_sum.shape[0] // 2
        chip_sum = (partial_sum[:half] + pair_send(partial_sum, 2)).astype(jnp.bfloat16)
        received = chip_exchange(chip_sum.reshape(chips, piece_rows, LANES), ring_y, ring_z, 0, 3)
        received = received.astype(jnp.float32)
        received = received.reshape(2, chips // 2, 2, local_rows, width)
        first, second = jnp.sum(received[0], axis=0), jnp.sum(received[1], axis=0)
        middle = jnp.where(zero_blocks >= 2, first[1], second[0])
        mixed = jnp.stack([first[0], middle, second[1]])
        updated = (carried.astype(jnp.float32) + probs[:, :, None] * mixed).astype(jnp.bfloat16)
        stored = jnp.where(segment_index == tick, updated, stored)
        if tick + 1 < segment_count:
            carried = shifted(updated, "segment", 1)
    return stored[None]


def solution(mesh):
    placed = (
        P(None, "shard", None),
        P("segment", None),
        P("segment", None, "shard"),
        P("segment", None, "shard"),
        P("segment", "shard", None),
        P("segment"),
        P("segment", None, "shard"),
    )
    return jax.shard_map(
        shards,
        mesh=mesh,
        in_specs=placed,
        out_specs=P("segment", None, "shard", None),
        check_vma=False,
    )
```

```python
import functools

import jax
import jax.numpy as jnp
from jax import lax
from jax.experimental import pallas as pl
from jax.experimental.pallas import tpu as pltpu
from jax.sharding import PartitionSpec as P

FF = 16384
LANES = 128


def shifted(value, axis, steps):
    count = lax.axis_size(axis)
    initial, last = (max(0, -steps), min(count, count - steps))
    return lax.ppermute(value, axis, [(source, source + steps) for source in range(initial, last)])


def normalize(rows, row_gain):
    values = rows.astype(jnp.float32)
    scale = lax.rsqrt(jnp.mean(values * values, axis=-1, keepdims=True) + 1e-05)
    return (values * scale * row_gain).astype(jnp.bfloat16)


def signed(index):
    return (index + 1) // 2 * (2 * lax.rem(index, 2) - 1)


def chip_exchange_kernel(ring_y, ring_z, per_expert, x_ref, o_ref, send_sem, recv_sem):
    me = lax.axis_index("shard")
    segment = lax.axis_index("segment")
    core = lax.rem(me, 2)
    chip = me // 2
    y, z = chip // ring_z, lax.rem(chip, ring_z)
    chips = ring_y * ring_z

    def peer(step, sign):
        z_index = lax.rem(step, ring_z)
        y_index = lax.rem(step // ring_z + z_index, ring_y)
        peer_y = lax.rem(y + sign * signed(y_index) + ring_y, ring_y)
        peer_z = lax.rem(z + sign * signed(z_index) + ring_z, ring_z)
        return peer_y * ring_z + peer_z

    def source(dest_chip):
        if per_expert:
            return x_ref.at[dest_chip // per_expert]
        return x_ref.at[lax.rem(dest_chip, ring_z) * ring_y + dest_chip // ring_z]

    def copy_of(dest_chip, slot):
        return pltpu.make_async_remote_copy(
            src_ref=source(dest_chip),
            dst_ref=o_ref.at[slot],
            send_sem=send_sem.at[dest_chip],
            recv_sem=recv_sem.at[slot],
            device_id=(segment, dest_chip * 2 + core),
            device_id_type=pl.DeviceIdType.MESH,
        )

    barrier = pltpu.get_barrier_semaphore()

    def greet(step, carry):
        dest = peer(step, 1) * 2 + core
        pl.semaphore_signal(barrier, 1, device_id=(segment, dest), device_id_type=pl.DeviceIdType.MESH)
        return carry

    lax.fori_loop(1, chips, greet, 0)
    pl.semaphore_wait(barrier, chips - 1)

    def start(step, carry):
        copy_of(peer(step, 1), chip).start()
        return carry

    lax.fori_loop(1, chips, start, 0)
    o_ref[chip] = source(chip)[...]

    def finish(step, carry):
        copy_of(peer(step, 1), chip).wait_send()
        origin = peer(step, -1)
        copy_of(origin, origin).wait_recv()
        return carry

    lax.fori_loop(1, chips, finish, 0)


def chip_exchange(pieces, ring_y, ring_z, per_expert, collective):
    rows, lanes = pieces.shape[1], pieces.shape[2]
    chips = ring_y * ring_z
    return pl.pallas_call(
        functools.partial(chip_exchange_kernel, ring_y, ring_z, per_expert),
        out_shape=jax.ShapeDtypeStruct((chips, rows, lanes), pieces.dtype),
        in_specs=[pl.BlockSpec(memory_space=pltpu.VMEM)],
        out_specs=pl.BlockSpec(memory_space=pltpu.VMEM),
        scratch_shapes=[pltpu.SemaphoreType.DMA((chips,)), pltpu.SemaphoreType.DMA((chips,))],
        compiler_params=pltpu.CompilerParams(collective_id=collective, has_side_effects=True),
    )(pieces)


def ring_gather_kernel(ring_y, ring_z, x_ref, o_ref, send_y, recv_y, send_up, send_down, recv_z, send_c, recv_c):
    me = lax.axis_index("shard")
    segment = lax.axis_index("segment")
    core = lax.rem(me, 2)
    chip = me // 2
    y, z = chip // ring_z, lax.rem(chip, ring_z)
    half_z = ring_z // 2

    def device(peer_y, peer_z):
        return (segment, (peer_y * ring_z + peer_z) * 2 + core)

    up_z, down_z = lax.rem(z + 1, ring_z), lax.rem(z + ring_z - 1, ring_z)
    partner = (segment, me + 1 - 2 * core)
    barrier = pltpu.get_barrier_semaphore()
    for step in range(1, ring_y):
        pl.semaphore_signal(barrier, 1, device_id=device(lax.rem(y + step, ring_y), z), device_id_type=pl.DeviceIdType.MESH)
    pl.semaphore_signal(barrier, 1, device_id=device(y, up_z), device_id_type=pl.DeviceIdType.MESH)
    pl.semaphore_signal(barrier, 1, device_id=device(y, down_z), device_id_type=pl.DeviceIdType.MESH)
    pl.semaphore_signal(barrier, 1, device_id=partner, device_id_type=pl.DeviceIdType.MESH)
    pl.semaphore_wait(barrier, ring_y + 2)

    def y_copy(peer_y, slot):
        return pltpu.make_async_remote_copy(
            src_ref=x_ref.at[peer_y * 2 // ring_y],
            dst_ref=o_ref.at[0, z, slot],
            send_sem=send_y.at[peer_y],
            recv_sem=recv_y.at[slot],
            device_id=device(peer_y, z),
            device_id_type=pl.DeviceIdType.MESH,
        )

    for step in range(1, ring_y):
        y_copy(lax.rem(y + step, ring_y), y).start()
    o_ref[0, z, y] = x_ref[y * 2 // ring_y]
    for step in range(1, ring_y):
        origin = lax.rem(y + ring_y - step, ring_y)
        y_copy(origin, origin).wait_recv()
        y_copy(lax.rem(y + step, ring_y), y).wait_send()

    def z_copy(slot, peer_z, sems, index):
        return pltpu.make_async_remote_copy(
            src_ref=o_ref.at[0, slot],
            dst_ref=o_ref.at[0, slot],
            send_sem=sems.at[index],
            recv_sem=recv_z.at[slot],
            device_id=device(y, peer_z),
            device_id_type=pl.DeviceIdType.MESH,
        )

    for step in range(half_z):
        up_slot = lax.rem(z + ring_z - step, ring_z)
        if step > 0:
            z_copy(up_slot, down_z, send_up, step).wait_recv()
        z_copy(up_slot, up_z, send_up, step).start()
        if step < half_z - 1:
            down_slot = lax.rem(z + step, ring_z)
            if step > 0:
                z_copy(down_slot, up_z, send_down, step).wait_recv()
            z_copy(down_slot, down_z, send_down, step).start()
    z_copy(lax.rem(z + ring_z - half_z, ring_z), down_z, send_up, 0).wait_recv()
    z_copy(lax.rem(z + half_z - 1, ring_z), up_z, send_down, 0).wait_recv()
    for step in range(half_z):
        z_copy(lax.rem(z + ring_z - step, ring_z), up_z, send_up, step).wait_send()
        if step < half_z - 1:
            z_copy(lax.rem(z + step, ring_z), down_z, send_down, step).wait_send()

    pair = pltpu.make_async_remote_copy(
        src_ref=o_ref.at[0],
        dst_ref=o_ref.at[1],
        send_sem=send_c,
        recv_sem=recv_c,
        device_id=partner,
        device_id_type=pl.DeviceIdType.MESH,
    )
    pair.start()
    pair.wait()


def ring_gather(pieces, ring_y, ring_z, collective):
    rows, lanes = pieces.shape[1], pieces.shape[2]
    return pl.pallas_call(
        functools.partial(ring_gather_kernel, ring_y, ring_z),
        out_shape=jax.ShapeDtypeStruct((2, ring_z, ring_y, rows, lanes), pieces.dtype),
        in_specs=[pl.BlockSpec(memory_space=pltpu.VMEM)],
        out_specs=pl.BlockSpec(memory_space=pltpu.VMEM),
        scratch_shapes=[
            pltpu.SemaphoreType.DMA((ring_y,)),
            pltpu.SemaphoreType.DMA((ring_y,)),
            pltpu.SemaphoreType.DMA((ring_z // 2,)),
            pltpu.SemaphoreType.DMA((ring_z // 2,)),
            pltpu.SemaphoreType.DMA((ring_z,)),
            pltpu.SemaphoreType.DMA(()),
            pltpu.SemaphoreType.DMA(()),
        ],
        compiler_params=pltpu.CompilerParams(collective_id=collective, has_side_effects=True),
    )(pieces)


def pair_barrier():
    me = lax.axis_index("shard")
    partner = (lax.axis_index("segment"), me + 1 - 2 * lax.rem(me, 2))
    barrier = pltpu.get_barrier_semaphore()
    pl.semaphore_signal(barrier, 1, device_id=partner, device_id_type=pl.DeviceIdType.MESH)
    pl.semaphore_wait(barrier, 1)
    return partner


def pair_gather_kernel(x_ref, o_ref, send_sem, recv_sem, local_sem):
    partner = pair_barrier()
    copy = pltpu.make_async_remote_copy(
        src_ref=x_ref,
        dst_ref=o_ref.at[1],
        send_sem=send_sem,
        recv_sem=recv_sem,
        device_id=partner,
        device_id_type=pl.DeviceIdType.MESH,
    )
    copy.start()
    local = pltpu.make_async_copy(x_ref, o_ref.at[0], local_sem)
    local.start()
    local.wait()
    copy.wait()


def pair_gather(value, collective):
    return pl.pallas_call(
        pair_gather_kernel,
        out_shape=jax.ShapeDtypeStruct((2,) + value.shape, value.dtype),
        in_specs=[pl.BlockSpec(memory_space=pltpu.VMEM)],
        out_specs=pl.BlockSpec(memory_space=pltpu.VMEM),
        scratch_shapes=[pltpu.SemaphoreType.DMA(()), pltpu.SemaphoreType.DMA(()), pltpu.SemaphoreType.DMA(())],
        compiler_params=pltpu.CompilerParams(collective_id=collective, has_side_effects=True),
    )(value)


def pair_send_kernel(x_ref, o_ref, send_sem, recv_sem):
    partner = pair_barrier()
    rows = o_ref.shape[0]
    copy = pltpu.make_async_remote_copy(
        src_ref=x_ref.at[pl.ds(rows, rows)],
        dst_ref=o_ref,
        send_sem=send_sem,
        recv_sem=recv_sem,
        device_id=partner,
        device_id_type=pl.DeviceIdType.MESH,
    )
    copy.start()
    copy.wait()


def pair_send(value, collective):
    return pl.pallas_call(
        pair_send_kernel,
        out_shape=jax.ShapeDtypeStruct((value.shape[0] // 2, value.shape[1]), value.dtype),
        in_specs=[pl.BlockSpec(memory_space=pltpu.VMEM)],
        out_specs=pl.BlockSpec(memory_space=pltpu.VMEM),
        scratch_shapes=[pltpu.SemaphoreType.DMA(()), pltpu.SemaphoreType.DMA(())],
        compiler_params=pltpu.CompilerParams(collective_id=collective, has_side_effects=True),
    )(value)


def shards(tokens, norm_gain, w_gate, w_up, w_down, block_counts, gate_prob):
    segment_index = lax.axis_index("segment")
    segment_count = lax.axis_size("segment")
    shard_count = lax.axis_size("shard")
    hidden_count = w_gate.shape[2]
    per_expert = FF // hidden_count
    zero_blocks = block_counts[0]
    row_gain = norm_gain[0]
    gate_part = w_gate[0]
    up_part = w_up[0]
    down_part = w_down[0]
    probs = gate_prob[0]
    local_rows = tokens.shape[1]
    width = tokens.shape[2]
    piece_rows = 2 * local_rows * width // LANES
    chips = shard_count // 2
    ring_z = 8
    ring_y = chips // ring_z
    carried = tokens
    stored = jnp.zeros_like(tokens)
    for tick in range(segment_count):
        normed = normalize(carried, row_gain)
        pieces = jnp.stack([normed[0:2], normed[1:3]]).reshape(2, piece_rows, LANES)
        block_rows = ring_gather(pieces, ring_y, ring_z, 0).reshape(shard_count * 2 * local_rows, width)
        gate_val = jnp.dot(block_rows, gate_part, preferred_element_type=jnp.float32)
        up_val = jnp.dot(block_rows, up_part, preferred_element_type=jnp.float32)
        hidden = (jax.nn.silu(gate_val) * up_val).astype(jnp.bfloat16)
        partial_sum = jnp.dot(hidden, down_part, preferred_element_type=jnp.float32)
        half = partial_sum.shape[0] // 2
        chip_sum = (partial_sum[:half] + pair_send(partial_sum, 2)).astype(jnp.bfloat16)
        received = chip_exchange(chip_sum.reshape(chips, piece_rows, LANES), ring_y, ring_z, 0, 3)
        received = received.astype(jnp.float32)
        received = received.reshape(2, chips // 2, 2, local_rows, width)
        first, second = jnp.sum(received[0], axis=0), jnp.sum(received[1], axis=0)
        middle = jnp.where(zero_blocks >= 2, first[1], second[0])
        mixed = jnp.stack([first[0], middle, second[1]])
        updated = (carried.astype(jnp.float32) + probs[:, :, None] * mixed).astype(jnp.bfloat16)
        stored = jnp.where(segment_index == tick, updated, stored)
        if tick + 1 < segment_count:
            carried = shifted(updated, "segment", 1)
    return stored[None]


def solution(mesh):
    placed = (
        P(None, "shard", None),
        P("segment", None),
        P("segment", None, "shard"),
        P("segment", None, "shard"),
        P("segment", "shard", None),
        P("segment"),
        P("segment", None, "shard"),
    )
    return jax.shard_map(
        shards,
        mesh=mesh,
        in_specs=placed,
        out_specs=P("segment", None, "shard", None),
        check_vma=False,
    )
```

```python
import functools

import jax
import jax.numpy as jnp
from jax import lax
from jax.experimental import pallas as pl
from jax.experimental.pallas import tpu as pltpu
from jax.sharding import PartitionSpec as P

FF = 16384
LANES = 128


def shifted(value, axis, steps):
    count = lax.axis_size(axis)
    initial, last = (max(0, -steps), min(count, count - steps))
    return lax.ppermute(value, axis, [(source, source + steps) for source in range(initial, last)])


def normalize(rows, row_gain):
    values = rows.astype(jnp.float32)
    scale = lax.rsqrt(jnp.mean(values * values, axis=-1, keepdims=True) + 1e-05)
    return (values * scale * row_gain).astype(jnp.bfloat16)


def signed(index):
    return (index + 1) // 2 * (2 * lax.rem(index, 2) - 1)


def chip_exchange_kernel(ring_y, ring_z, per_expert, x_ref, o_ref, send_sem, recv_sem):
    me = lax.axis_index("shard")
    segment = lax.axis_index("segment")
    core = lax.rem(me, 2)
    chip = me // 2
    y, z = chip // ring_z, lax.rem(chip, ring_z)
    chips = ring_y * ring_z

    def peer(step, sign):
        z_index = lax.rem(step, ring_z)
        y_index = lax.rem(step // ring_z + z_index, ring_y)
        peer_y = lax.rem(y + sign * signed(y_index) + ring_y, ring_y)
        peer_z = lax.rem(z + sign * signed(z_index) + ring_z, ring_z)
        return peer_y * ring_z + peer_z

    def source(dest_chip):
        if per_expert:
            return x_ref.at[dest_chip // per_expert]
        return x_ref.at[lax.rem(dest_chip, ring_z) * ring_y + dest_chip // ring_z]

    def copy_of(dest_chip, slot):
        return pltpu.make_async_remote_copy(
            src_ref=source(dest_chip),
            dst_ref=o_ref.at[slot],
            send_sem=send_sem.at[dest_chip],
            recv_sem=recv_sem.at[slot],
            device_id=(segment, dest_chip * 2 + core),
            device_id_type=pl.DeviceIdType.MESH,
        )

    barrier = pltpu.get_barrier_semaphore()

    def greet(step, carry):
        dest = peer(step, 1) * 2 + core
        pl.semaphore_signal(barrier, 1, device_id=(segment, dest), device_id_type=pl.DeviceIdType.MESH)
        return carry

    lax.fori_loop(1, chips, greet, 0)
    pl.semaphore_wait(barrier, chips - 1)

    def start(step, carry):
        copy_of(peer(step, 1), chip).start()
        return carry

    lax.fori_loop(1, chips, start, 0)
    o_ref[chip] = source(chip)[...]

    def finish(step, carry):
        copy_of(peer(step, 1), chip).wait_send()
        origin = peer(step, -1)
        copy_of(origin, origin).wait_recv()
        return carry

    lax.fori_loop(1, chips, finish, 0)


def chip_exchange(pieces, ring_y, ring_z, per_expert, collective):
    rows, lanes = pieces.shape[1], pieces.shape[2]
    chips = ring_y * ring_z
    return pl.pallas_call(
        functools.partial(chip_exchange_kernel, ring_y, ring_z, per_expert),
        out_shape=jax.ShapeDtypeStruct((chips, rows, lanes), pieces.dtype),
        in_specs=[pl.BlockSpec(memory_space=pltpu.VMEM)],
        out_specs=pl.BlockSpec(memory_space=pltpu.VMEM),
        scratch_shapes=[pltpu.SemaphoreType.DMA((chips,)), pltpu.SemaphoreType.DMA((chips,))],
        compiler_params=pltpu.CompilerParams(collective_id=collective, has_side_effects=True),
    )(pieces)


def ring_gather_kernel(ring_y, ring_z, x_ref, o_ref, send_y, recv_y, send_up, send_down, recv_z, send_c, recv_c):
    me = lax.axis_index("shard")
    segment = lax.axis_index("segment")
    core = lax.rem(me, 2)
    chip = me // 2
    y, z = chip // ring_z, lax.rem(chip, ring_z)
    half_z = ring_z // 2

    def device(peer_y, peer_z):
        return (segment, (peer_y * ring_z + peer_z) * 2 + core)

    up_z, down_z = lax.rem(z + 1, ring_z), lax.rem(z + ring_z - 1, ring_z)
    partner = (segment, me + 1 - 2 * core)
    barrier = pltpu.get_barrier_semaphore()
    for step in range(1, ring_y):
        pl.semaphore_signal(barrier, 1, device_id=device(lax.rem(y + step, ring_y), z), device_id_type=pl.DeviceIdType.MESH)
    pl.semaphore_signal(barrier, 1, device_id=device(y, up_z), device_id_type=pl.DeviceIdType.MESH)
    pl.semaphore_signal(barrier, 1, device_id=device(y, down_z), device_id_type=pl.DeviceIdType.MESH)
    pl.semaphore_signal(barrier, 1, device_id=partner, device_id_type=pl.DeviceIdType.MESH)
    pl.semaphore_wait(barrier, ring_y + 2)

    def y_copy(peer_y, slot):
        return pltpu.make_async_remote_copy(
            src_ref=x_ref.at[peer_y * 2 // ring_y],
            dst_ref=o_ref.at[0, z, slot],
            send_sem=send_y.at[peer_y],
            recv_sem=recv_y.at[slot],
            device_id=device(peer_y, z),
            device_id_type=pl.DeviceIdType.MESH,
        )

    for step in range(1, ring_y):
        y_copy(lax.rem(y + step, ring_y), y).start()
    o_ref[0, z, y] = x_ref[y * 2 // ring_y]
    for step in range(1, ring_y):
        origin = lax.rem(y + ring_y - step, ring_y)
        y_copy(origin, origin).wait_recv()
        y_copy(lax.rem(y + step, ring_y), y).wait_send()

    def z_copy(slot, peer_z, sems, index):
        return pltpu.make_async_remote_copy(
            src_ref=o_ref.at[0, slot],
            dst_ref=o_ref.at[0, slot],
            send_sem=sems.at[index],
            recv_sem=recv_z.at[slot],
            device_id=device(y, peer_z),
            device_id_type=pl.DeviceIdType.MESH,
        )

    for step in range(half_z):
        up_slot = lax.rem(z + ring_z - step, ring_z)
        if step > 0:
            z_copy(up_slot, down_z, send_up, step).wait_recv()
        z_copy(up_slot, up_z, send_up, step).start()
        if step < half_z - 1:
            down_slot = lax.rem(z + step, ring_z)
            if step > 0:
                z_copy(down_slot, up_z, send_down, step).wait_recv()
            z_copy(down_slot, down_z, send_down, step).start()
    z_copy(lax.rem(z + ring_z - half_z, ring_z), down_z, send_up, 0).wait_recv()
    z_copy(lax.rem(z + half_z - 1, ring_z), up_z, send_down, 0).wait_recv()
    for step in range(half_z):
        z_copy(lax.rem(z + ring_z - step, ring_z), up_z, send_up, step).wait_send()
        if step < half_z - 1:
            z_copy(lax.rem(z + step, ring_z), down_z, send_down, step).wait_send()

    pair = pltpu.make_async_remote_copy(
        src_ref=o_ref.at[0],
        dst_ref=o_ref.at[1],
        send_sem=send_c,
        recv_sem=recv_c,
        device_id=partner,
        device_id_type=pl.DeviceIdType.MESH,
    )
    pair.start()
    pair.wait()


def ring_gather(pieces, ring_y, ring_z, collective):
    rows, lanes = pieces.shape[1], pieces.shape[2]
    return pl.pallas_call(
        functools.partial(ring_gather_kernel, ring_y, ring_z),
        out_shape=jax.ShapeDtypeStruct((2, ring_z, ring_y, rows, lanes), pieces.dtype),
        in_specs=[pl.BlockSpec(memory_space=pltpu.VMEM)],
        out_specs=pl.BlockSpec(memory_space=pltpu.VMEM),
        scratch_shapes=[
            pltpu.SemaphoreType.DMA((ring_y,)),
            pltpu.SemaphoreType.DMA((ring_y,)),
            pltpu.SemaphoreType.DMA((ring_z // 2,)),
            pltpu.SemaphoreType.DMA((ring_z // 2,)),
            pltpu.SemaphoreType.DMA((ring_z,)),
            pltpu.SemaphoreType.DMA(()),
            pltpu.SemaphoreType.DMA(()),
        ],
        compiler_params=pltpu.CompilerParams(collective_id=collective, has_side_effects=True),
    )(pieces)


def expert_kernel(x_ref, gate_ref, up_ref, down_ref, o_ref):
    @pl.when(pl.program_id(0) == 0)
    def _():
        o_ref[...] = jnp.zeros_like(o_ref)

    rows = x_ref[...]
    gate_val = jnp.dot(rows, gate_ref[...], preferred_element_type=jnp.float32)
    up_val = jnp.dot(rows, up_ref[...], preferred_element_type=jnp.float32)
    hidden = (gate_val / (1.0 + jnp.exp(-gate_val)) * up_val).astype(jnp.bfloat16)
    o_ref[...] += jnp.dot(hidden, down_ref[...], preferred_element_type=jnp.float32)


def expert(rows, gate_part, up_part, down_part, chunk=128):
    count, width = rows.shape
    hidden = gate_part.shape[1]
    return pl.pallas_call(
        expert_kernel,
        out_shape=jax.ShapeDtypeStruct((count, width), jnp.float32),
        grid=(hidden // chunk,),
        in_specs=[
            pl.BlockSpec((count, width), lambda k: (0, 0)),
            pl.BlockSpec((width, chunk), lambda k: (0, k)),
            pl.BlockSpec((width, chunk), lambda k: (0, k)),
            pl.BlockSpec((chunk, width), lambda k: (k, 0)),
        ],
        out_specs=pl.BlockSpec((count, width), lambda k: (0, 0)),
        compiler_params=pltpu.CompilerParams(dimension_semantics=("arbitrary",)),
        cost_estimate=pl.CostEstimate(
            flops=6 * count * width * hidden,
            transcendentals=count * hidden,
            bytes_accessed=2 * (count * width + 3 * width * hidden) + 4 * count * width,
        ),
    )(rows, gate_part, up_part, down_part)


def pair_barrier():
    me = lax.axis_index("shard")
    partner = (lax.axis_index("segment"), me + 1 - 2 * lax.rem(me, 2))
    barrier = pltpu.get_barrier_semaphore()
    pl.semaphore_signal(barrier, 1, device_id=partner, device_id_type=pl.DeviceIdType.MESH)
    pl.semaphore_wait(barrier, 1)
    return partner


def pair_gather_kernel(x_ref, o_ref, send_sem, recv_sem, local_sem):
    partner = pair_barrier()
    copy = pltpu.make_async_remote_copy(
        src_ref=x_ref,
        dst_ref=o_ref.at[1],
        send_sem=send_sem,
        recv_sem=recv_sem,
        device_id=partner,
        device_id_type=pl.DeviceIdType.MESH,
    )
    copy.start()
    local = pltpu.make_async_copy(x_ref, o_ref.at[0], local_sem)
    local.start()
    local.wait()
    copy.wait()


def pair_gather(value, collective):
    return pl.pallas_call(
        pair_gather_kernel,
        out_shape=jax.ShapeDtypeStruct((2,) + value.shape, value.dtype),
        in_specs=[pl.BlockSpec(memory_space=pltpu.VMEM)],
        out_specs=pl.BlockSpec(memory_space=pltpu.VMEM),
        scratch_shapes=[pltpu.SemaphoreType.DMA(()), pltpu.SemaphoreType.DMA(()), pltpu.SemaphoreType.DMA(())],
        compiler_params=pltpu.CompilerParams(collective_id=collective, has_side_effects=True),
    )(value)


def pair_send_kernel(x_ref, o_ref, send_sem, recv_sem):
    partner = pair_barrier()
    rows = o_ref.shape[0]
    copy = pltpu.make_async_remote_copy(
        src_ref=x_ref.at[pl.ds(rows, rows)],
        dst_ref=o_ref,
        send_sem=send_sem,
        recv_sem=recv_sem,
        device_id=partner,
        device_id_type=pl.DeviceIdType.MESH,
    )
    copy.start()
    copy.wait()


def pair_send(value, collective):
    return pl.pallas_call(
        pair_send_kernel,
        out_shape=jax.ShapeDtypeStruct((value.shape[0] // 2, value.shape[1]), value.dtype),
        in_specs=[pl.BlockSpec(memory_space=pltpu.VMEM)],
        out_specs=pl.BlockSpec(memory_space=pltpu.VMEM),
        scratch_shapes=[pltpu.SemaphoreType.DMA(()), pltpu.SemaphoreType.DMA(())],
        compiler_params=pltpu.CompilerParams(collective_id=collective, has_side_effects=True),
    )(value)


def shards(tokens, norm_gain, w_gate, w_up, w_down, block_counts, gate_prob):
    segment_index = lax.axis_index("segment")
    segment_count = lax.axis_size("segment")
    shard_count = lax.axis_size("shard")
    hidden_count = w_gate.shape[2]
    per_expert = FF // hidden_count
    zero_blocks = block_counts[0]
    row_gain = norm_gain[0]
    gate_part = w_gate[0]
    up_part = w_up[0]
    down_part = w_down[0]
    probs = gate_prob[0]
    local_rows = tokens.shape[1]
    width = tokens.shape[2]
    piece_rows = 2 * local_rows * width // LANES
    chips = shard_count // 2
    ring_z = 8
    ring_y = chips // ring_z
    carried = tokens
    stored = jnp.zeros_like(tokens)
    for tick in range(segment_count):
        normed = normalize(carried, row_gain)
        pieces = jnp.stack([normed[0:2], normed[1:3]]).reshape(2, piece_rows, LANES)
        block_rows = ring_gather(pieces, ring_y, ring_z, 0).reshape(shard_count * 2 * local_rows, width)
        partial_sum = expert(block_rows, gate_part, up_part, down_part)
        half = partial_sum.shape[0] // 2
        chip_sum = (partial_sum[:half] + pair_send(partial_sum, 2)).astype(jnp.bfloat16)
        received = chip_exchange(chip_sum.reshape(chips, piece_rows, LANES), ring_y, ring_z, 0, 3)
        received = received.astype(jnp.float32)
        received = received.reshape(2, chips // 2, 2, local_rows, width)
        first, second = jnp.sum(received[0], axis=0), jnp.sum(received[1], axis=0)
        middle = jnp.where(zero_blocks >= 2, first[1], second[0])
        mixed = jnp.stack([first[0], middle, second[1]])
        updated = (carried.astype(jnp.float32) + probs[:, :, None] * mixed).astype(jnp.bfloat16)
        stored = jnp.where(segment_index == tick, updated, stored)
        if tick + 1 < segment_count:
            carried = shifted(updated, "segment", 1)
    return stored[None]


def solution(mesh):
    placed = (
        P(None, "shard", None),
        P("segment", None),
        P("segment", None, "shard"),
        P("segment", None, "shard"),
        P("segment", "shard", None),
        P("segment"),
        P("segment", None, "shard"),
    )
    return jax.shard_map(
        shards,
        mesh=mesh,
        in_specs=placed,
        out_specs=P("segment", None, "shard", None),
        check_vma=False,
    )
```

```python
import functools

import jax
import jax.numpy as jnp
from jax import lax
from jax.experimental import pallas as pl
from jax.experimental.pallas import tpu as pltpu
from jax.sharding import PartitionSpec as P

FF = 16384
LANES = 128


def shifted(value, axis, steps):
    count = lax.axis_size(axis)
    initial, last = (max(0, -steps), min(count, count - steps))
    return lax.ppermute(value, axis, [(source, source + steps) for source in range(initial, last)])


def normalize(rows, row_gain):
    values = rows.astype(jnp.float32)
    scale = lax.rsqrt(jnp.mean(values * values, axis=-1, keepdims=True) + 1e-05)
    return (values * scale * row_gain).astype(jnp.bfloat16)


def signed(index):
    return (index + 1) // 2 * (2 * lax.rem(index, 2) - 1)


def chip_exchange_kernel(ring_y, ring_z, per_expert, x_ref, o_ref, send_sem, recv_sem):
    me = lax.axis_index("shard")
    segment = lax.axis_index("segment")
    core = lax.rem(me, 2)
    chip = me // 2
    y, z = chip // ring_z, lax.rem(chip, ring_z)
    chips = ring_y * ring_z

    def peer(step, sign):
        z_index = lax.rem(step, ring_z)
        y_index = lax.rem(step // ring_z + z_index, ring_y)
        peer_y = lax.rem(y + sign * signed(y_index) + ring_y, ring_y)
        peer_z = lax.rem(z + sign * signed(z_index) + ring_z, ring_z)
        return peer_y * ring_z + peer_z

    def source(dest_chip):
        if per_expert:
            return x_ref.at[dest_chip // per_expert]
        return x_ref.at[lax.rem(dest_chip, ring_z) * ring_y + dest_chip // ring_z]

    def copy_of(dest_chip, slot):
        return pltpu.make_async_remote_copy(
            src_ref=source(dest_chip),
            dst_ref=o_ref.at[slot],
            send_sem=send_sem.at[dest_chip],
            recv_sem=recv_sem.at[slot],
            device_id=(segment, dest_chip * 2 + core),
            device_id_type=pl.DeviceIdType.MESH,
        )

    barrier = pltpu.get_barrier_semaphore()

    def greet(step, carry):
        dest = peer(step, 1) * 2 + core
        pl.semaphore_signal(barrier, 1, device_id=(segment, dest), device_id_type=pl.DeviceIdType.MESH)
        return carry

    lax.fori_loop(1, chips, greet, 0)
    pl.semaphore_wait(barrier, chips - 1)

    def start(step, carry):
        copy_of(peer(step, 1), chip).start()
        return carry

    lax.fori_loop(1, chips, start, 0)
    o_ref[chip] = source(chip)[...]

    def finish(step, carry):
        copy_of(peer(step, 1), chip).wait_send()
        origin = peer(step, -1)
        copy_of(origin, origin).wait_recv()
        return carry

    lax.fori_loop(1, chips, finish, 0)


def chip_exchange(pieces, ring_y, ring_z, per_expert, collective):
    rows, lanes = pieces.shape[1], pieces.shape[2]
    chips = ring_y * ring_z
    return pl.pallas_call(
        functools.partial(chip_exchange_kernel, ring_y, ring_z, per_expert),
        out_shape=jax.ShapeDtypeStruct((chips, rows, lanes), pieces.dtype),
        in_specs=[pl.BlockSpec(memory_space=pltpu.VMEM)],
        out_specs=pl.BlockSpec(memory_space=pltpu.VMEM),
        scratch_shapes=[pltpu.SemaphoreType.DMA((chips,)), pltpu.SemaphoreType.DMA((chips,))],
        compiler_params=pltpu.CompilerParams(collective_id=collective, has_side_effects=True),
    )(pieces)


def ring_gather_kernel(ring_y, ring_z, x_ref, o_ref, send_y, recv_y, send_up, send_down, recv_z, send_c, recv_c):
    me = lax.axis_index("shard")
    segment = lax.axis_index("segment")
    core = lax.rem(me, 2)
    chip = me // 2
    y, z = chip // ring_z, lax.rem(chip, ring_z)
    half_z = ring_z // 2

    def device(peer_y, peer_z):
        return (segment, (peer_y * ring_z + peer_z) * 2 + core)

    up_z, down_z = lax.rem(z + 1, ring_z), lax.rem(z + ring_z - 1, ring_z)
    partner = (segment, me + 1 - 2 * core)
    barrier = pltpu.get_barrier_semaphore()
    for step in range(1, ring_y):
        pl.semaphore_signal(barrier, 1, device_id=device(lax.rem(y + step, ring_y), z), device_id_type=pl.DeviceIdType.MESH)
    pl.semaphore_signal(barrier, 1, device_id=device(y, up_z), device_id_type=pl.DeviceIdType.MESH)
    pl.semaphore_signal(barrier, 1, device_id=device(y, down_z), device_id_type=pl.DeviceIdType.MESH)
    pl.semaphore_signal(barrier, 1, device_id=partner, device_id_type=pl.DeviceIdType.MESH)
    pl.semaphore_wait(barrier, ring_y + 2)

    def y_copy(peer_y, slot):
        return pltpu.make_async_remote_copy(
            src_ref=x_ref.at[peer_y * 2 // ring_y],
            dst_ref=o_ref.at[0, z, slot],
            send_sem=send_y.at[peer_y],
            recv_sem=recv_y.at[slot],
            device_id=device(peer_y, z),
            device_id_type=pl.DeviceIdType.MESH,
        )

    for step in range(1, ring_y):
        y_copy(lax.rem(y + step, ring_y), y).start()
    o_ref[0, z, y] = x_ref[y * 2 // ring_y]
    for step in range(1, ring_y):
        origin = lax.rem(y + ring_y - step, ring_y)
        y_copy(origin, origin).wait_recv()
        y_copy(lax.rem(y + step, ring_y), y).wait_send()

    def z_copy(slot, peer_z, sems, index):
        return pltpu.make_async_remote_copy(
            src_ref=o_ref.at[0, slot],
            dst_ref=o_ref.at[0, slot],
            send_sem=sems.at[index],
            recv_sem=recv_z.at[slot],
            device_id=device(y, peer_z),
            device_id_type=pl.DeviceIdType.MESH,
        )

    for step in range(half_z):
        up_slot = lax.rem(z + ring_z - step, ring_z)
        if step > 0:
            z_copy(up_slot, down_z, send_up, step).wait_recv()
        z_copy(up_slot, up_z, send_up, step).start()
        if step < half_z - 1:
            down_slot = lax.rem(z + step, ring_z)
            if step > 0:
                z_copy(down_slot, up_z, send_down, step).wait_recv()
            z_copy(down_slot, down_z, send_down, step).start()
    z_copy(lax.rem(z + ring_z - half_z, ring_z), down_z, send_up, 0).wait_recv()
    z_copy(lax.rem(z + half_z - 1, ring_z), up_z, send_down, 0).wait_recv()
    for step in range(half_z):
        z_copy(lax.rem(z + ring_z - step, ring_z), up_z, send_up, step).wait_send()
        if step < half_z - 1:
            z_copy(lax.rem(z + step, ring_z), down_z, send_down, step).wait_send()

    pair = pltpu.make_async_remote_copy(
        src_ref=o_ref.at[0],
        dst_ref=o_ref.at[1],
        send_sem=send_c,
        recv_sem=recv_c,
        device_id=partner,
        device_id_type=pl.DeviceIdType.MESH,
    )
    pair.start()
    pair.wait()


def ring_gather(pieces, ring_y, ring_z, collective):
    rows, lanes = pieces.shape[1], pieces.shape[2]
    return pl.pallas_call(
        functools.partial(ring_gather_kernel, ring_y, ring_z),
        out_shape=jax.ShapeDtypeStruct((2, ring_z, ring_y, rows, lanes), pieces.dtype),
        in_specs=[pl.BlockSpec(memory_space=pltpu.VMEM)],
        out_specs=pl.BlockSpec(memory_space=pltpu.VMEM),
        scratch_shapes=[
            pltpu.SemaphoreType.DMA((ring_y,)),
            pltpu.SemaphoreType.DMA((ring_y,)),
            pltpu.SemaphoreType.DMA((ring_z // 2,)),
            pltpu.SemaphoreType.DMA((ring_z // 2,)),
            pltpu.SemaphoreType.DMA((ring_z,)),
            pltpu.SemaphoreType.DMA(()),
            pltpu.SemaphoreType.DMA(()),
        ],
        compiler_params=pltpu.CompilerParams(collective_id=collective, has_side_effects=True),
    )(pieces)


def expert_kernel(x_ref, gate_ref, up_ref, down_ref, o_ref):
    rows = x_ref[...]
    gate_val = jnp.dot(rows, gate_ref[...], preferred_element_type=jnp.float32)
    up_val = jnp.dot(rows, up_ref[...], preferred_element_type=jnp.float32)
    hidden = (gate_val / (1.0 + jnp.exp(-gate_val)) * up_val).astype(jnp.bfloat16)
    term = jnp.dot(hidden, down_ref[...], preferred_element_type=jnp.float32)

    @pl.when(pl.program_id(0) == 0)
    def _():
        o_ref[...] = term

    @pl.when(pl.program_id(0) > 0)
    def _():
        o_ref[...] += term


def expert(rows, gate_part, up_part, down_part, chunk=256):
    count, width = rows.shape
    hidden = gate_part.shape[1]
    return pl.pallas_call(
        expert_kernel,
        out_shape=jax.ShapeDtypeStruct((count, width), jnp.float32),
        grid=(hidden // chunk,),
        in_specs=[
            pl.BlockSpec((count, width), lambda k: (0, 0)),
            pl.BlockSpec((width, chunk), lambda k: (0, k)),
            pl.BlockSpec((width, chunk), lambda k: (0, k)),
            pl.BlockSpec((chunk, width), lambda k: (k, 0)),
        ],
        out_specs=pl.BlockSpec((count, width), lambda k: (0, 0)),
        compiler_params=pltpu.CompilerParams(dimension_semantics=("arbitrary",)),
        cost_estimate=pl.CostEstimate(
            flops=6 * count * width * hidden,
            transcendentals=count * hidden,
            bytes_accessed=2 * (count * width + 3 * width * hidden) + 4 * count * width,
        ),
    )(rows, gate_part, up_part, down_part)


def pair_barrier():
    me = lax.axis_index("shard")
    partner = (lax.axis_index("segment"), me + 1 - 2 * lax.rem(me, 2))
    barrier = pltpu.get_barrier_semaphore()
    pl.semaphore_signal(barrier, 1, device_id=partner, device_id_type=pl.DeviceIdType.MESH)
    pl.semaphore_wait(barrier, 1)
    return partner


def pair_gather_kernel(x_ref, o_ref, send_sem, recv_sem, local_sem):
    partner = pair_barrier()
    copy = pltpu.make_async_remote_copy(
        src_ref=x_ref,
        dst_ref=o_ref.at[1],
        send_sem=send_sem,
        recv_sem=recv_sem,
        device_id=partner,
        device_id_type=pl.DeviceIdType.MESH,
    )
    copy.start()
    local = pltpu.make_async_copy(x_ref, o_ref.at[0], local_sem)
    local.start()
    local.wait()
    copy.wait()


def pair_gather(value, collective):
    return pl.pallas_call(
        pair_gather_kernel,
        out_shape=jax.ShapeDtypeStruct((2,) + value.shape, value.dtype),
        in_specs=[pl.BlockSpec(memory_space=pltpu.VMEM)],
        out_specs=pl.BlockSpec(memory_space=pltpu.VMEM),
        scratch_shapes=[pltpu.SemaphoreType.DMA(()), pltpu.SemaphoreType.DMA(()), pltpu.SemaphoreType.DMA(())],
        compiler_params=pltpu.CompilerParams(collective_id=collective, has_side_effects=True),
    )(value)


def pair_send_kernel(x_ref, o_ref, send_sem, recv_sem):
    partner = pair_barrier()
    rows = o_ref.shape[0]
    copy = pltpu.make_async_remote_copy(
        src_ref=x_ref.at[pl.ds(rows, rows)],
        dst_ref=o_ref,
        send_sem=send_sem,
        recv_sem=recv_sem,
        device_id=partner,
        device_id_type=pl.DeviceIdType.MESH,
    )
    copy.start()
    copy.wait()


def pair_send(value, collective):
    return pl.pallas_call(
        pair_send_kernel,
        out_shape=jax.ShapeDtypeStruct((value.shape[0] // 2, value.shape[1]), value.dtype),
        in_specs=[pl.BlockSpec(memory_space=pltpu.VMEM)],
        out_specs=pl.BlockSpec(memory_space=pltpu.VMEM),
        scratch_shapes=[pltpu.SemaphoreType.DMA(()), pltpu.SemaphoreType.DMA(())],
        compiler_params=pltpu.CompilerParams(collective_id=collective, has_side_effects=True),
    )(value)


def shards(tokens, norm_gain, w_gate, w_up, w_down, block_counts, gate_prob):
    segment_index = lax.axis_index("segment")
    segment_count = lax.axis_size("segment")
    shard_count = lax.axis_size("shard")
    hidden_count = w_gate.shape[2]
    per_expert = FF // hidden_count
    zero_blocks = block_counts[0]
    row_gain = norm_gain[0]
    gate_part = w_gate[0]
    up_part = w_up[0]
    down_part = w_down[0]
    probs = gate_prob[0]
    local_rows = tokens.shape[1]
    width = tokens.shape[2]
    piece_rows = 2 * local_rows * width // LANES
    chips = shard_count // 2
    ring_z = 8
    ring_y = chips // ring_z
    carried = tokens
    stored = jnp.zeros_like(tokens)
    for tick in range(segment_count):
        normed = normalize(carried, row_gain)
        pieces = jnp.stack([normed[0:2], normed[1:3]]).reshape(2, piece_rows, LANES)
        block_rows = ring_gather(pieces, ring_y, ring_z, 0).reshape(shard_count * 2 * local_rows, width)
        partial_sum = expert(block_rows, gate_part, up_part, down_part)
        half = partial_sum.shape[0] // 2
        chip_sum = (partial_sum[:half] + pair_send(partial_sum, 2)).astype(jnp.bfloat16)
        received = chip_exchange(chip_sum.reshape(chips, piece_rows, LANES), ring_y, ring_z, 0, 3)
        received = received.astype(jnp.float32)
        received = received.reshape(2, chips // 2, 2, local_rows, width)
        first, second = jnp.sum(received[0], axis=0), jnp.sum(received[1], axis=0)
        middle = jnp.where(zero_blocks >= 2, first[1], second[0])
        mixed = jnp.stack([first[0], middle, second[1]])
        updated = (carried.astype(jnp.float32) + probs[:, :, None] * mixed).astype(jnp.bfloat16)
        stored = jnp.where(segment_index == tick, updated, stored)
        if tick + 1 < segment_count:
            carried = shifted(updated, "segment", 1)
    return stored[None]


def solution(mesh):
    placed = (
        P(None, "shard", None),
        P("segment", None),
        P("segment", None, "shard"),
        P("segment", None, "shard"),
        P("segment", "shard", None),
        P("segment"),
        P("segment", None, "shard"),
    )
    return jax.shard_map(
        shards,
        mesh=mesh,
        in_specs=placed,
        out_specs=P("segment", None, "shard", None),
        check_vma=False,
    )
```

```python
import functools

import jax
import jax.numpy as jnp
from jax import lax
from jax.experimental import pallas as pl
from jax.experimental.pallas import tpu as pltpu
from jax.sharding import PartitionSpec as P

FF = 16384
LANES = 128


def shifted(value, axis, steps):
    count = lax.axis_size(axis)
    initial, last = (max(0, -steps), min(count, count - steps))
    return lax.ppermute(value, axis, [(source, source + steps) for source in range(initial, last)])


def normalize(rows, row_gain):
    values = rows.astype(jnp.float32)
    scale = lax.rsqrt(jnp.mean(values * values, axis=-1, keepdims=True) + 1e-05)
    return (values * scale * row_gain).astype(jnp.bfloat16)


def signed(index):
    return (index + 1) // 2 * (2 * lax.rem(index, 2) - 1)


def chip_exchange_kernel(ring_y, ring_z, per_expert, x_ref, o_ref, send_sem, recv_sem):
    me = lax.axis_index("shard")
    segment = lax.axis_index("segment")
    core = lax.rem(me, 2)
    chip = me // 2
    y, z = chip // ring_z, lax.rem(chip, ring_z)
    chips = ring_y * ring_z

    def peer(step, sign):
        z_index = lax.rem(step, ring_z)
        y_index = lax.rem(step // ring_z + z_index, ring_y)
        peer_y = lax.rem(y + sign * signed(y_index) + ring_y, ring_y)
        peer_z = lax.rem(z + sign * signed(z_index) + ring_z, ring_z)
        return peer_y * ring_z + peer_z

    def source(dest_chip):
        if per_expert:
            return x_ref.at[dest_chip // per_expert]
        return x_ref.at[lax.rem(dest_chip, ring_z) * ring_y + dest_chip // ring_z]

    def copy_of(dest_chip, slot):
        return pltpu.make_async_remote_copy(
            src_ref=source(dest_chip),
            dst_ref=o_ref.at[slot],
            send_sem=send_sem.at[dest_chip],
            recv_sem=recv_sem.at[slot],
            device_id=(segment, dest_chip * 2 + core),
            device_id_type=pl.DeviceIdType.MESH,
        )

    barrier = pltpu.get_barrier_semaphore()

    def greet(step, carry):
        dest = peer(step, 1) * 2 + core
        pl.semaphore_signal(barrier, 1, device_id=(segment, dest), device_id_type=pl.DeviceIdType.MESH)
        return carry

    lax.fori_loop(1, chips, greet, 0)
    pl.semaphore_wait(barrier, chips - 1)

    def start(step, carry):
        copy_of(peer(step, 1), chip).start()
        return carry

    lax.fori_loop(1, chips, start, 0)
    o_ref[chip] = source(chip)[...]

    def finish(step, carry):
        copy_of(peer(step, 1), chip).wait_send()
        origin = peer(step, -1)
        copy_of(origin, origin).wait_recv()
        return carry

    lax.fori_loop(1, chips, finish, 0)


def chip_exchange(pieces, ring_y, ring_z, per_expert, collective):
    rows, lanes = pieces.shape[1], pieces.shape[2]
    chips = ring_y * ring_z
    return pl.pallas_call(
        functools.partial(chip_exchange_kernel, ring_y, ring_z, per_expert),
        out_shape=jax.ShapeDtypeStruct((chips, rows, lanes), pieces.dtype),
        in_specs=[pl.BlockSpec(memory_space=pltpu.VMEM)],
        out_specs=pl.BlockSpec(memory_space=pltpu.VMEM),
        scratch_shapes=[pltpu.SemaphoreType.DMA((chips,)), pltpu.SemaphoreType.DMA((chips,))],
        compiler_params=pltpu.CompilerParams(collective_id=collective, has_side_effects=True),
    )(pieces)


def ring_gather_kernel(ring_y, ring_z, x_ref, o_ref, send_y, recv_y, send_up, send_down, recv_z, send_c, recv_c):
    me = lax.axis_index("shard")
    segment = lax.axis_index("segment")
    core = lax.rem(me, 2)
    chip = me // 2
    y, z = chip // ring_z, lax.rem(chip, ring_z)
    half_z = ring_z // 2

    def device(peer_y, peer_z):
        return (segment, (peer_y * ring_z + peer_z) * 2 + core)

    up_z, down_z = lax.rem(z + 1, ring_z), lax.rem(z + ring_z - 1, ring_z)
    partner = (segment, me + 1 - 2 * core)
    barrier = pltpu.get_barrier_semaphore()
    for step in range(1, ring_y):
        pl.semaphore_signal(barrier, 1, device_id=device(lax.rem(y + step, ring_y), z), device_id_type=pl.DeviceIdType.MESH)
    pl.semaphore_signal(barrier, 1, device_id=device(y, up_z), device_id_type=pl.DeviceIdType.MESH)
    pl.semaphore_signal(barrier, 1, device_id=device(y, down_z), device_id_type=pl.DeviceIdType.MESH)
    pl.semaphore_signal(barrier, 1, device_id=partner, device_id_type=pl.DeviceIdType.MESH)
    pl.semaphore_wait(barrier, ring_y + 2)

    def y_copy(peer_y, slot):
        return pltpu.make_async_remote_copy(
            src_ref=x_ref.at[peer_y * 2 // ring_y],
            dst_ref=o_ref.at[0, z, slot],
            send_sem=send_y.at[peer_y],
            recv_sem=recv_y.at[slot],
            device_id=device(peer_y, z),
            device_id_type=pl.DeviceIdType.MESH,
        )

    for step in range(1, ring_y):
        y_copy(lax.rem(y + step, ring_y), y).start()
    o_ref[0, z, y] = x_ref[y * 2 // ring_y]
    for step in range(1, ring_y):
        origin = lax.rem(y + ring_y - step, ring_y)
        y_copy(origin, origin).wait_recv()
        y_copy(lax.rem(y + step, ring_y), y).wait_send()

    def z_copy(slot, peer_z, sems, index):
        return pltpu.make_async_remote_copy(
            src_ref=o_ref.at[0, slot],
            dst_ref=o_ref.at[0, slot],
            send_sem=sems.at[index],
            recv_sem=recv_z.at[slot],
            device_id=device(y, peer_z),
            device_id_type=pl.DeviceIdType.MESH,
        )

    for step in range(half_z):
        up_slot = lax.rem(z + ring_z - step, ring_z)
        if step > 0:
            z_copy(up_slot, down_z, send_up, step).wait_recv()
        z_copy(up_slot, up_z, send_up, step).start()
        if step < half_z - 1:
            down_slot = lax.rem(z + step, ring_z)
            if step > 0:
                z_copy(down_slot, up_z, send_down, step).wait_recv()
            z_copy(down_slot, down_z, send_down, step).start()
    z_copy(lax.rem(z + ring_z - half_z, ring_z), down_z, send_up, 0).wait_recv()
    z_copy(lax.rem(z + half_z - 1, ring_z), up_z, send_down, 0).wait_recv()
    for step in range(half_z):
        z_copy(lax.rem(z + ring_z - step, ring_z), up_z, send_up, step).wait_send()
        if step < half_z - 1:
            z_copy(lax.rem(z + step, ring_z), down_z, send_down, step).wait_send()

    pair = pltpu.make_async_remote_copy(
        src_ref=o_ref.at[0],
        dst_ref=o_ref.at[1],
        send_sem=send_c,
        recv_sem=recv_c,
        device_id=partner,
        device_id_type=pl.DeviceIdType.MESH,
    )
    pair.start()
    pair.wait()


def ring_gather(pieces, ring_y, ring_z, collective):
    rows, lanes = pieces.shape[1], pieces.shape[2]
    return pl.pallas_call(
        functools.partial(ring_gather_kernel, ring_y, ring_z),
        out_shape=jax.ShapeDtypeStruct((2, ring_z, ring_y, rows, lanes), pieces.dtype),
        in_specs=[pl.BlockSpec(memory_space=pltpu.VMEM)],
        out_specs=pl.BlockSpec(memory_space=pltpu.VMEM),
        scratch_shapes=[
            pltpu.SemaphoreType.DMA((ring_y,)),
            pltpu.SemaphoreType.DMA((ring_y,)),
            pltpu.SemaphoreType.DMA((ring_z // 2,)),
            pltpu.SemaphoreType.DMA((ring_z // 2,)),
            pltpu.SemaphoreType.DMA((ring_z,)),
            pltpu.SemaphoreType.DMA(()),
            pltpu.SemaphoreType.DMA(()),
        ],
        compiler_params=pltpu.CompilerParams(collective_id=collective, has_side_effects=True),
    )(pieces)


def expert_kernel(x_ref, gate_ref, up_ref, down_ref, o_ref):
    rows = x_ref[...]
    gate_val = jnp.dot(rows, gate_ref[...], preferred_element_type=jnp.float32)
    up_val = jnp.dot(rows, up_ref[...], preferred_element_type=jnp.float32)
    hidden = (gate_val / (1.0 + jnp.exp(-gate_val)) * up_val).astype(jnp.bfloat16)
    term = jnp.dot(hidden, down_ref[...], preferred_element_type=jnp.float32)

    @pl.when(pl.program_id(0) == 0)
    def _():
        o_ref[...] = term

    @pl.when(pl.program_id(0) > 0)
    def _():
        o_ref[...] += term


def expert(rows, gate_part, up_part, down_part, chunk=256):
    count, width = rows.shape
    hidden = gate_part.shape[1]
    return pl.pallas_call(
        expert_kernel,
        out_shape=jax.ShapeDtypeStruct((count, width), jnp.float32),
        grid=(hidden // chunk,),
        in_specs=[
            pl.BlockSpec((count, width), lambda k: (0, 0)),
            pl.BlockSpec((width, chunk), lambda k: (0, k)),
            pl.BlockSpec((width, chunk), lambda k: (0, k)),
            pl.BlockSpec((chunk, width), lambda k: (k, 0)),
        ],
        out_specs=pl.BlockSpec((count, width), lambda k: (0, 0)),
        compiler_params=pltpu.CompilerParams(dimension_semantics=("arbitrary",)),
        cost_estimate=pl.CostEstimate(
            flops=6 * count * width * hidden,
            transcendentals=count * hidden,
            bytes_accessed=2 * (count * width + 3 * width * hidden) + 4 * count * width,
        ),
    )(rows, gate_part, up_part, down_part)


def pair_barrier():
    me = lax.axis_index("shard")
    partner = (lax.axis_index("segment"), me + 1 - 2 * lax.rem(me, 2))
    barrier = pltpu.get_barrier_semaphore()
    pl.semaphore_signal(barrier, 1, device_id=partner, device_id_type=pl.DeviceIdType.MESH)
    pl.semaphore_wait(barrier, 1)
    return partner


def pair_gather_kernel(x_ref, o_ref, send_sem, recv_sem, local_sem):
    partner = pair_barrier()
    copy = pltpu.make_async_remote_copy(
        src_ref=x_ref,
        dst_ref=o_ref.at[1],
        send_sem=send_sem,
        recv_sem=recv_sem,
        device_id=partner,
        device_id_type=pl.DeviceIdType.MESH,
    )
    copy.start()
    local = pltpu.make_async_copy(x_ref, o_ref.at[0], local_sem)
    local.start()
    local.wait()
    copy.wait()


def pair_gather(value, collective):
    return pl.pallas_call(
        pair_gather_kernel,
        out_shape=jax.ShapeDtypeStruct((2,) + value.shape, value.dtype),
        in_specs=[pl.BlockSpec(memory_space=pltpu.VMEM)],
        out_specs=pl.BlockSpec(memory_space=pltpu.VMEM),
        scratch_shapes=[pltpu.SemaphoreType.DMA(()), pltpu.SemaphoreType.DMA(()), pltpu.SemaphoreType.DMA(())],
        compiler_params=pltpu.CompilerParams(collective_id=collective, has_side_effects=True),
    )(value)


def pair_send_kernel(x_ref, o_ref, send_sem, recv_sem):
    partner = pair_barrier()
    rows = o_ref.shape[0]
    copy = pltpu.make_async_remote_copy(
        src_ref=x_ref.at[pl.ds(rows, rows)],
        dst_ref=o_ref,
        send_sem=send_sem,
        recv_sem=recv_sem,
        device_id=partner,
        device_id_type=pl.DeviceIdType.MESH,
    )
    copy.start()
    copy.wait()


def pair_send(value, collective):
    return pl.pallas_call(
        pair_send_kernel,
        out_shape=jax.ShapeDtypeStruct((value.shape[0] // 2, value.shape[1]), value.dtype),
        in_specs=[pl.BlockSpec(memory_space=pltpu.VMEM)],
        out_specs=pl.BlockSpec(memory_space=pltpu.VMEM),
        scratch_shapes=[pltpu.SemaphoreType.DMA(()), pltpu.SemaphoreType.DMA(())],
        compiler_params=pltpu.CompilerParams(collective_id=collective, has_side_effects=True),
    )(value)


def shards(tokens, norm_gain, w_gate, w_up, w_down, block_counts, gate_prob):
    segment_index = lax.axis_index("segment")
    segment_count = lax.axis_size("segment")
    shard_count = lax.axis_size("shard")
    hidden_count = w_gate.shape[2]
    per_expert = FF // hidden_count
    zero_blocks = block_counts[0]
    row_gain = norm_gain[0]
    gate_part = w_gate[0]
    up_part = w_up[0]
    down_part = w_down[0]
    probs = gate_prob[0]
    local_rows = tokens.shape[1]
    width = tokens.shape[2]
    piece_rows = 2 * local_rows * width // LANES
    chips = shard_count // 2
    ring_z = 8
    ring_y = chips // ring_z
    carried = tokens
    stored = jnp.zeros_like(tokens)
    for tick in range(segment_count):
        normed = normalize(carried, row_gain)
        pieces = jnp.stack([normed[0:2], normed[1:3]]).reshape(2, piece_rows, LANES)
        block_rows = ring_gather(pieces, ring_y, ring_z, 0).reshape(shard_count * 2 * local_rows, width)
        partial_sum = expert(block_rows, gate_part, up_part, down_part)
        half = partial_sum.shape[0] // 2
        partner_sum = pair_send(partial_sum.astype(jnp.bfloat16), 2).astype(jnp.float32)
        chip_sum = (partial_sum[:half] + partner_sum).astype(jnp.bfloat16)
        received = chip_exchange(chip_sum.reshape(chips, piece_rows, LANES), ring_y, ring_z, 0, 3)
        received = received.astype(jnp.float32)
        received = received.reshape(2, chips // 2, 2, local_rows, width)
        first, second = jnp.sum(received[0], axis=0), jnp.sum(received[1], axis=0)
        middle = jnp.where(zero_blocks >= 2, first[1], second[0])
        mixed = jnp.stack([first[0], middle, second[1]])
        updated = (carried.astype(jnp.float32) + probs[:, :, None] * mixed).astype(jnp.bfloat16)
        stored = jnp.where(segment_index == tick, updated, stored)
        if tick + 1 < segment_count:
            carried = shifted(updated, "segment", 1)
    return stored[None]


def solution(mesh):
    placed = (
        P(None, "shard", None),
        P("segment", None),
        P("segment", None, "shard"),
        P("segment", None, "shard"),
        P("segment", "shard", None),
        P("segment"),
        P("segment", None, "shard"),
    )
    return jax.shard_map(
        shards,
        mesh=mesh,
        in_specs=placed,
        out_specs=P("segment", None, "shard", None),
        check_vma=False,
    )
```

```python
import functools

import jax
import jax.numpy as jnp
from jax import lax
from jax.experimental import pallas as pl
from jax.experimental.pallas import tpu as pltpu
from jax.sharding import PartitionSpec as P

FF = 16384
LANES = 128


def shifted(value, axis, steps):
    count = lax.axis_size(axis)
    initial, last = (max(0, -steps), min(count, count - steps))
    return lax.ppermute(value, axis, [(source, source + steps) for source in range(initial, last)])


def normalize(rows, row_gain):
    values = rows.astype(jnp.float32)
    scale = lax.rsqrt(jnp.mean(values * values, axis=-1, keepdims=True) + 1e-05)
    return (values * scale * row_gain).astype(jnp.bfloat16)


def signed(index):
    return (index + 1) // 2 * (2 * lax.rem(index, 2) - 1)


def chip_exchange_kernel(ring_y, ring_z, per_expert, x_ref, o_ref, send_sem, recv_sem):
    me = lax.axis_index("shard")
    segment = lax.axis_index("segment")
    core = lax.rem(me, 2)
    chip = me // 2
    y, z = chip // ring_z, lax.rem(chip, ring_z)
    chips = ring_y * ring_z

    def peer(step, sign):
        z_index = lax.rem(step, ring_z)
        y_index = lax.rem(step // ring_z + z_index, ring_y)
        peer_y = lax.rem(y + sign * signed(y_index) + ring_y, ring_y)
        peer_z = lax.rem(z + sign * signed(z_index) + ring_z, ring_z)
        return peer_y * ring_z + peer_z

    def source(dest_chip):
        if per_expert:
            return x_ref.at[dest_chip // per_expert]
        return x_ref.at[lax.rem(dest_chip, ring_z) * ring_y + dest_chip // ring_z]

    def copy_of(dest_chip, slot):
        return pltpu.make_async_remote_copy(
            src_ref=source(dest_chip),
            dst_ref=o_ref.at[slot],
            send_sem=send_sem.at[dest_chip],
            recv_sem=recv_sem.at[slot],
            device_id=(segment, dest_chip * 2 + core),
            device_id_type=pl.DeviceIdType.MESH,
        )

    barrier = pltpu.get_barrier_semaphore()

    def greet(step, carry):
        dest = peer(step, 1) * 2 + core
        pl.semaphore_signal(barrier, 1, device_id=(segment, dest), device_id_type=pl.DeviceIdType.MESH)
        return carry

    lax.fori_loop(1, chips, greet, 0)
    pl.semaphore_wait(barrier, chips - 1)

    def start(step, carry):
        copy_of(peer(step, 1), chip).start()
        return carry

    lax.fori_loop(1, chips, start, 0)
    o_ref[chip] = source(chip)[...]

    def finish(step, carry):
        copy_of(peer(step, 1), chip).wait_send()
        origin = peer(step, -1)
        copy_of(origin, origin).wait_recv()
        return carry

    lax.fori_loop(1, chips, finish, 0)


def chip_exchange(pieces, ring_y, ring_z, per_expert, collective):
    rows, lanes = pieces.shape[1], pieces.shape[2]
    chips = ring_y * ring_z
    return pl.pallas_call(
        functools.partial(chip_exchange_kernel, ring_y, ring_z, per_expert),
        out_shape=jax.ShapeDtypeStruct((chips, rows, lanes), pieces.dtype),
        in_specs=[pl.BlockSpec(memory_space=pltpu.VMEM)],
        out_specs=pl.BlockSpec(memory_space=pltpu.VMEM),
        scratch_shapes=[pltpu.SemaphoreType.DMA((chips,)), pltpu.SemaphoreType.DMA((chips,))],
        compiler_params=pltpu.CompilerParams(collective_id=collective, has_side_effects=True),
    )(pieces)


def ring_gather_kernel(ring_y, ring_z, x_ref, o_ref, send_y, recv_y, send_up, send_down, recv_z, send_c, recv_c):
    me = lax.axis_index("shard")
    segment = lax.axis_index("segment")
    core = lax.rem(me, 2)
    chip = me // 2
    y, z = chip // ring_z, lax.rem(chip, ring_z)
    half_z = ring_z // 2

    def device(peer_y, peer_z):
        return (segment, (peer_y * ring_z + peer_z) * 2 + core)

    up_z, down_z = lax.rem(z + 1, ring_z), lax.rem(z + ring_z - 1, ring_z)
    partner = (segment, me + 1 - 2 * core)
    barrier = pltpu.get_barrier_semaphore()
    for step in range(1, ring_y):
        pl.semaphore_signal(barrier, 1, device_id=device(lax.rem(y + step, ring_y), z), device_id_type=pl.DeviceIdType.MESH)
    pl.semaphore_signal(barrier, 1, device_id=device(y, up_z), device_id_type=pl.DeviceIdType.MESH)
    pl.semaphore_signal(barrier, 1, device_id=device(y, down_z), device_id_type=pl.DeviceIdType.MESH)
    pl.semaphore_signal(barrier, 1, device_id=partner, device_id_type=pl.DeviceIdType.MESH)
    pl.semaphore_wait(barrier, ring_y + 2)

    def y_copy(peer_y, slot):
        return pltpu.make_async_remote_copy(
            src_ref=x_ref.at[peer_y * 2 // ring_y],
            dst_ref=o_ref.at[0, z, slot],
            send_sem=send_y.at[peer_y],
            recv_sem=recv_y.at[slot],
            device_id=device(peer_y, z),
            device_id_type=pl.DeviceIdType.MESH,
        )

    for step in range(1, ring_y):
        y_copy(lax.rem(y + step, ring_y), y).start()
    o_ref[0, z, y] = x_ref[y * 2 // ring_y]
    for step in range(1, ring_y):
        origin = lax.rem(y + ring_y - step, ring_y)
        y_copy(origin, origin).wait_recv()
        y_copy(lax.rem(y + step, ring_y), y).wait_send()

    def z_copy(slot, peer_z, sems, index):
        return pltpu.make_async_remote_copy(
            src_ref=o_ref.at[0, slot],
            dst_ref=o_ref.at[0, slot],
            send_sem=sems.at[index],
            recv_sem=recv_z.at[slot],
            device_id=device(y, peer_z),
            device_id_type=pl.DeviceIdType.MESH,
        )

    for step in range(half_z):
        up_slot = lax.rem(z + ring_z - step, ring_z)
        if step > 0:
            z_copy(up_slot, down_z, send_up, step).wait_recv()
        z_copy(up_slot, up_z, send_up, step).start()
        if step < half_z - 1:
            down_slot = lax.rem(z + step, ring_z)
            if step > 0:
                z_copy(down_slot, up_z, send_down, step).wait_recv()
            z_copy(down_slot, down_z, send_down, step).start()
    z_copy(lax.rem(z + ring_z - half_z, ring_z), down_z, send_up, 0).wait_recv()
    z_copy(lax.rem(z + half_z - 1, ring_z), up_z, send_down, 0).wait_recv()
    for step in range(half_z):
        z_copy(lax.rem(z + ring_z - step, ring_z), up_z, send_up, step).wait_send()
        if step < half_z - 1:
            z_copy(lax.rem(z + step, ring_z), down_z, send_down, step).wait_send()

    pair = pltpu.make_async_remote_copy(
        src_ref=o_ref.at[0],
        dst_ref=o_ref.at[1],
        send_sem=send_c,
        recv_sem=recv_c,
        device_id=partner,
        device_id_type=pl.DeviceIdType.MESH,
    )
    pair.start()
    pair.wait()


def ring_gather(pieces, ring_y, ring_z, collective):
    rows, lanes = pieces.shape[1], pieces.shape[2]
    return pl.pallas_call(
        functools.partial(ring_gather_kernel, ring_y, ring_z),
        out_shape=jax.ShapeDtypeStruct((2, ring_z, ring_y, rows, lanes), pieces.dtype),
        in_specs=[pl.BlockSpec(memory_space=pltpu.VMEM)],
        out_specs=pl.BlockSpec(memory_space=pltpu.VMEM),
        scratch_shapes=[
            pltpu.SemaphoreType.DMA((ring_y,)),
            pltpu.SemaphoreType.DMA((ring_y,)),
            pltpu.SemaphoreType.DMA((ring_z // 2,)),
            pltpu.SemaphoreType.DMA((ring_z // 2,)),
            pltpu.SemaphoreType.DMA((ring_z,)),
            pltpu.SemaphoreType.DMA(()),
            pltpu.SemaphoreType.DMA(()),
        ],
        compiler_params=pltpu.CompilerParams(collective_id=collective, has_side_effects=True),
    )(pieces)


def expert_kernel(x_ref, gate_ref, up_ref, down_ref, o_ref):
    rows = x_ref[...]
    gate_val = jnp.dot(rows, gate_ref[...], preferred_element_type=jnp.float32)
    up_val = jnp.dot(rows, up_ref[...], preferred_element_type=jnp.float32)
    hidden = (gate_val / (1.0 + jnp.exp(-gate_val)) * up_val).astype(jnp.bfloat16)
    term = jnp.dot(hidden, down_ref[...], preferred_element_type=jnp.float32)

    @pl.when(pl.program_id(0) == 0)
    def _():
        o_ref[...] = term

    @pl.when(pl.program_id(0) > 0)
    def _():
        o_ref[...] += term


def expert(rows, gate_part, up_part, down_part, chunk=256):
    count, width = rows.shape
    hidden = gate_part.shape[1]
    return pl.pallas_call(
        expert_kernel,
        out_shape=jax.ShapeDtypeStruct((count, width), jnp.float32),
        grid=(hidden // chunk,),
        in_specs=[
            pl.BlockSpec((count, width), lambda k: (0, 0)),
            pl.BlockSpec((width, chunk), lambda k: (0, k)),
            pl.BlockSpec((width, chunk), lambda k: (0, k)),
            pl.BlockSpec((chunk, width), lambda k: (k, 0)),
        ],
        out_specs=pl.BlockSpec((count, width), lambda k: (0, 0)),
        compiler_params=pltpu.CompilerParams(dimension_semantics=("arbitrary",)),
        cost_estimate=pl.CostEstimate(
            flops=6 * count * width * hidden,
            transcendentals=count * hidden,
            bytes_accessed=2 * (count * width + 3 * width * hidden) + 4 * count * width,
        ),
    )(rows, gate_part, up_part, down_part)


def segment_shift_kernel(x_ref, o_ref, send_sem, recv_sem):
    me = lax.axis_index("shard")
    segment = lax.axis_index("segment")
    count = lax.axis_size("segment")
    after = (lax.rem(segment + 1, count), me)
    before = (lax.rem(segment + count - 1, count), me)
    barrier = pltpu.get_barrier_semaphore()
    pl.semaphore_signal(barrier, 1, device_id=after, device_id_type=pl.DeviceIdType.MESH)
    pl.semaphore_signal(barrier, 1, device_id=before, device_id_type=pl.DeviceIdType.MESH)
    pl.semaphore_wait(barrier, 2)
    copies = [
        pltpu.make_async_remote_copy(
            src_ref=x_ref,
            dst_ref=o_ref.at[slot],
            send_sem=send_sem.at[slot],
            recv_sem=recv_sem.at[slot],
            device_id=peer,
            device_id_type=pl.DeviceIdType.MESH,
        )
        for slot, peer in ((0, after), (1, before))
    ]
    for copy in copies:
        copy.start()
    for copy in copies:
        copy.wait()


def segment_shift(value, collective):
    return pl.pallas_call(
        segment_shift_kernel,
        out_shape=jax.ShapeDtypeStruct((2,) + value.shape, value.dtype),
        in_specs=[pl.BlockSpec(memory_space=pltpu.VMEM)],
        out_specs=pl.BlockSpec(memory_space=pltpu.VMEM),
        scratch_shapes=[pltpu.SemaphoreType.DMA((2,)), pltpu.SemaphoreType.DMA((2,))],
        compiler_params=pltpu.CompilerParams(collective_id=collective, has_side_effects=True),
    )(value)[0]


def pair_barrier():
    me = lax.axis_index("shard")
    partner = (lax.axis_index("segment"), me + 1 - 2 * lax.rem(me, 2))
    barrier = pltpu.get_barrier_semaphore()
    pl.semaphore_signal(barrier, 1, device_id=partner, device_id_type=pl.DeviceIdType.MESH)
    pl.semaphore_wait(barrier, 1)
    return partner


def pair_gather_kernel(x_ref, o_ref, send_sem, recv_sem, local_sem):
    partner = pair_barrier()
    copy = pltpu.make_async_remote_copy(
        src_ref=x_ref,
        dst_ref=o_ref.at[1],
        send_sem=send_sem,
        recv_sem=recv_sem,
        device_id=partner,
        device_id_type=pl.DeviceIdType.MESH,
    )
    copy.start()
    local = pltpu.make_async_copy(x_ref, o_ref.at[0], local_sem)
    local.start()
    local.wait()
    copy.wait()


def pair_gather(value, collective):
    return pl.pallas_call(
        pair_gather_kernel,
        out_shape=jax.ShapeDtypeStruct((2,) + value.shape, value.dtype),
        in_specs=[pl.BlockSpec(memory_space=pltpu.VMEM)],
        out_specs=pl.BlockSpec(memory_space=pltpu.VMEM),
        scratch_shapes=[pltpu.SemaphoreType.DMA(()), pltpu.SemaphoreType.DMA(()), pltpu.SemaphoreType.DMA(())],
        compiler_params=pltpu.CompilerParams(collective_id=collective, has_side_effects=True),
    )(value)


def pair_send_kernel(x_ref, o_ref, send_sem, recv_sem):
    partner = pair_barrier()
    rows = o_ref.shape[0]
    copy = pltpu.make_async_remote_copy(
        src_ref=x_ref.at[pl.ds(rows, rows)],
        dst_ref=o_ref,
        send_sem=send_sem,
        recv_sem=recv_sem,
        device_id=partner,
        device_id_type=pl.DeviceIdType.MESH,
    )
    copy.start()
    copy.wait()


def pair_send(value, collective):
    return pl.pallas_call(
        pair_send_kernel,
        out_shape=jax.ShapeDtypeStruct((value.shape[0] // 2, value.shape[1]), value.dtype),
        in_specs=[pl.BlockSpec(memory_space=pltpu.VMEM)],
        out_specs=pl.BlockSpec(memory_space=pltpu.VMEM),
        scratch_shapes=[pltpu.SemaphoreType.DMA(()), pltpu.SemaphoreType.DMA(())],
        compiler_params=pltpu.CompilerParams(collective_id=collective, has_side_effects=True),
    )(value)


def shards(tokens, norm_gain, w_gate, w_up, w_down, block_counts, gate_prob):
    segment_index = lax.axis_index("segment")
    segment_count = lax.axis_size("segment")
    shard_count = lax.axis_size("shard")
    hidden_count = w_gate.shape[2]
    per_expert = FF // hidden_count
    zero_blocks = block_counts[0]
    row_gain = norm_gain[0]
    gate_part = w_gate[0]
    up_part = w_up[0]
    down_part = w_down[0]
    probs = gate_prob[0]
    local_rows = tokens.shape[1]
    width = tokens.shape[2]
    piece_rows = 2 * local_rows * width // LANES
    chips = shard_count // 2
    ring_z = 8
    ring_y = chips // ring_z
    carried = tokens
    stored = jnp.zeros_like(tokens)
    for tick in range(segment_count):
        normed = normalize(carried, row_gain)
        pieces = jnp.stack([normed[0:2], normed[1:3]]).reshape(2, piece_rows, LANES)
        block_rows = ring_gather(pieces, ring_y, ring_z, 0).reshape(shard_count * 2 * local_rows, width)
        partial_sum = expert(block_rows, gate_part, up_part, down_part)
        half = partial_sum.shape[0] // 2
        chip_sum = (partial_sum[:half] + pair_send(partial_sum, 2)).astype(jnp.bfloat16)
        received = chip_exchange(chip_sum.reshape(chips, piece_rows, LANES), ring_y, ring_z, 0, 3)
        received = received.astype(jnp.float32)
        received = received.reshape(2, chips // 2, 2, local_rows, width)
        first, second = jnp.sum(received[0], axis=0), jnp.sum(received[1], axis=0)
        middle = jnp.where(zero_blocks >= 2, first[1], second[0])
        mixed = jnp.stack([first[0], middle, second[1]])
        updated = (carried.astype(jnp.float32) + probs[:, :, None] * mixed).astype(jnp.bfloat16)
        stored = jnp.where(segment_index == tick, updated, stored)
        if tick + 1 < segment_count:
            carried = segment_shift(updated, 4)
    return stored[None]


def solution(mesh):
    placed = (
        P(None, "shard", None),
        P("segment", None),
        P("segment", None, "shard"),
        P("segment", None, "shard"),
        P("segment", "shard", None),
        P("segment"),
        P("segment", None, "shard"),
    )
    return jax.shard_map(
        shards,
        mesh=mesh,
        in_specs=placed,
        out_specs=P("segment", None, "shard", None),
        check_vma=False,
    )
```

```python
import functools

import jax
import jax.numpy as jnp
from jax import lax
from jax.experimental import pallas as pl
from jax.experimental.pallas import tpu as pltpu
from jax.sharding import PartitionSpec as P

FF = 16384
LANES = 128


def shifted(value, axis, steps):
    count = lax.axis_size(axis)
    initial, last = (max(0, -steps), min(count, count - steps))
    return lax.ppermute(value, axis, [(source, source + steps) for source in range(initial, last)])


def normalize(rows, row_gain):
    values = rows.astype(jnp.float32)
    scale = lax.rsqrt(jnp.mean(values * values, axis=-1, keepdims=True) + 1e-05)
    return (values * scale * row_gain).astype(jnp.bfloat16)


def signed(index):
    return (index + 1) // 2 * (2 * lax.rem(index, 2) - 1)


def chip_exchange_kernel(ring_y, ring_z, per_expert, x_ref, o_ref, send_sem, recv_sem):
    me = lax.axis_index("shard")
    segment = lax.axis_index("segment")
    core = lax.rem(me, 2)
    chip = me // 2
    y, z = chip // ring_z, lax.rem(chip, ring_z)
    chips = ring_y * ring_z

    def peer(step, sign):
        z_index = lax.rem(step, ring_z)
        y_index = lax.rem(step // ring_z + z_index, ring_y)
        peer_y = lax.rem(y + sign * signed(y_index) + ring_y, ring_y)
        peer_z = lax.rem(z + sign * signed(z_index) + ring_z, ring_z)
        return peer_y * ring_z + peer_z

    def source(dest_chip):
        if per_expert:
            return x_ref.at[dest_chip // per_expert]
        return x_ref.at[lax.rem(dest_chip, ring_z) * ring_y + dest_chip // ring_z]

    def copy_of(dest_chip, slot):
        return pltpu.make_async_remote_copy(
            src_ref=source(dest_chip),
            dst_ref=o_ref.at[slot],
            send_sem=send_sem.at[dest_chip],
            recv_sem=recv_sem.at[slot],
            device_id=(segment, dest_chip * 2 + core),
            device_id_type=pl.DeviceIdType.MESH,
        )

    barrier = pltpu.get_barrier_semaphore()

    def greet(step, carry):
        dest = peer(step, 1) * 2 + core
        pl.semaphore_signal(barrier, 1, device_id=(segment, dest), device_id_type=pl.DeviceIdType.MESH)
        return carry

    lax.fori_loop(1, chips, greet, 0)
    pl.semaphore_wait(barrier, chips - 1)

    def start(step, carry):
        copy_of(peer(step, 1), chip).start()
        return carry

    lax.fori_loop(1, chips, start, 0)
    o_ref[chip] = source(chip)[...]

    def finish(step, carry):
        copy_of(peer(step, 1), chip).wait_send()
        origin = peer(step, -1)
        copy_of(origin, origin).wait_recv()
        return carry

    lax.fori_loop(1, chips, finish, 0)


def chip_exchange(pieces, ring_y, ring_z, per_expert, collective):
    rows, lanes = pieces.shape[1], pieces.shape[2]
    chips = ring_y * ring_z
    return pl.pallas_call(
        functools.partial(chip_exchange_kernel, ring_y, ring_z, per_expert),
        out_shape=jax.ShapeDtypeStruct((chips, rows, lanes), pieces.dtype),
        in_specs=[pl.BlockSpec(memory_space=pltpu.VMEM)],
        out_specs=pl.BlockSpec(memory_space=pltpu.VMEM),
        scratch_shapes=[pltpu.SemaphoreType.DMA((chips,)), pltpu.SemaphoreType.DMA((chips,))],
        compiler_params=pltpu.CompilerParams(collective_id=collective, has_side_effects=True),
    )(pieces)


def ring_gather_kernel(ring_y, ring_z, x_ref, o_ref, send_y, recv_y, send_up, send_down, recv_z, send_c, recv_c):
    me = lax.axis_index("shard")
    segment = lax.axis_index("segment")
    core = lax.rem(me, 2)
    chip = me // 2
    y, z = chip // ring_z, lax.rem(chip, ring_z)
    half_z = ring_z // 2

    def device(peer_y, peer_z):
        return (segment, (peer_y * ring_z + peer_z) * 2 + core)

    up_z, down_z = lax.rem(z + 1, ring_z), lax.rem(z + ring_z - 1, ring_z)
    partner = (segment, me + 1 - 2 * core)
    barrier = pltpu.get_barrier_semaphore()
    for step in range(1, ring_y):
        pl.semaphore_signal(barrier, 1, device_id=device(lax.rem(y + step, ring_y), z), device_id_type=pl.DeviceIdType.MESH)
    pl.semaphore_signal(barrier, 1, device_id=device(y, up_z), device_id_type=pl.DeviceIdType.MESH)
    pl.semaphore_signal(barrier, 1, device_id=device(y, down_z), device_id_type=pl.DeviceIdType.MESH)
    pl.semaphore_signal(barrier, 1, device_id=partner, device_id_type=pl.DeviceIdType.MESH)
    pl.semaphore_wait(barrier, ring_y + 2)

    def y_copy(peer_y, slot):
        return pltpu.make_async_remote_copy(
            src_ref=x_ref.at[peer_y * 2 // ring_y],
            dst_ref=o_ref.at[0, z, slot],
            send_sem=send_y.at[peer_y],
            recv_sem=recv_y.at[slot],
            device_id=device(peer_y, z),
            device_id_type=pl.DeviceIdType.MESH,
        )

    for step in range(1, ring_y):
        y_copy(lax.rem(y + step, ring_y), y).start()
    o_ref[0, z, y] = x_ref[y * 2 // ring_y]
    for step in range(1, ring_y):
        origin = lax.rem(y + ring_y - step, ring_y)
        y_copy(origin, origin).wait_recv()
        y_copy(lax.rem(y + step, ring_y), y).wait_send()

    def pair_copy(slot):
        return pltpu.make_async_remote_copy(
            src_ref=o_ref.at[0, slot],
            dst_ref=o_ref.at[1, slot],
            send_sem=send_c.at[slot],
            recv_sem=recv_c.at[slot],
            device_id=partner,
            device_id_type=pl.DeviceIdType.MESH,
        )

    pair_copy(z).start()

    def z_copy(slot, peer_z, sems, index):
        return pltpu.make_async_remote_copy(
            src_ref=o_ref.at[0, slot],
            dst_ref=o_ref.at[0, slot],
            send_sem=sems.at[index],
            recv_sem=recv_z.at[slot],
            device_id=device(y, peer_z),
            device_id_type=pl.DeviceIdType.MESH,
        )

    for step in range(half_z):
        up_slot = lax.rem(z + ring_z - step, ring_z)
        if step > 0:
            z_copy(up_slot, down_z, send_up, step).wait_recv()
            pair_copy(up_slot).start()
        z_copy(up_slot, up_z, send_up, step).start()
        if step < half_z - 1:
            down_slot = lax.rem(z + step, ring_z)
            if step > 0:
                z_copy(down_slot, up_z, send_down, step).wait_recv()
                pair_copy(down_slot).start()
            z_copy(down_slot, down_z, send_down, step).start()
    last_up = lax.rem(z + ring_z - half_z, ring_z)
    z_copy(last_up, down_z, send_up, 0).wait_recv()
    pair_copy(last_up).start()
    last_down = lax.rem(z + half_z - 1, ring_z)
    z_copy(last_down, up_z, send_down, 0).wait_recv()
    pair_copy(last_down).start()
    for step in range(half_z):
        z_copy(lax.rem(z + ring_z - step, ring_z), up_z, send_up, step).wait_send()
        if step < half_z - 1:
            z_copy(lax.rem(z + step, ring_z), down_z, send_down, step).wait_send()

    for slot in range(ring_z):
        pair_copy(slot).wait_send()
        pair_copy(slot).wait_recv()


def ring_gather(pieces, ring_y, ring_z, collective):
    rows, lanes = pieces.shape[1], pieces.shape[2]
    return pl.pallas_call(
        functools.partial(ring_gather_kernel, ring_y, ring_z),
        out_shape=jax.ShapeDtypeStruct((2, ring_z, ring_y, rows, lanes), pieces.dtype),
        in_specs=[pl.BlockSpec(memory_space=pltpu.VMEM)],
        out_specs=pl.BlockSpec(memory_space=pltpu.VMEM),
        scratch_shapes=[
            pltpu.SemaphoreType.DMA((ring_y,)),
            pltpu.SemaphoreType.DMA((ring_y,)),
            pltpu.SemaphoreType.DMA((ring_z // 2,)),
            pltpu.SemaphoreType.DMA((ring_z // 2,)),
            pltpu.SemaphoreType.DMA((ring_z,)),
            pltpu.SemaphoreType.DMA((ring_z,)),
            pltpu.SemaphoreType.DMA((ring_z,)),
        ],
        compiler_params=pltpu.CompilerParams(collective_id=collective, has_side_effects=True),
    )(pieces)


def expert_kernel(x_ref, gate_ref, up_ref, down_ref, o_ref):
    rows = x_ref[...]
    gate_val = jnp.dot(rows, gate_ref[...], preferred_element_type=jnp.float32)
    up_val = jnp.dot(rows, up_ref[...], preferred_element_type=jnp.float32)
    hidden = (gate_val / (1.0 + jnp.exp(-gate_val)) * up_val).astype(jnp.bfloat16)
    term = jnp.dot(hidden, down_ref[...], preferred_element_type=jnp.float32)

    @pl.when(pl.program_id(0) == 0)
    def _():
        o_ref[...] = term

    @pl.when(pl.program_id(0) > 0)
    def _():
        o_ref[...] += term


def expert(rows, gate_part, up_part, down_part, chunk=256):
    count, width = rows.shape
    hidden = gate_part.shape[1]
    return pl.pallas_call(
        expert_kernel,
        out_shape=jax.ShapeDtypeStruct((count, width), jnp.float32),
        grid=(hidden // chunk,),
        in_specs=[
            pl.BlockSpec((count, width), lambda k: (0, 0)),
            pl.BlockSpec((width, chunk), lambda k: (0, k)),
            pl.BlockSpec((width, chunk), lambda k: (0, k)),
            pl.BlockSpec((chunk, width), lambda k: (k, 0)),
        ],
        out_specs=pl.BlockSpec((count, width), lambda k: (0, 0)),
        compiler_params=pltpu.CompilerParams(dimension_semantics=("arbitrary",)),
        cost_estimate=pl.CostEstimate(
            flops=6 * count * width * hidden,
            transcendentals=count * hidden,
            bytes_accessed=2 * (count * width + 3 * width * hidden) + 4 * count * width,
        ),
    )(rows, gate_part, up_part, down_part)


def pair_barrier():
    me = lax.axis_index("shard")
    partner = (lax.axis_index("segment"), me + 1 - 2 * lax.rem(me, 2))
    barrier = pltpu.get_barrier_semaphore()
    pl.semaphore_signal(barrier, 1, device_id=partner, device_id_type=pl.DeviceIdType.MESH)
    pl.semaphore_wait(barrier, 1)
    return partner


def pair_gather_kernel(x_ref, o_ref, send_sem, recv_sem, local_sem):
    partner = pair_barrier()
    copy = pltpu.make_async_remote_copy(
        src_ref=x_ref,
        dst_ref=o_ref.at[1],
        send_sem=send_sem,
        recv_sem=recv_sem,
        device_id=partner,
        device_id_type=pl.DeviceIdType.MESH,
    )
    copy.start()
    local = pltpu.make_async_copy(x_ref, o_ref.at[0], local_sem)
    local.start()
    local.wait()
    copy.wait()


def pair_gather(value, collective):
    return pl.pallas_call(
        pair_gather_kernel,
        out_shape=jax.ShapeDtypeStruct((2,) + value.shape, value.dtype),
        in_specs=[pl.BlockSpec(memory_space=pltpu.VMEM)],
        out_specs=pl.BlockSpec(memory_space=pltpu.VMEM),
        scratch_shapes=[pltpu.SemaphoreType.DMA(()), pltpu.SemaphoreType.DMA(()), pltpu.SemaphoreType.DMA(())],
        compiler_params=pltpu.CompilerParams(collective_id=collective, has_side_effects=True),
    )(value)


def pair_send_kernel(x_ref, o_ref, send_sem, recv_sem):
    partner = pair_barrier()
    rows = o_ref.shape[0]
    copy = pltpu.make_async_remote_copy(
        src_ref=x_ref.at[pl.ds(rows, rows)],
        dst_ref=o_ref,
        send_sem=send_sem,
        recv_sem=recv_sem,
        device_id=partner,
        device_id_type=pl.DeviceIdType.MESH,
    )
    copy.start()
    copy.wait()


def pair_send(value, collective):
    return pl.pallas_call(
        pair_send_kernel,
        out_shape=jax.ShapeDtypeStruct((value.shape[0] // 2, value.shape[1]), value.dtype),
        in_specs=[pl.BlockSpec(memory_space=pltpu.VMEM)],
        out_specs=pl.BlockSpec(memory_space=pltpu.VMEM),
        scratch_shapes=[pltpu.SemaphoreType.DMA(()), pltpu.SemaphoreType.DMA(())],
        compiler_params=pltpu.CompilerParams(collective_id=collective, has_side_effects=True),
    )(value)


def shards(tokens, norm_gain, w_gate, w_up, w_down, block_counts, gate_prob):
    segment_index = lax.axis_index("segment")
    segment_count = lax.axis_size("segment")
    shard_count = lax.axis_size("shard")
    hidden_count = w_gate.shape[2]
    per_expert = FF // hidden_count
    zero_blocks = block_counts[0]
    row_gain = norm_gain[0]
    gate_part = w_gate[0]
    up_part = w_up[0]
    down_part = w_down[0]
    probs = gate_prob[0]
    local_rows = tokens.shape[1]
    width = tokens.shape[2]
    piece_rows = 2 * local_rows * width // LANES
    chips = shard_count // 2
    ring_z = 8
    ring_y = chips // ring_z
    carried = tokens
    stored = jnp.zeros_like(tokens)
    for tick in range(segment_count):
        normed = normalize(carried, row_gain)
        pieces = jnp.stack([normed[0:2], normed[1:3]]).reshape(2, piece_rows, LANES)
        block_rows = ring_gather(pieces, ring_y, ring_z, 0).reshape(shard_count * 2 * local_rows, width)
        partial_sum = expert(block_rows, gate_part, up_part, down_part)
        half = partial_sum.shape[0] // 2
        chip_sum = (partial_sum[:half] + pair_send(partial_sum, 2)).astype(jnp.bfloat16)
        received = chip_exchange(chip_sum.reshape(chips, piece_rows, LANES), ring_y, ring_z, 0, 3)
        received = received.astype(jnp.float32)
        received = received.reshape(2, chips // 2, 2, local_rows, width)
        first, second = jnp.sum(received[0], axis=0), jnp.sum(received[1], axis=0)
        middle = jnp.where(zero_blocks >= 2, first[1], second[0])
        mixed = jnp.stack([first[0], middle, second[1]])
        updated = (carried.astype(jnp.float32) + probs[:, :, None] * mixed).astype(jnp.bfloat16)
        stored = jnp.where(segment_index == tick, updated, stored)
        if tick + 1 < segment_count:
            carried = shifted(updated, "segment", 1)
    return stored[None]


def solution(mesh):
    placed = (
        P(None, "shard", None),
        P("segment", None),
        P("segment", None, "shard"),
        P("segment", None, "shard"),
        P("segment", "shard", None),
        P("segment"),
        P("segment", None, "shard"),
    )
    return jax.shard_map(
        shards,
        mesh=mesh,
        in_specs=placed,
        out_specs=P("segment", None, "shard", None),
        check_vma=False,
    )
```

```python
import functools

import jax
import jax.numpy as jnp
from jax import lax
from jax.experimental import pallas as pl
from jax.experimental.pallas import tpu as pltpu
from jax.sharding import PartitionSpec as P

FF = 16384
LANES = 128


def shifted(value, axis, steps):
    count = lax.axis_size(axis)
    initial, last = (max(0, -steps), min(count, count - steps))
    return lax.ppermute(value, axis, [(source, source + steps) for source in range(initial, last)])


def normalize(rows, row_gain):
    values = rows.astype(jnp.float32)
    scale = lax.rsqrt(jnp.mean(values * values, axis=-1, keepdims=True) + 1e-05)
    return (values * scale * row_gain).astype(jnp.bfloat16)


def signed(index):
    return (index + 1) // 2 * (2 * lax.rem(index, 2) - 1)


def chip_exchange_kernel(ring_y, ring_z, per_expert, x_ref, o_ref, send_sem, recv_sem):
    me = lax.axis_index("shard")
    segment = lax.axis_index("segment")
    core = lax.rem(me, 2)
    chip = me // 2
    y, z = chip // ring_z, lax.rem(chip, ring_z)
    chips = ring_y * ring_z

    def peer(step, sign):
        z_index = lax.rem(step, ring_z)
        y_index = lax.rem(step // ring_z + z_index, ring_y)
        peer_y = lax.rem(y + sign * signed(y_index) + ring_y, ring_y)
        peer_z = lax.rem(z + sign * signed(z_index) + ring_z, ring_z)
        return peer_y * ring_z + peer_z

    def source(dest_chip):
        if per_expert:
            return x_ref.at[dest_chip // per_expert]
        return x_ref.at[lax.rem(dest_chip, ring_z) * ring_y + dest_chip // ring_z]

    def copy_of(dest_chip, slot):
        return pltpu.make_async_remote_copy(
            src_ref=source(dest_chip),
            dst_ref=o_ref.at[slot],
            send_sem=send_sem.at[dest_chip],
            recv_sem=recv_sem.at[slot],
            device_id=(segment, dest_chip * 2 + core),
            device_id_type=pl.DeviceIdType.MESH,
        )

    barrier = pltpu.get_barrier_semaphore()

    def greet(step, carry):
        dest = peer(step, 1) * 2 + core
        pl.semaphore_signal(barrier, 1, device_id=(segment, dest), device_id_type=pl.DeviceIdType.MESH)
        return carry

    lax.fori_loop(1, chips, greet, 0)
    pl.semaphore_wait(barrier, chips - 1)

    def start(step, carry):
        copy_of(peer(step, 1), chip).start()
        return carry

    lax.fori_loop(1, chips, start, 0)
    o_ref[chip] = source(chip)[...]

    def finish(step, carry):
        copy_of(peer(step, 1), chip).wait_send()
        origin = peer(step, -1)
        copy_of(origin, origin).wait_recv()
        return carry

    lax.fori_loop(1, chips, finish, 0)


def chip_exchange(pieces, ring_y, ring_z, per_expert, collective):
    rows, lanes = pieces.shape[1], pieces.shape[2]
    chips = ring_y * ring_z
    return pl.pallas_call(
        functools.partial(chip_exchange_kernel, ring_y, ring_z, per_expert),
        out_shape=jax.ShapeDtypeStruct((chips, rows, lanes), pieces.dtype),
        in_specs=[pl.BlockSpec(memory_space=pltpu.VMEM)],
        out_specs=pl.BlockSpec(memory_space=pltpu.VMEM),
        scratch_shapes=[pltpu.SemaphoreType.DMA((chips,)), pltpu.SemaphoreType.DMA((chips,))],
        compiler_params=pltpu.CompilerParams(collective_id=collective, has_side_effects=True),
    )(pieces)


def ring_gather_kernel(ring_y, ring_z, x_ref, o_ref, send_y, recv_y, send_up, send_down, recv_z, send_c, recv_c):
    me = lax.axis_index("shard")
    segment = lax.axis_index("segment")
    core = lax.rem(me, 2)
    chip = me // 2
    y, z = chip // ring_z, lax.rem(chip, ring_z)
    half_z = ring_z // 2

    def device(peer_y, peer_z):
        return (segment, (peer_y * ring_z + peer_z) * 2 + core)

    up_z, down_z = lax.rem(z + 1, ring_z), lax.rem(z + ring_z - 1, ring_z)
    partner = (segment, me + 1 - 2 * core)
    barrier = pltpu.get_barrier_semaphore()
    for step in range(1, ring_y):
        pl.semaphore_signal(barrier, 1, device_id=device(lax.rem(y + step, ring_y), z), device_id_type=pl.DeviceIdType.MESH)
    pl.semaphore_signal(barrier, 1, device_id=device(y, up_z), device_id_type=pl.DeviceIdType.MESH)
    pl.semaphore_signal(barrier, 1, device_id=device(y, down_z), device_id_type=pl.DeviceIdType.MESH)
    pl.semaphore_signal(barrier, 1, device_id=partner, device_id_type=pl.DeviceIdType.MESH)
    pl.semaphore_wait(barrier, ring_y + 2)

    def y_copy(peer_y, slot):
        return pltpu.make_async_remote_copy(
            src_ref=x_ref.at[peer_y * 2 // ring_y],
            dst_ref=o_ref.at[0, z, slot],
            send_sem=send_y.at[peer_y],
            recv_sem=recv_y.at[slot],
            device_id=device(peer_y, z),
            device_id_type=pl.DeviceIdType.MESH,
        )

    for step in range(1, ring_y):
        y_copy(lax.rem(y + step, ring_y), y).start()
    o_ref[0, z, y] = x_ref[y * 2 // ring_y]
    for step in range(1, ring_y):
        origin = lax.rem(y + ring_y - step, ring_y)
        y_copy(origin, origin).wait_recv()
        y_copy(lax.rem(y + step, ring_y), y).wait_send()

    def pair_copy(slot):
        return pltpu.make_async_remote_copy(
            src_ref=o_ref.at[0, slot],
            dst_ref=o_ref.at[1, slot],
            send_sem=send_c.at[slot],
            recv_sem=recv_c.at[slot],
            device_id=partner,
            device_id_type=pl.DeviceIdType.MESH,
        )

    pair_copy(z).start()

    def z_copy(slot, peer_z, sems, index):
        return pltpu.make_async_remote_copy(
            src_ref=o_ref.at[0, slot],
            dst_ref=o_ref.at[0, slot],
            send_sem=sems.at[index],
            recv_sem=recv_z.at[slot],
            device_id=device(y, peer_z),
            device_id_type=pl.DeviceIdType.MESH,
        )

    for step in range(half_z):
        up_slot = lax.rem(z + ring_z - step, ring_z)
        if step > 0:
            z_copy(up_slot, down_z, send_up, step).wait_recv()
            pair_copy(up_slot).start()
        z_copy(up_slot, up_z, send_up, step).start()
        if step < half_z - 1:
            down_slot = lax.rem(z + step, ring_z)
            if step > 0:
                z_copy(down_slot, up_z, send_down, step).wait_recv()
                pair_copy(down_slot).start()
            z_copy(down_slot, down_z, send_down, step).start()
    last_up = lax.rem(z + ring_z - half_z, ring_z)
    z_copy(last_up, down_z, send_up, 0).wait_recv()
    pair_copy(last_up).start()
    last_down = lax.rem(z + half_z - 1, ring_z)
    z_copy(last_down, up_z, send_down, 0).wait_recv()
    pair_copy(last_down).start()
    for step in range(half_z):
        z_copy(lax.rem(z + ring_z - step, ring_z), up_z, send_up, step).wait_send()
        if step < half_z - 1:
            z_copy(lax.rem(z + step, ring_z), down_z, send_down, step).wait_send()

    for slot in range(ring_z):
        pair_copy(slot).wait_send()
        pair_copy(slot).wait_recv()


def ring_gather(pieces, ring_y, ring_z, collective):
    rows, lanes = pieces.shape[1], pieces.shape[2]
    return pl.pallas_call(
        functools.partial(ring_gather_kernel, ring_y, ring_z),
        out_shape=jax.ShapeDtypeStruct((2, ring_z, ring_y, rows, lanes), pieces.dtype),
        in_specs=[pl.BlockSpec(memory_space=pltpu.VMEM)],
        out_specs=pl.BlockSpec(memory_space=pltpu.VMEM),
        scratch_shapes=[
            pltpu.SemaphoreType.DMA((ring_y,)),
            pltpu.SemaphoreType.DMA((ring_y,)),
            pltpu.SemaphoreType.DMA((ring_z // 2,)),
            pltpu.SemaphoreType.DMA((ring_z // 2,)),
            pltpu.SemaphoreType.DMA((ring_z,)),
            pltpu.SemaphoreType.DMA((ring_z,)),
            pltpu.SemaphoreType.DMA((ring_z,)),
        ],
        compiler_params=pltpu.CompilerParams(collective_id=collective, has_side_effects=True),
    )(pieces)


def expert_kernel(x_ref, gate_ref, up_ref, down_ref, own_ref, other_ref, acc_ref):
    step, last = pl.program_id(0), pl.num_programs(0) - 1
    rows = x_ref[...]
    gate_val = jnp.dot(rows, gate_ref[...], preferred_element_type=jnp.float32)
    up_val = jnp.dot(rows, up_ref[...], preferred_element_type=jnp.float32)
    hidden = (gate_val / (1.0 + jnp.exp(-gate_val)) * up_val).astype(jnp.bfloat16)
    term = jnp.dot(hidden, down_ref[...], preferred_element_type=jnp.float32)
    half = own_ref.shape[0]

    @pl.when(step == 0)
    def _():
        acc_ref[...] = term

    @pl.when((step > 0) & (step < last))
    def _():
        acc_ref[...] += term

    @pl.when(step == last)
    def _():
        total = acc_ref[...] + term
        own_ref[...] = total[:half]
        other_ref[...] = total[half:].astype(other_ref.dtype)


def expert(rows, gate_part, up_part, down_part, chunk=256):
    count, width = rows.shape
    hidden = gate_part.shape[1]
    half = count // 2
    return pl.pallas_call(
        expert_kernel,
        out_shape=(
            jax.ShapeDtypeStruct((half, width), jnp.float32),
            jax.ShapeDtypeStruct((half, width), jnp.bfloat16),
        ),
        grid=(hidden // chunk,),
        in_specs=[
            pl.BlockSpec((count, width), lambda k: (0, 0)),
            pl.BlockSpec((width, chunk), lambda k: (0, k)),
            pl.BlockSpec((width, chunk), lambda k: (0, k)),
            pl.BlockSpec((chunk, width), lambda k: (k, 0)),
        ],
        out_specs=(
            pl.BlockSpec((half, width), lambda k: (0, 0)),
            pl.BlockSpec((half, width), lambda k: (0, 0)),
        ),
        scratch_shapes=[pltpu.VMEM((count, width), jnp.float32)],
        compiler_params=pltpu.CompilerParams(dimension_semantics=("arbitrary",)),
        cost_estimate=pl.CostEstimate(
            flops=6 * count * width * hidden,
            transcendentals=count * hidden,
            bytes_accessed=2 * (count * width + 3 * width * hidden) + 3 * half * width * 2,
        ),
    )(rows, gate_part, up_part, down_part)


def pair_barrier():
    me = lax.axis_index("shard")
    partner = (lax.axis_index("segment"), me + 1 - 2 * lax.rem(me, 2))
    barrier = pltpu.get_barrier_semaphore()
    pl.semaphore_signal(barrier, 1, device_id=partner, device_id_type=pl.DeviceIdType.MESH)
    pl.semaphore_wait(barrier, 1)
    return partner


def pair_gather_kernel(x_ref, o_ref, send_sem, recv_sem, local_sem):
    partner = pair_barrier()
    copy = pltpu.make_async_remote_copy(
        src_ref=x_ref,
        dst_ref=o_ref.at[1],
        send_sem=send_sem,
        recv_sem=recv_sem,
        device_id=partner,
        device_id_type=pl.DeviceIdType.MESH,
    )
    copy.start()
    local = pltpu.make_async_copy(x_ref, o_ref.at[0], local_sem)
    local.start()
    local.wait()
    copy.wait()


def pair_gather(value, collective):
    return pl.pallas_call(
        pair_gather_kernel,
        out_shape=jax.ShapeDtypeStruct((2,) + value.shape, value.dtype),
        in_specs=[pl.BlockSpec(memory_space=pltpu.VMEM)],
        out_specs=pl.BlockSpec(memory_space=pltpu.VMEM),
        scratch_shapes=[pltpu.SemaphoreType.DMA(()), pltpu.SemaphoreType.DMA(()), pltpu.SemaphoreType.DMA(())],
        compiler_params=pltpu.CompilerParams(collective_id=collective, has_side_effects=True),
    )(value)


def pair_send_kernel(x_ref, o_ref, send_sem, recv_sem):
    partner = pair_barrier()
    copy = pltpu.make_async_remote_copy(
        src_ref=x_ref,
        dst_ref=o_ref,
        send_sem=send_sem,
        recv_sem=recv_sem,
        device_id=partner,
        device_id_type=pl.DeviceIdType.MESH,
    )
    copy.start()
    copy.wait()


def pair_send(value, collective):
    return pl.pallas_call(
        pair_send_kernel,
        out_shape=jax.ShapeDtypeStruct(value.shape, value.dtype),
        in_specs=[pl.BlockSpec(memory_space=pltpu.VMEM)],
        out_specs=pl.BlockSpec(memory_space=pltpu.VMEM),
        scratch_shapes=[pltpu.SemaphoreType.DMA(()), pltpu.SemaphoreType.DMA(())],
        compiler_params=pltpu.CompilerParams(collective_id=collective, has_side_effects=True),
    )(value)


def shards(tokens, norm_gain, w_gate, w_up, w_down, block_counts, gate_prob):
    segment_index = lax.axis_index("segment")
    segment_count = lax.axis_size("segment")
    shard_count = lax.axis_size("shard")
    hidden_count = w_gate.shape[2]
    per_expert = FF // hidden_count
    zero_blocks = block_counts[0]
    row_gain = norm_gain[0]
    gate_part = w_gate[0]
    up_part = w_up[0]
    down_part = w_down[0]
    probs = gate_prob[0]
    local_rows = tokens.shape[1]
    width = tokens.shape[2]
    piece_rows = 2 * local_rows * width // LANES
    chips = shard_count // 2
    ring_z = 8
    ring_y = chips // ring_z
    carried = tokens
    stored = jnp.zeros_like(tokens)
    for tick in range(segment_count):
        normed = normalize(carried, row_gain)
        pieces = jnp.stack([normed[0:2], normed[1:3]]).reshape(2, piece_rows, LANES)
        block_rows = ring_gather(pieces, ring_y, ring_z, 0).reshape(shard_count * 2 * local_rows, width)
        own_rows, other_rows = expert(block_rows, gate_part, up_part, down_part)
        chip_sum = (own_rows + pair_send(other_rows, 2).astype(jnp.float32)).astype(jnp.bfloat16)
        received = chip_exchange(chip_sum.reshape(chips, piece_rows, LANES), ring_y, ring_z, 0, 3)
        received = received.astype(jnp.float32)
        received = received.reshape(2, chips // 2, 2, local_rows, width)
        first, second = jnp.sum(received[0], axis=0), jnp.sum(received[1], axis=0)
        middle = jnp.where(zero_blocks >= 2, first[1], second[0])
        mixed = jnp.stack([first[0], middle, second[1]])
        updated = (carried.astype(jnp.float32) + probs[:, :, None] * mixed).astype(jnp.bfloat16)
        stored = jnp.where(segment_index == tick, updated, stored)
        if tick + 1 < segment_count:
            carried = shifted(updated, "segment", 1)
    return stored[None]


def solution(mesh):
    placed = (
        P(None, "shard", None),
        P("segment", None),
        P("segment", None, "shard"),
        P("segment", None, "shard"),
        P("segment", "shard", None),
        P("segment"),
        P("segment", None, "shard"),
    )
    return jax.shard_map(
        shards,
        mesh=mesh,
        in_specs=placed,
        out_specs=P("segment", None, "shard", None),
        check_vma=False,
    )
```

```python
import functools

import jax
import jax.numpy as jnp
from jax import lax
from jax.experimental import pallas as pl
from jax.experimental.pallas import tpu as pltpu
from jax.sharding import PartitionSpec as P

FF = 16384
LANES = 128


def shifted(value, axis, steps):
    count = lax.axis_size(axis)
    initial, last = (max(0, -steps), min(count, count - steps))
    return lax.ppermute(value, axis, [(source, source + steps) for source in range(initial, last)])


def normalize(rows, row_gain):
    values = rows.astype(jnp.float32)
    scale = lax.rsqrt(jnp.mean(values * values, axis=-1, keepdims=True) + 1e-05)
    return (values * scale * row_gain).astype(jnp.bfloat16)


def signed(index):
    return (index + 1) // 2 * (2 * lax.rem(index, 2) - 1)


def chip_exchange_kernel(ring_y, ring_z, per_expert, x_ref, o_ref, send_sem, recv_sem):
    me = lax.axis_index("shard")
    segment = lax.axis_index("segment")
    core = lax.rem(me, 2)
    chip = me // 2
    y, z = chip // ring_z, lax.rem(chip, ring_z)
    chips = ring_y * ring_z

    def peer(step, sign):
        z_index = lax.rem(step, ring_z)
        y_index = lax.rem(step // ring_z + z_index, ring_y)
        peer_y = lax.rem(y + sign * signed(y_index) + ring_y, ring_y)
        peer_z = lax.rem(z + sign * signed(z_index) + ring_z, ring_z)
        return peer_y * ring_z + peer_z

    def source(dest_chip):
        if per_expert:
            return x_ref.at[dest_chip // per_expert]
        return x_ref.at[lax.rem(dest_chip, ring_z) * ring_y + dest_chip // ring_z]

    def copy_of(dest_chip, slot):
        return pltpu.make_async_remote_copy(
            src_ref=source(dest_chip),
            dst_ref=o_ref.at[slot],
            send_sem=send_sem.at[dest_chip],
            recv_sem=recv_sem.at[slot],
            device_id=(segment, dest_chip * 2 + core),
            device_id_type=pl.DeviceIdType.MESH,
        )

    barrier = pltpu.get_barrier_semaphore()

    def greet(step, carry):
        dest = peer(step, 1) * 2 + core
        pl.semaphore_signal(barrier, 1, device_id=(segment, dest), device_id_type=pl.DeviceIdType.MESH)
        return carry

    lax.fori_loop(1, chips, greet, 0)
    pl.semaphore_wait(barrier, chips - 1)

    def start(step, carry):
        copy_of(peer(chips - step, 1), chip).start()
        return carry

    lax.fori_loop(1, chips, start, 0)
    o_ref[chip] = source(chip)[...]

    def finish(step, carry):
        copy_of(peer(step, 1), chip).wait_send()
        origin = peer(step, -1)
        copy_of(origin, origin).wait_recv()
        return carry

    lax.fori_loop(1, chips, finish, 0)


def chip_exchange(pieces, ring_y, ring_z, per_expert, collective):
    rows, lanes = pieces.shape[1], pieces.shape[2]
    chips = ring_y * ring_z
    return pl.pallas_call(
        functools.partial(chip_exchange_kernel, ring_y, ring_z, per_expert),
        out_shape=jax.ShapeDtypeStruct((chips, rows, lanes), pieces.dtype),
        in_specs=[pl.BlockSpec(memory_space=pltpu.VMEM)],
        out_specs=pl.BlockSpec(memory_space=pltpu.VMEM),
        scratch_shapes=[pltpu.SemaphoreType.DMA((chips,)), pltpu.SemaphoreType.DMA((chips,))],
        compiler_params=pltpu.CompilerParams(collective_id=collective, has_side_effects=True),
    )(pieces)


def ring_gather_kernel(ring_y, ring_z, x_ref, o_ref, send_y, recv_y, send_up, send_down, recv_z, send_c, recv_c):
    me = lax.axis_index("shard")
    segment = lax.axis_index("segment")
    core = lax.rem(me, 2)
    chip = me // 2
    y, z = chip // ring_z, lax.rem(chip, ring_z)
    half_z = ring_z // 2

    def device(peer_y, peer_z):
        return (segment, (peer_y * ring_z + peer_z) * 2 + core)

    up_z, down_z = lax.rem(z + 1, ring_z), lax.rem(z + ring_z - 1, ring_z)
    partner = (segment, me + 1 - 2 * core)
    barrier = pltpu.get_barrier_semaphore()
    for step in range(1, ring_y):
        pl.semaphore_signal(barrier, 1, device_id=device(lax.rem(y + step, ring_y), z), device_id_type=pl.DeviceIdType.MESH)
    pl.semaphore_signal(barrier, 1, device_id=device(y, up_z), device_id_type=pl.DeviceIdType.MESH)
    pl.semaphore_signal(barrier, 1, device_id=device(y, down_z), device_id_type=pl.DeviceIdType.MESH)
    pl.semaphore_signal(barrier, 1, device_id=partner, device_id_type=pl.DeviceIdType.MESH)
    pl.semaphore_wait(barrier, ring_y + 2)

    def y_copy(peer_y, slot):
        return pltpu.make_async_remote_copy(
            src_ref=x_ref.at[peer_y * 2 // ring_y],
            dst_ref=o_ref.at[0, z, slot],
            send_sem=send_y.at[peer_y],
            recv_sem=recv_y.at[slot],
            device_id=device(peer_y, z),
            device_id_type=pl.DeviceIdType.MESH,
        )

    for step in range(1, ring_y):
        y_copy(lax.rem(y + step, ring_y), y).start()
    o_ref[0, z, y] = x_ref[y * 2 // ring_y]
    for step in range(1, ring_y):
        origin = lax.rem(y + ring_y - step, ring_y)
        y_copy(origin, origin).wait_recv()
        y_copy(lax.rem(y + step, ring_y), y).wait_send()

    def pair_copy(slot):
        return pltpu.make_async_remote_copy(
            src_ref=o_ref.at[0, slot],
            dst_ref=o_ref.at[1, slot],
            send_sem=send_c.at[slot],
            recv_sem=recv_c.at[slot],
            device_id=partner,
            device_id_type=pl.DeviceIdType.MESH,
        )

    pair_copy(z).start()

    def z_copy(slot, peer_z, sems, index):
        return pltpu.make_async_remote_copy(
            src_ref=o_ref.at[0, slot],
            dst_ref=o_ref.at[0, slot],
            send_sem=sems.at[index],
            recv_sem=recv_z.at[slot],
            device_id=device(y, peer_z),
            device_id_type=pl.DeviceIdType.MESH,
        )

    for step in range(half_z):
        up_slot = lax.rem(z + ring_z - step, ring_z)
        if step > 0:
            z_copy(up_slot, down_z, send_up, step).wait_recv()
            pair_copy(up_slot).start()
        z_copy(up_slot, up_z, send_up, step).start()
        if step < half_z - 1:
            down_slot = lax.rem(z + step, ring_z)
            if step > 0:
                z_copy(down_slot, up_z, send_down, step).wait_recv()
                pair_copy(down_slot).start()
            z_copy(down_slot, down_z, send_down, step).start()
    last_up = lax.rem(z + ring_z - half_z, ring_z)
    z_copy(last_up, down_z, send_up, 0).wait_recv()
    pair_copy(last_up).start()
    last_down = lax.rem(z + half_z - 1, ring_z)
    z_copy(last_down, up_z, send_down, 0).wait_recv()
    pair_copy(last_down).start()
    for step in range(half_z):
        z_copy(lax.rem(z + ring_z - step, ring_z), up_z, send_up, step).wait_send()
        if step < half_z - 1:
            z_copy(lax.rem(z + step, ring_z), down_z, send_down, step).wait_send()

    for slot in range(ring_z):
        pair_copy(slot).wait_send()
        pair_copy(slot).wait_recv()


def ring_gather(pieces, ring_y, ring_z, collective):
    rows, lanes = pieces.shape[1], pieces.shape[2]
    return pl.pallas_call(
        functools.partial(ring_gather_kernel, ring_y, ring_z),
        out_shape=jax.ShapeDtypeStruct((2, ring_z, ring_y, rows, lanes), pieces.dtype),
        in_specs=[pl.BlockSpec(memory_space=pltpu.VMEM)],
        out_specs=pl.BlockSpec(memory_space=pltpu.VMEM),
        scratch_shapes=[
            pltpu.SemaphoreType.DMA((ring_y,)),
            pltpu.SemaphoreType.DMA((ring_y,)),
            pltpu.SemaphoreType.DMA((ring_z // 2,)),
            pltpu.SemaphoreType.DMA((ring_z // 2,)),
            pltpu.SemaphoreType.DMA((ring_z,)),
            pltpu.SemaphoreType.DMA((ring_z,)),
            pltpu.SemaphoreType.DMA((ring_z,)),
        ],
        compiler_params=pltpu.CompilerParams(collective_id=collective, has_side_effects=True),
    )(pieces)


def expert_kernel(x_ref, gate_ref, up_ref, down_ref, own_ref, other_ref, acc_ref):
    step, last = pl.program_id(0), pl.num_programs(0) - 1
    rows = x_ref[...]
    gate_val = jnp.dot(rows, gate_ref[...], preferred_element_type=jnp.float32)
    up_val = jnp.dot(rows, up_ref[...], preferred_element_type=jnp.float32)
    hidden = (gate_val / (1.0 + jnp.exp(-gate_val)) * up_val).astype(jnp.bfloat16)
    term = jnp.dot(hidden, down_ref[...], preferred_element_type=jnp.float32)
    half = own_ref.shape[0]

    @pl.when(step == 0)
    def _():
        acc_ref[...] = term

    @pl.when((step > 0) & (step < last))
    def _():
        acc_ref[...] += term

    @pl.when(step == last)
    def _():
        total = acc_ref[...] + term
        own_ref[...] = total[:half]
        other_ref[...] = total[half:].astype(other_ref.dtype)


def expert(rows, gate_part, up_part, down_part, chunk=256):
    count, width = rows.shape
    hidden = gate_part.shape[1]
    half = count // 2
    return pl.pallas_call(
        expert_kernel,
        out_shape=(
            jax.ShapeDtypeStruct((half, width), jnp.float32),
            jax.ShapeDtypeStruct((half, width), jnp.bfloat16),
        ),
        grid=(hidden // chunk,),
        in_specs=[
            pl.BlockSpec((count, width), lambda k: (0, 0)),
            pl.BlockSpec((width, chunk), lambda k: (0, k)),
            pl.BlockSpec((width, chunk), lambda k: (0, k)),
            pl.BlockSpec((chunk, width), lambda k: (k, 0)),
        ],
        out_specs=(
            pl.BlockSpec((half, width), lambda k: (0, 0)),
            pl.BlockSpec((half, width), lambda k: (0, 0)),
        ),
        scratch_shapes=[pltpu.VMEM((count, width), jnp.float32)],
        compiler_params=pltpu.CompilerParams(dimension_semantics=("arbitrary",)),
        cost_estimate=pl.CostEstimate(
            flops=6 * count * width * hidden,
            transcendentals=count * hidden,
            bytes_accessed=2 * (count * width + 3 * width * hidden) + 3 * half * width * 2,
        ),
    )(rows, gate_part, up_part, down_part)


def pair_barrier():
    me = lax.axis_index("shard")
    partner = (lax.axis_index("segment"), me + 1 - 2 * lax.rem(me, 2))
    barrier = pltpu.get_barrier_semaphore()
    pl.semaphore_signal(barrier, 1, device_id=partner, device_id_type=pl.DeviceIdType.MESH)
    pl.semaphore_wait(barrier, 1)
    return partner


def pair_gather_kernel(x_ref, o_ref, send_sem, recv_sem, local_sem):
    partner = pair_barrier()
    copy = pltpu.make_async_remote_copy(
        src_ref=x_ref,
        dst_ref=o_ref.at[1],
        send_sem=send_sem,
        recv_sem=recv_sem,
        device_id=partner,
        device_id_type=pl.DeviceIdType.MESH,
    )
    copy.start()
    local = pltpu.make_async_copy(x_ref, o_ref.at[0], local_sem)
    local.start()
    local.wait()
    copy.wait()


def pair_gather(value, collective):
    return pl.pallas_call(
        pair_gather_kernel,
        out_shape=jax.ShapeDtypeStruct((2,) + value.shape, value.dtype),
        in_specs=[pl.BlockSpec(memory_space=pltpu.VMEM)],
        out_specs=pl.BlockSpec(memory_space=pltpu.VMEM),
        scratch_shapes=[pltpu.SemaphoreType.DMA(()), pltpu.SemaphoreType.DMA(()), pltpu.SemaphoreType.DMA(())],
        compiler_params=pltpu.CompilerParams(collective_id=collective, has_side_effects=True),
    )(value)


def pair_send_kernel(x_ref, o_ref, send_sem, recv_sem):
    partner = pair_barrier()
    copy = pltpu.make_async_remote_copy(
        src_ref=x_ref,
        dst_ref=o_ref,
        send_sem=send_sem,
        recv_sem=recv_sem,
        device_id=partner,
        device_id_type=pl.DeviceIdType.MESH,
    )
    copy.start()
    copy.wait()


def pair_send(value, collective):
    return pl.pallas_call(
        pair_send_kernel,
        out_shape=jax.ShapeDtypeStruct(value.shape, value.dtype),
        in_specs=[pl.BlockSpec(memory_space=pltpu.VMEM)],
        out_specs=pl.BlockSpec(memory_space=pltpu.VMEM),
        scratch_shapes=[pltpu.SemaphoreType.DMA(()), pltpu.SemaphoreType.DMA(())],
        compiler_params=pltpu.CompilerParams(collective_id=collective, has_side_effects=True),
    )(value)


def shards(tokens, norm_gain, w_gate, w_up, w_down, block_counts, gate_prob):
    segment_index = lax.axis_index("segment")
    segment_count = lax.axis_size("segment")
    shard_count = lax.axis_size("shard")
    hidden_count = w_gate.shape[2]
    per_expert = FF // hidden_count
    zero_blocks = block_counts[0]
    row_gain = norm_gain[0]
    gate_part = w_gate[0]
    up_part = w_up[0]
    down_part = w_down[0]
    probs = gate_prob[0]
    local_rows = tokens.shape[1]
    width = tokens.shape[2]
    piece_rows = 2 * local_rows * width // LANES
    chips = shard_count // 2
    ring_z = 8
    ring_y = chips // ring_z
    carried = tokens
    stored = jnp.zeros_like(tokens)
    for tick in range(segment_count):
        normed = normalize(carried, row_gain)
        pieces = jnp.stack([normed[0:2], normed[1:3]]).reshape(2, piece_rows, LANES)
        block_rows = ring_gather(pieces, ring_y, ring_z, 0).reshape(shard_count * 2 * local_rows, width)
        own_rows, other_rows = expert(block_rows, gate_part, up_part, down_part)
        chip_sum = (own_rows + pair_send(other_rows, 2).astype(jnp.float32)).astype(jnp.bfloat16)
        received = chip_exchange(chip_sum.reshape(chips, piece_rows, LANES), ring_y, ring_z, 0, 3)
        received = received.astype(jnp.float32)
        received = received.reshape(2, chips // 2, 2, local_rows, width)
        first, second = jnp.sum(received[0], axis=0), jnp.sum(received[1], axis=0)
        middle = jnp.where(zero_blocks >= 2, first[1], second[0])
        mixed = jnp.stack([first[0], middle, second[1]])
        updated = (carried.astype(jnp.float32) + probs[:, :, None] * mixed).astype(jnp.bfloat16)
        stored = jnp.where(segment_index == tick, updated, stored)
        if tick + 1 < segment_count:
            carried = shifted(updated, "segment", 1)
    return stored[None]


def solution(mesh):
    placed = (
        P(None, "shard", None),
        P("segment", None),
        P("segment", None, "shard"),
        P("segment", None, "shard"),
        P("segment", "shard", None),
        P("segment"),
        P("segment", None, "shard"),
    )
    return jax.shard_map(
        shards,
        mesh=mesh,
        in_specs=placed,
        out_specs=P("segment", None, "shard", None),
        check_vma=False,
    )
```

```python
import functools

import jax
import jax.numpy as jnp
from jax import lax
from jax.experimental import pallas as pl
from jax.experimental.pallas import tpu as pltpu
from jax.sharding import PartitionSpec as P

FF = 16384
LANES = 128


def shifted(value, axis, steps):
    count = lax.axis_size(axis)
    initial, last = (max(0, -steps), min(count, count - steps))
    return lax.ppermute(value, axis, [(source, source + steps) for source in range(initial, last)])


def normalize(rows, row_gain):
    values = rows.astype(jnp.float32)
    scale = lax.rsqrt(jnp.mean(values * values, axis=-1, keepdims=True) + 1e-05)
    return (values * scale * row_gain).astype(jnp.bfloat16)


def signed(index):
    return (index + 1) // 2 * (2 * lax.rem(index, 2) - 1)


def chip_exchange_kernel(ring_y, ring_z, per_expert, x_ref, o_ref, send_sem, recv_sem):
    me = lax.axis_index("shard")
    segment = lax.axis_index("segment")
    core = lax.rem(me, 2)
    chip = me // 2
    y, z = chip // ring_z, lax.rem(chip, ring_z)
    chips = ring_y * ring_z

    def peer(step, sign):
        z_index = lax.rem(step, ring_z)
        y_index = lax.rem(step // ring_z + z_index, ring_y)
        peer_y = lax.rem(y + sign * signed(y_index) + ring_y, ring_y)
        peer_z = lax.rem(z + sign * signed(z_index) + ring_z, ring_z)
        return peer_y * ring_z + peer_z

    def source(dest_chip):
        if per_expert:
            return x_ref.at[dest_chip // per_expert]
        return x_ref.at[lax.rem(dest_chip, ring_z) * ring_y + dest_chip // ring_z]

    def copy_of(dest_chip, slot):
        return pltpu.make_async_remote_copy(
            src_ref=source(dest_chip),
            dst_ref=o_ref.at[slot],
            send_sem=send_sem.at[dest_chip],
            recv_sem=recv_sem.at[slot],
            device_id=(segment, dest_chip * 2 + core),
            device_id_type=pl.DeviceIdType.MESH,
        )

    barrier = pltpu.get_barrier_semaphore()

    def greet(step, carry):
        dest = peer(step, 1) * 2 + core
        pl.semaphore_signal(barrier, 1, device_id=(segment, dest), device_id_type=pl.DeviceIdType.MESH)
        return carry

    lax.fori_loop(1, chips, greet, 0)
    pl.semaphore_wait(barrier, chips - 1)

    def start(step, carry):
        copy_of(peer(step, 1), chip).start()
        return carry

    lax.fori_loop(1, chips, start, 0)
    o_ref[chip] = source(chip)[...]

    def finish(step, carry):
        copy_of(peer(step, 1), chip).wait_send()
        origin = peer(step, -1)
        copy_of(origin, origin).wait_recv()
        return carry

    lax.fori_loop(1, chips, finish, 0)


def chip_exchange(pieces, ring_y, ring_z, per_expert, collective):
    rows, lanes = pieces.shape[1], pieces.shape[2]
    chips = ring_y * ring_z
    return pl.pallas_call(
        functools.partial(chip_exchange_kernel, ring_y, ring_z, per_expert),
        out_shape=jax.ShapeDtypeStruct((chips, rows, lanes), pieces.dtype),
        in_specs=[pl.BlockSpec(memory_space=pltpu.VMEM)],
        out_specs=pl.BlockSpec(memory_space=pltpu.VMEM),
        scratch_shapes=[pltpu.SemaphoreType.DMA((chips,)), pltpu.SemaphoreType.DMA((chips,))],
        compiler_params=pltpu.CompilerParams(collective_id=collective, has_side_effects=True),
    )(pieces)


def ring_gather_kernel(ring_y, ring_z, x_ref, o_ref, send_y, recv_y, send_up, send_down, recv_z, send_c, recv_c):
    me = lax.axis_index("shard")
    segment = lax.axis_index("segment")
    core = lax.rem(me, 2)
    chip = me // 2
    y, z = chip // ring_z, lax.rem(chip, ring_z)
    half_z = ring_z // 2

    def device(peer_y, peer_z):
        return (segment, (peer_y * ring_z + peer_z) * 2 + core)

    up_z, down_z = lax.rem(z + 1, ring_z), lax.rem(z + ring_z - 1, ring_z)
    partner = (segment, me + 1 - 2 * core)
    barrier = pltpu.get_barrier_semaphore()
    for step in range(1, ring_y):
        pl.semaphore_signal(barrier, 1, device_id=device(lax.rem(y + step, ring_y), z), device_id_type=pl.DeviceIdType.MESH)
    pl.semaphore_signal(barrier, 1, device_id=device(y, up_z), device_id_type=pl.DeviceIdType.MESH)
    pl.semaphore_signal(barrier, 1, device_id=device(y, down_z), device_id_type=pl.DeviceIdType.MESH)
    pl.semaphore_signal(barrier, 1, device_id=partner, device_id_type=pl.DeviceIdType.MESH)
    pl.semaphore_wait(barrier, ring_y + 2)

    def y_copy(peer_y, slot):
        return pltpu.make_async_remote_copy(
            src_ref=x_ref.at[peer_y * 2 // ring_y],
            dst_ref=o_ref.at[0, z, slot],
            send_sem=send_y.at[peer_y],
            recv_sem=recv_y.at[slot],
            device_id=device(peer_y, z),
            device_id_type=pl.DeviceIdType.MESH,
        )

    for step in range(1, ring_y):
        y_copy(lax.rem(y + step, ring_y), y).start()
    o_ref[0, z, y] = x_ref[y * 2 // ring_y]
    for step in range(1, ring_y):
        origin = lax.rem(y + ring_y - step, ring_y)
        y_copy(origin, origin).wait_recv()
        y_copy(lax.rem(y + step, ring_y), y).wait_send()

    def pair_copy(slot):
        return pltpu.make_async_remote_copy(
            src_ref=o_ref.at[0, slot],
            dst_ref=o_ref.at[1, slot],
            send_sem=send_c.at[slot],
            recv_sem=recv_c.at[slot],
            device_id=partner,
            device_id_type=pl.DeviceIdType.MESH,
        )

    pair_copy(z).start()

    def z_copy(slot, peer_z, sems, index):
        return pltpu.make_async_remote_copy(
            src_ref=o_ref.at[0, slot],
            dst_ref=o_ref.at[0, slot],
            send_sem=sems.at[index],
            recv_sem=recv_z.at[slot],
            device_id=device(y, peer_z),
            device_id_type=pl.DeviceIdType.MESH,
        )

    for step in range(half_z):
        up_slot = lax.rem(z + ring_z - step, ring_z)
        if step > 0:
            z_copy(up_slot, down_z, send_up, step).wait_recv()
            pair_copy(up_slot).start()
        z_copy(up_slot, up_z, send_up, step).start()
        if step < half_z - 1:
            down_slot = lax.rem(z + step, ring_z)
            if step > 0:
                z_copy(down_slot, up_z, send_down, step).wait_recv()
                pair_copy(down_slot).start()
            z_copy(down_slot, down_z, send_down, step).start()
    last_up = lax.rem(z + ring_z - half_z, ring_z)
    z_copy(last_up, down_z, send_up, 0).wait_recv()
    pair_copy(last_up).start()
    last_down = lax.rem(z + half_z - 1, ring_z)
    z_copy(last_down, up_z, send_down, 0).wait_recv()
    pair_copy(last_down).start()
    for step in range(half_z):
        z_copy(lax.rem(z + ring_z - step, ring_z), up_z, send_up, step).wait_send()
        if step < half_z - 1:
            z_copy(lax.rem(z + step, ring_z), down_z, send_down, step).wait_send()

    for slot in range(ring_z):
        pair_copy(slot).wait_send()
        pair_copy(slot).wait_recv()


def ring_gather(pieces, ring_y, ring_z, collective):
    rows, lanes = pieces.shape[1], pieces.shape[2]
    return pl.pallas_call(
        functools.partial(ring_gather_kernel, ring_y, ring_z),
        out_shape=jax.ShapeDtypeStruct((2, ring_z, ring_y, rows, lanes), pieces.dtype),
        in_specs=[pl.BlockSpec(memory_space=pltpu.VMEM)],
        out_specs=pl.BlockSpec(memory_space=pltpu.VMEM),
        scratch_shapes=[
            pltpu.SemaphoreType.DMA((ring_y,)),
            pltpu.SemaphoreType.DMA((ring_y,)),
            pltpu.SemaphoreType.DMA((ring_z // 2,)),
            pltpu.SemaphoreType.DMA((ring_z // 2,)),
            pltpu.SemaphoreType.DMA((ring_z,)),
            pltpu.SemaphoreType.DMA((ring_z,)),
            pltpu.SemaphoreType.DMA((ring_z,)),
        ],
        compiler_params=pltpu.CompilerParams(collective_id=collective, has_side_effects=True),
    )(pieces)


def expert_kernel(x_ref, gate_ref, up_ref, down_ref, own_ref, other_ref, acc_ref, rows_ref):
    step, last = pl.program_id(0), pl.num_programs(0) - 1

    @pl.when(step == 0)
    def _():
        rows_ref[...] = x_ref[...].reshape(rows_ref.shape)

    rows = rows_ref[...]
    gate_val = jnp.dot(rows, gate_ref[...], preferred_element_type=jnp.float32)
    up_val = jnp.dot(rows, up_ref[...], preferred_element_type=jnp.float32)
    hidden = (gate_val / (1.0 + jnp.exp(-gate_val)) * up_val).astype(jnp.bfloat16)
    term = jnp.dot(hidden, down_ref[...], preferred_element_type=jnp.float32)
    half = own_ref.shape[0]

    @pl.when(step == 0)
    def _():
        acc_ref[...] = term

    @pl.when((step > 0) & (step < last))
    def _():
        acc_ref[...] += term

    @pl.when(step == last)
    def _():
        total = acc_ref[...] + term
        own_ref[...] = total[:half]
        other_ref[...] = total[half:].astype(other_ref.dtype)


def expert(rows, gate_part, up_part, down_part, chunk=256):
    width = gate_part.shape[0]
    count = rows.size // width
    hidden = gate_part.shape[1]
    half = count // 2
    return pl.pallas_call(
        expert_kernel,
        out_shape=(
            jax.ShapeDtypeStruct((half, width), jnp.float32),
            jax.ShapeDtypeStruct((half, width), jnp.bfloat16),
        ),
        grid=(hidden // chunk,),
        in_specs=[
            pl.BlockSpec(rows.shape, lambda k: (0, 0, 0)),
            pl.BlockSpec((width, chunk), lambda k: (0, k)),
            pl.BlockSpec((width, chunk), lambda k: (0, k)),
            pl.BlockSpec((chunk, width), lambda k: (k, 0)),
        ],
        out_specs=(
            pl.BlockSpec((half, width), lambda k: (0, 0)),
            pl.BlockSpec((half, width), lambda k: (0, 0)),
        ),
        scratch_shapes=[pltpu.VMEM((count, width), jnp.float32), pltpu.VMEM((count, width), rows.dtype)],
        compiler_params=pltpu.CompilerParams(dimension_semantics=("arbitrary",)),
        cost_estimate=pl.CostEstimate(
            flops=6 * count * width * hidden,
            transcendentals=count * hidden,
            bytes_accessed=2 * (count * width + 3 * width * hidden) + 3 * half * width * 2,
        ),
    )(rows, gate_part, up_part, down_part)


def pair_barrier():
    me = lax.axis_index("shard")
    partner = (lax.axis_index("segment"), me + 1 - 2 * lax.rem(me, 2))
    barrier = pltpu.get_barrier_semaphore()
    pl.semaphore_signal(barrier, 1, device_id=partner, device_id_type=pl.DeviceIdType.MESH)
    pl.semaphore_wait(barrier, 1)
    return partner


def pair_gather_kernel(x_ref, o_ref, send_sem, recv_sem, local_sem):
    partner = pair_barrier()
    copy = pltpu.make_async_remote_copy(
        src_ref=x_ref,
        dst_ref=o_ref.at[1],
        send_sem=send_sem,
        recv_sem=recv_sem,
        device_id=partner,
        device_id_type=pl.DeviceIdType.MESH,
    )
    copy.start()
    local = pltpu.make_async_copy(x_ref, o_ref.at[0], local_sem)
    local.start()
    local.wait()
    copy.wait()


def pair_gather(value, collective):
    return pl.pallas_call(
        pair_gather_kernel,
        out_shape=jax.ShapeDtypeStruct((2,) + value.shape, value.dtype),
        in_specs=[pl.BlockSpec(memory_space=pltpu.VMEM)],
        out_specs=pl.BlockSpec(memory_space=pltpu.VMEM),
        scratch_shapes=[pltpu.SemaphoreType.DMA(()), pltpu.SemaphoreType.DMA(()), pltpu.SemaphoreType.DMA(())],
        compiler_params=pltpu.CompilerParams(collective_id=collective, has_side_effects=True),
    )(value)


def pair_send_kernel(x_ref, o_ref, send_sem, recv_sem):
    partner = pair_barrier()
    copy = pltpu.make_async_remote_copy(
        src_ref=x_ref,
        dst_ref=o_ref,
        send_sem=send_sem,
        recv_sem=recv_sem,
        device_id=partner,
        device_id_type=pl.DeviceIdType.MESH,
    )
    copy.start()
    copy.wait()


def pair_send(value, collective):
    return pl.pallas_call(
        pair_send_kernel,
        out_shape=jax.ShapeDtypeStruct(value.shape, value.dtype),
        in_specs=[pl.BlockSpec(memory_space=pltpu.VMEM)],
        out_specs=pl.BlockSpec(memory_space=pltpu.VMEM),
        scratch_shapes=[pltpu.SemaphoreType.DMA(()), pltpu.SemaphoreType.DMA(())],
        compiler_params=pltpu.CompilerParams(collective_id=collective, has_side_effects=True),
    )(value)


def shards(tokens, norm_gain, w_gate, w_up, w_down, block_counts, gate_prob):
    segment_index = lax.axis_index("segment")
    segment_count = lax.axis_size("segment")
    shard_count = lax.axis_size("shard")
    hidden_count = w_gate.shape[2]
    per_expert = FF // hidden_count
    zero_blocks = block_counts[0]
    row_gain = norm_gain[0]
    gate_part = w_gate[0]
    up_part = w_up[0]
    down_part = w_down[0]
    probs = gate_prob[0]
    local_rows = tokens.shape[1]
    width = tokens.shape[2]
    piece_rows = 2 * local_rows * width // LANES
    chips = shard_count // 2
    ring_z = 8
    ring_y = chips // ring_z
    carried = tokens
    stored = jnp.zeros_like(tokens)
    for tick in range(segment_count):
        normed = normalize(carried, row_gain)
        pieces = jnp.stack([normed[0:2], normed[1:3]]).reshape(2, piece_rows, LANES)
        block_rows = ring_gather(pieces, ring_y, ring_z, 0).reshape(shard_count, piece_rows, LANES)
        own_rows, other_rows = expert(block_rows, gate_part, up_part, down_part)
        chip_sum = (own_rows + pair_send(other_rows, 2).astype(jnp.float32)).astype(jnp.bfloat16)
        received = chip_exchange(chip_sum.reshape(chips, piece_rows, LANES), ring_y, ring_z, 0, 3)
        received = received.astype(jnp.float32)
        received = received.reshape(2, chips // 2, 2, local_rows, width)
        first, second = jnp.sum(received[0], axis=0), jnp.sum(received[1], axis=0)
        middle = jnp.where(zero_blocks >= 2, first[1], second[0])
        mixed = jnp.stack([first[0], middle, second[1]])
        updated = (carried.astype(jnp.float32) + probs[:, :, None] * mixed).astype(jnp.bfloat16)
        stored = jnp.where(segment_index == tick, updated, stored)
        if tick + 1 < segment_count:
            carried = shifted(updated, "segment", 1)
    return stored[None]


def solution(mesh):
    placed = (
        P(None, "shard", None),
        P("segment", None),
        P("segment", None, "shard"),
        P("segment", None, "shard"),
        P("segment", "shard", None),
        P("segment"),
        P("segment", None, "shard"),
    )
    return jax.shard_map(
        shards,
        mesh=mesh,
        in_specs=placed,
        out_specs=P("segment", None, "shard", None),
        check_vma=False,
    )
```

```python
import functools

import jax
import jax.numpy as jnp
from jax import lax
from jax.experimental import pallas as pl
from jax.experimental.pallas import tpu as pltpu
from jax.sharding import PartitionSpec as P

FF = 16384
LANES = 128


def shifted(value, axis, steps):
    count = lax.axis_size(axis)
    initial, last = (max(0, -steps), min(count, count - steps))
    return lax.ppermute(value, axis, [(source, source + steps) for source in range(initial, last)])


def normalize(rows, row_gain):
    values = rows.astype(jnp.float32)
    scale = lax.rsqrt(jnp.mean(values * values, axis=-1, keepdims=True) + 1e-05)
    return (values * scale * row_gain).astype(jnp.bfloat16)


def signed(index):
    return (index + 1) // 2 * (2 * lax.rem(index, 2) - 1)


def chip_exchange_kernel(ring_y, ring_z, per_expert, x_ref, o_ref, send_sem, recv_sem):
    me = lax.axis_index("shard")
    segment = lax.axis_index("segment")
    core = lax.rem(me, 2)
    chip = me // 2
    y, z = chip // ring_z, lax.rem(chip, ring_z)
    chips = ring_y * ring_z

    def peer(step, sign):
        z_index = lax.rem(step, ring_z)
        y_index = lax.rem(step // ring_z + z_index, ring_y)
        peer_y = lax.rem(y + sign * signed(y_index) + ring_y, ring_y)
        peer_z = lax.rem(z + sign * signed(z_index) + ring_z, ring_z)
        return peer_y * ring_z + peer_z

    def source(dest_chip):
        if per_expert:
            return x_ref.at[dest_chip // per_expert]
        return x_ref.at[lax.rem(dest_chip, ring_z) * ring_y + dest_chip // ring_z]

    def copy_of(dest_chip, slot):
        return pltpu.make_async_remote_copy(
            src_ref=source(dest_chip),
            dst_ref=o_ref.at[slot],
            send_sem=send_sem.at[dest_chip],
            recv_sem=recv_sem.at[slot],
            device_id=(segment, dest_chip * 2 + core),
            device_id_type=pl.DeviceIdType.MESH,
        )

    barrier = pltpu.get_barrier_semaphore()

    def greet(step, carry):
        dest = peer(step, 1) * 2 + core
        pl.semaphore_signal(barrier, 1, device_id=(segment, dest), device_id_type=pl.DeviceIdType.MESH)
        return carry

    lax.fori_loop(1, chips, greet, 0)
    pl.semaphore_wait(barrier, chips - 1)

    def start(step, carry):
        copy_of(peer(step, 1), chip).start()
        return carry

    lax.fori_loop(1, chips, start, 0)
    o_ref[chip] = source(chip)[...]

    def finish(step, carry):
        copy_of(peer(step, 1), chip).wait_send()
        origin = peer(step, -1)
        copy_of(origin, origin).wait_recv()
        return carry

    lax.fori_loop(1, chips, finish, 0)


def chip_exchange(pieces, ring_y, ring_z, per_expert, collective):
    rows, lanes = pieces.shape[1], pieces.shape[2]
    chips = ring_y * ring_z
    return pl.pallas_call(
        functools.partial(chip_exchange_kernel, ring_y, ring_z, per_expert),
        out_shape=jax.ShapeDtypeStruct((chips, rows, lanes), pieces.dtype),
        in_specs=[pl.BlockSpec(memory_space=pltpu.VMEM)],
        out_specs=pl.BlockSpec(memory_space=pltpu.VMEM),
        scratch_shapes=[pltpu.SemaphoreType.DMA((chips,)), pltpu.SemaphoreType.DMA((chips,))],
        compiler_params=pltpu.CompilerParams(collective_id=collective, has_side_effects=True),
    )(pieces)


def ring_gather_kernel(ring_y, ring_z, x_ref, o_ref, send_y, recv_y, send_up, send_down, recv_z, send_c, recv_c):
    me = lax.axis_index("shard")
    segment = lax.axis_index("segment")
    core = lax.rem(me, 2)
    chip = me // 2
    y, z = chip // ring_z, lax.rem(chip, ring_z)
    half_z = ring_z // 2

    def device(peer_y, peer_z):
        return (segment, (peer_y * ring_z + peer_z) * 2 + core)

    up_z, down_z = lax.rem(z + 1, ring_z), lax.rem(z + ring_z - 1, ring_z)
    partner = (segment, me + 1 - 2 * core)
    barrier = pltpu.get_barrier_semaphore()
    for step in range(1, ring_y):
        pl.semaphore_signal(barrier, 1, device_id=device(lax.rem(y + step, ring_y), z), device_id_type=pl.DeviceIdType.MESH)
    pl.semaphore_signal(barrier, 1, device_id=device(y, up_z), device_id_type=pl.DeviceIdType.MESH)
    pl.semaphore_signal(barrier, 1, device_id=device(y, down_z), device_id_type=pl.DeviceIdType.MESH)
    pl.semaphore_signal(barrier, 1, device_id=partner, device_id_type=pl.DeviceIdType.MESH)
    pl.semaphore_wait(barrier, ring_y + 2)

    def y_copy(peer_y, slot):
        return pltpu.make_async_remote_copy(
            src_ref=x_ref.at[peer_y * 2 // ring_y],
            dst_ref=o_ref.at[0, z, slot],
            send_sem=send_y.at[peer_y],
            recv_sem=recv_y.at[slot],
            device_id=device(peer_y, z),
            device_id_type=pl.DeviceIdType.MESH,
        )

    for step in range(1, ring_y):
        y_copy(lax.rem(y + step, ring_y), y).start()
    o_ref[0, z, y] = x_ref[y * 2 // ring_y]
    for step in range(1, ring_y):
        origin = lax.rem(y + ring_y - step, ring_y)
        y_copy(origin, origin).wait_recv()
        y_copy(lax.rem(y + step, ring_y), y).wait_send()

    def pair_copy(slot):
        return pltpu.make_async_remote_copy(
            src_ref=o_ref.at[0, slot],
            dst_ref=o_ref.at[1, slot],
            send_sem=send_c.at[slot],
            recv_sem=recv_c.at[slot],
            device_id=partner,
            device_id_type=pl.DeviceIdType.MESH,
        )

    pair_copy(z).start()

    def z_copy(slot, peer_z, sems, index):
        return pltpu.make_async_remote_copy(
            src_ref=o_ref.at[0, slot],
            dst_ref=o_ref.at[0, slot],
            send_sem=sems.at[index],
            recv_sem=recv_z.at[slot],
            device_id=device(y, peer_z),
            device_id_type=pl.DeviceIdType.MESH,
        )

    for step in range(half_z):
        up_slot = lax.rem(z + ring_z - step, ring_z)
        if step > 0:
            z_copy(up_slot, down_z, send_up, step).wait_recv()
            pair_copy(up_slot).start()
        z_copy(up_slot, up_z, send_up, step).start()
        if step < half_z - 1:
            down_slot = lax.rem(z + step, ring_z)
            if step > 0:
                z_copy(down_slot, up_z, send_down, step).wait_recv()
                pair_copy(down_slot).start()
            z_copy(down_slot, down_z, send_down, step).start()
    last_up = lax.rem(z + ring_z - half_z, ring_z)
    z_copy(last_up, down_z, send_up, 0).wait_recv()
    pair_copy(last_up).start()
    last_down = lax.rem(z + half_z - 1, ring_z)
    z_copy(last_down, up_z, send_down, 0).wait_recv()
    pair_copy(last_down).start()
    for step in range(half_z):
        z_copy(lax.rem(z + ring_z - step, ring_z), up_z, send_up, step).wait_send()
        if step < half_z - 1:
            z_copy(lax.rem(z + step, ring_z), down_z, send_down, step).wait_send()

    for slot in range(ring_z):
        pair_copy(slot).wait_send()
        pair_copy(slot).wait_recv()


def ring_gather(pieces, ring_y, ring_z, collective):
    rows, lanes = pieces.shape[1], pieces.shape[2]
    return pl.pallas_call(
        functools.partial(ring_gather_kernel, ring_y, ring_z),
        out_shape=jax.ShapeDtypeStruct((2, ring_z, ring_y, rows, lanes), pieces.dtype),
        in_specs=[pl.BlockSpec(memory_space=pltpu.VMEM)],
        out_specs=pl.BlockSpec(memory_space=pltpu.VMEM),
        scratch_shapes=[
            pltpu.SemaphoreType.DMA((ring_y,)),
            pltpu.SemaphoreType.DMA((ring_y,)),
            pltpu.SemaphoreType.DMA((ring_z // 2,)),
            pltpu.SemaphoreType.DMA((ring_z // 2,)),
            pltpu.SemaphoreType.DMA((ring_z,)),
            pltpu.SemaphoreType.DMA((ring_z,)),
            pltpu.SemaphoreType.DMA((ring_z,)),
        ],
        compiler_params=pltpu.CompilerParams(collective_id=collective, has_side_effects=True),
    )(pieces)


def expert_kernel(single, x_ref, gate_ref, up_ref, down_ref, own_ref, other_ref, *scratch):
    acc_ref, rows_ref = (None,) + scratch if single else scratch
    step, last = pl.program_id(0), pl.num_programs(0) - 1

    @pl.when(step == 0)
    def _():
        rows_ref[...] = x_ref[...].reshape(rows_ref.shape)

    rows = rows_ref[...]
    gate_val = jnp.dot(rows, gate_ref[...], preferred_element_type=jnp.float32)
    up_val = jnp.dot(rows, up_ref[...], preferred_element_type=jnp.float32)
    hidden = (gate_val / (1.0 + jnp.exp(-gate_val)) * up_val).astype(jnp.bfloat16)
    term = jnp.dot(hidden, down_ref[...], preferred_element_type=jnp.float32)
    half = own_ref.shape[0]
    if acc_ref is None:
        own_ref[...] = term[:half]
        other_ref[...] = term[half:].astype(other_ref.dtype)
        return

    @pl.when(step == 0)
    def _():
        acc_ref[...] = term

    @pl.when((step > 0) & (step < last))
    def _():
        acc_ref[...] += term

    @pl.when(step == last)
    def _():
        total = acc_ref[...] + term
        own_ref[...] = total[:half]
        other_ref[...] = total[half:].astype(other_ref.dtype)


def expert(rows, gate_part, up_part, down_part, chunk=512):
    width = gate_part.shape[0]
    count = rows.size // width
    hidden = gate_part.shape[1]
    half = count // 2
    single = hidden == chunk
    accumulator = [] if single else [pltpu.VMEM((count, width), jnp.float32)]
    return pl.pallas_call(
        functools.partial(expert_kernel, single),
        out_shape=(
            jax.ShapeDtypeStruct((half, width), jnp.float32),
            jax.ShapeDtypeStruct((half, width), jnp.bfloat16),
        ),
        grid=(hidden // chunk,),
        in_specs=[
            pl.BlockSpec(rows.shape, lambda k: (0, 0, 0)),
            pl.BlockSpec((width, chunk), lambda k: (0, k)),
            pl.BlockSpec((width, chunk), lambda k: (0, k)),
            pl.BlockSpec((chunk, width), lambda k: (k, 0)),
        ],
        out_specs=(
            pl.BlockSpec((half, width), lambda k: (0, 0)),
            pl.BlockSpec((half, width), lambda k: (0, 0)),
        ),
        scratch_shapes=accumulator + [pltpu.VMEM((count, width), rows.dtype)],
        compiler_params=pltpu.CompilerParams(dimension_semantics=("arbitrary",)),
        cost_estimate=pl.CostEstimate(
            flops=6 * count * width * hidden,
            transcendentals=count * hidden,
            bytes_accessed=2 * (count * width + 3 * width * hidden) + 3 * half * width * 2,
        ),
    )(rows, gate_part, up_part, down_part)


def pair_barrier():
    me = lax.axis_index("shard")
    partner = (lax.axis_index("segment"), me + 1 - 2 * lax.rem(me, 2))
    barrier = pltpu.get_barrier_semaphore()
    pl.semaphore_signal(barrier, 1, device_id=partner, device_id_type=pl.DeviceIdType.MESH)
    pl.semaphore_wait(barrier, 1)
    return partner


def pair_gather_kernel(x_ref, o_ref, send_sem, recv_sem, local_sem):
    partner = pair_barrier()
    copy = pltpu.make_async_remote_copy(
        src_ref=x_ref,
        dst_ref=o_ref.at[1],
        send_sem=send_sem,
        recv_sem=recv_sem,
        device_id=partner,
        device_id_type=pl.DeviceIdType.MESH,
    )
    copy.start()
    local = pltpu.make_async_copy(x_ref, o_ref.at[0], local_sem)
    local.start()
    local.wait()
    copy.wait()


def pair_gather(value, collective):
    return pl.pallas_call(
        pair_gather_kernel,
        out_shape=jax.ShapeDtypeStruct((2,) + value.shape, value.dtype),
        in_specs=[pl.BlockSpec(memory_space=pltpu.VMEM)],
        out_specs=pl.BlockSpec(memory_space=pltpu.VMEM),
        scratch_shapes=[pltpu.SemaphoreType.DMA(()), pltpu.SemaphoreType.DMA(()), pltpu.SemaphoreType.DMA(())],
        compiler_params=pltpu.CompilerParams(collective_id=collective, has_side_effects=True),
    )(value)


def pair_send_kernel(x_ref, o_ref, send_sem, recv_sem):
    partner = pair_barrier()
    copy = pltpu.make_async_remote_copy(
        src_ref=x_ref,
        dst_ref=o_ref,
        send_sem=send_sem,
        recv_sem=recv_sem,
        device_id=partner,
        device_id_type=pl.DeviceIdType.MESH,
    )
    copy.start()
    copy.wait()


def pair_send(value, collective):
    return pl.pallas_call(
        pair_send_kernel,
        out_shape=jax.ShapeDtypeStruct(value.shape, value.dtype),
        in_specs=[pl.BlockSpec(memory_space=pltpu.VMEM)],
        out_specs=pl.BlockSpec(memory_space=pltpu.VMEM),
        scratch_shapes=[pltpu.SemaphoreType.DMA(()), pltpu.SemaphoreType.DMA(())],
        compiler_params=pltpu.CompilerParams(collective_id=collective, has_side_effects=True),
    )(value)


def shards(tokens, norm_gain, w_gate, w_up, w_down, block_counts, gate_prob):
    segment_index = lax.axis_index("segment")
    segment_count = lax.axis_size("segment")
    shard_count = lax.axis_size("shard")
    hidden_count = w_gate.shape[2]
    per_expert = FF // hidden_count
    zero_blocks = block_counts[0]
    row_gain = norm_gain[0]
    gate_part = w_gate[0]
    up_part = w_up[0]
    down_part = w_down[0]
    probs = gate_prob[0]
    local_rows = tokens.shape[1]
    width = tokens.shape[2]
    piece_rows = 2 * local_rows * width // LANES
    chips = shard_count // 2
    ring_z = 8
    ring_y = chips // ring_z
    carried = tokens
    stored = jnp.zeros_like(tokens)
    for tick in range(segment_count):
        normed = normalize(carried, row_gain)
        pieces = jnp.stack([normed[0:2], normed[1:3]]).reshape(2, piece_rows, LANES)
        block_rows = ring_gather(pieces, ring_y, ring_z, 0).reshape(shard_count, piece_rows, LANES)
        own_rows, other_rows = expert(block_rows, gate_part, up_part, down_part)
        chip_sum = (own_rows + pair_send(other_rows, 2).astype(jnp.float32)).astype(jnp.bfloat16)
        received = chip_exchange(chip_sum.reshape(chips, piece_rows, LANES), ring_y, ring_z, 0, 3)
        received = received.astype(jnp.float32)
        received = received.reshape(2, chips // 2, 2, local_rows, width)
        first, second = jnp.sum(received[0], axis=0), jnp.sum(received[1], axis=0)
        middle = jnp.where(zero_blocks >= 2, first[1], second[0])
        mixed = jnp.stack([first[0], middle, second[1]])
        updated = (carried.astype(jnp.float32) + probs[:, :, None] * mixed).astype(jnp.bfloat16)
        stored = jnp.where(segment_index == tick, updated, stored)
        if tick + 1 < segment_count:
            carried = shifted(updated, "segment", 1)
    return stored[None]


def solution(mesh):
    placed = (
        P(None, "shard", None),
        P("segment", None),
        P("segment", None, "shard"),
        P("segment", None, "shard"),
        P("segment", "shard", None),
        P("segment"),
        P("segment", None, "shard"),
    )
    return jax.shard_map(
        shards,
        mesh=mesh,
        in_specs=placed,
        out_specs=P("segment", None, "shard", None),
        check_vma=False,
    )
```

```python
import functools

import jax
import jax.numpy as jnp
from jax import lax
from jax.experimental import pallas as pl
from jax.experimental.pallas import tpu as pltpu
from jax.sharding import PartitionSpec as P

FF = 16384
LANES = 128


def shifted(value, axis, steps):
    count = lax.axis_size(axis)
    initial, last = (max(0, -steps), min(count, count - steps))
    return lax.ppermute(value, axis, [(source, source + steps) for source in range(initial, last)])


def normalize(rows, row_gain):
    values = rows.astype(jnp.float32)
    scale = lax.rsqrt(jnp.mean(values * values, axis=-1, keepdims=True) + 1e-05)
    return (values * scale * row_gain).astype(jnp.bfloat16)


def signed(index):
    return (index + 1) // 2 * (2 * lax.rem(index, 2) - 1)


def chip_exchange_kernel(ring_y, ring_z, per_expert, x_ref, o_ref, send_sem, recv_sem):
    me = lax.axis_index("shard")
    segment = lax.axis_index("segment")
    core = lax.rem(me, 2)
    chip = me // 2
    y, z = chip // ring_z, lax.rem(chip, ring_z)
    chips = ring_y * ring_z

    def peer(step, sign):
        z_index = lax.rem(step, ring_z)
        y_index = lax.rem(step // ring_z + z_index, ring_y)
        peer_y = lax.rem(y + sign * signed(y_index) + ring_y, ring_y)
        peer_z = lax.rem(z + sign * signed(z_index) + ring_z, ring_z)
        return peer_y * ring_z + peer_z

    def source(dest_chip):
        if per_expert:
            return x_ref.at[dest_chip // per_expert]
        return x_ref.at[lax.rem(dest_chip, ring_z) * ring_y + dest_chip // ring_z]

    def copy_of(dest_chip, slot):
        return pltpu.make_async_remote_copy(
            src_ref=source(dest_chip),
            dst_ref=o_ref.at[slot],
            send_sem=send_sem.at[dest_chip],
            recv_sem=recv_sem.at[slot],
            device_id=(segment, dest_chip * 2 + core),
            device_id_type=pl.DeviceIdType.MESH,
        )

    barrier = pltpu.get_barrier_semaphore()

    def greet(step, carry):
        dest = peer(step, 1) * 2 + core
        pl.semaphore_signal(barrier, 1, device_id=(segment, dest), device_id_type=pl.DeviceIdType.MESH)
        return carry

    lax.fori_loop(1, chips, greet, 0)
    pl.semaphore_wait(barrier, chips - 1)

    def start(step, carry):
        copy_of(peer(step, 1), chip).start()
        return carry

    lax.fori_loop(1, chips, start, 0)
    o_ref[chip] = source(chip)[...]

    def finish(step, carry):
        copy_of(peer(step, 1), chip).wait_send()
        origin = peer(step, -1)
        copy_of(origin, origin).wait_recv()
        return carry

    lax.fori_loop(1, chips, finish, 0)


def chip_exchange(pieces, ring_y, ring_z, per_expert, collective):
    rows, lanes = pieces.shape[1], pieces.shape[2]
    chips = ring_y * ring_z
    return pl.pallas_call(
        functools.partial(chip_exchange_kernel, ring_y, ring_z, per_expert),
        out_shape=jax.ShapeDtypeStruct((chips, rows, lanes), pieces.dtype),
        in_specs=[pl.BlockSpec(memory_space=pltpu.VMEM)],
        out_specs=pl.BlockSpec(memory_space=pltpu.VMEM),
        scratch_shapes=[pltpu.SemaphoreType.DMA((chips,)), pltpu.SemaphoreType.DMA((chips,))],
        compiler_params=pltpu.CompilerParams(collective_id=collective, has_side_effects=True),
    )(pieces)


def ring_gather_kernel(ring_y, ring_z, x_ref, o_ref, send_y, recv_y, send_up, send_down, recv_z, send_c, recv_c):
    me = lax.axis_index("shard")
    segment = lax.axis_index("segment")
    core = lax.rem(me, 2)
    chip = me // 2
    y, z = chip // ring_z, lax.rem(chip, ring_z)
    half_z = ring_z // 2

    def device(peer_y, peer_z):
        return (segment, (peer_y * ring_z + peer_z) * 2 + core)

    up_z, down_z = lax.rem(z + 1, ring_z), lax.rem(z + ring_z - 1, ring_z)
    partner = (segment, me + 1 - 2 * core)
    barrier = pltpu.get_barrier_semaphore()
    for step in range(1, ring_y):
        pl.semaphore_signal(barrier, 1, device_id=device(lax.rem(y + step, ring_y), z), device_id_type=pl.DeviceIdType.MESH)
    pl.semaphore_signal(barrier, 1, device_id=device(y, up_z), device_id_type=pl.DeviceIdType.MESH)
    pl.semaphore_signal(barrier, 1, device_id=device(y, down_z), device_id_type=pl.DeviceIdType.MESH)
    pl.semaphore_signal(barrier, 1, device_id=partner, device_id_type=pl.DeviceIdType.MESH)
    pl.semaphore_wait(barrier, ring_y + 2)

    def y_copy(peer_y, slot):
        return pltpu.make_async_remote_copy(
            src_ref=x_ref.at[peer_y * 2 // ring_y],
            dst_ref=o_ref.at[0, z, slot],
            send_sem=send_y.at[peer_y],
            recv_sem=recv_y.at[slot],
            device_id=device(peer_y, z),
            device_id_type=pl.DeviceIdType.MESH,
        )

    for step in range(1, ring_y):
        y_copy(lax.rem(y + step, ring_y), y).start()
    o_ref[0, z, y] = x_ref[y * 2 // ring_y]
    for step in range(1, ring_y):
        origin = lax.rem(y + ring_y - step, ring_y)
        y_copy(origin, origin).wait_recv()
        y_copy(lax.rem(y + step, ring_y), y).wait_send()

    def pair_copy(slot):
        return pltpu.make_async_remote_copy(
            src_ref=o_ref.at[0, slot],
            dst_ref=o_ref.at[1, slot],
            send_sem=send_c.at[slot],
            recv_sem=recv_c.at[slot],
            device_id=partner,
            device_id_type=pl.DeviceIdType.MESH,
        )

    pair_copy(z).start()

    def z_copy(slot, peer_z, sems, index):
        return pltpu.make_async_remote_copy(
            src_ref=o_ref.at[0, slot],
            dst_ref=o_ref.at[0, slot],
            send_sem=sems.at[index],
            recv_sem=recv_z.at[slot],
            device_id=device(y, peer_z),
            device_id_type=pl.DeviceIdType.MESH,
        )

    for step in range(half_z):
        up_slot = lax.rem(z + ring_z - step, ring_z)
        if step > 0:
            z_copy(up_slot, down_z, send_up, step).wait_recv()
            pair_copy(up_slot).start()
        z_copy(up_slot, up_z, send_up, step).start()
        if step < half_z - 1:
            down_slot = lax.rem(z + step, ring_z)
            if step > 0:
                z_copy(down_slot, up_z, send_down, step).wait_recv()
                pair_copy(down_slot).start()
            z_copy(down_slot, down_z, send_down, step).start()
    last_up = lax.rem(z + ring_z - half_z, ring_z)
    z_copy(last_up, down_z, send_up, 0).wait_recv()
    pair_copy(last_up).start()
    last_down = lax.rem(z + half_z - 1, ring_z)
    z_copy(last_down, up_z, send_down, 0).wait_recv()
    pair_copy(last_down).start()
    for step in range(half_z):
        z_copy(lax.rem(z + ring_z - step, ring_z), up_z, send_up, step).wait_send()
        if step < half_z - 1:
            z_copy(lax.rem(z + step, ring_z), down_z, send_down, step).wait_send()

    for slot in range(ring_z):
        pair_copy(slot).wait_send()
        pair_copy(slot).wait_recv()


def ring_gather(pieces, ring_y, ring_z, collective):
    rows, lanes = pieces.shape[1], pieces.shape[2]
    return pl.pallas_call(
        functools.partial(ring_gather_kernel, ring_y, ring_z),
        out_shape=jax.ShapeDtypeStruct((2, ring_z, ring_y, rows, lanes), pieces.dtype),
        in_specs=[pl.BlockSpec(memory_space=pltpu.VMEM)],
        out_specs=pl.BlockSpec(memory_space=pltpu.VMEM),
        scratch_shapes=[
            pltpu.SemaphoreType.DMA((ring_y,)),
            pltpu.SemaphoreType.DMA((ring_y,)),
            pltpu.SemaphoreType.DMA((ring_z // 2,)),
            pltpu.SemaphoreType.DMA((ring_z // 2,)),
            pltpu.SemaphoreType.DMA((ring_z,)),
            pltpu.SemaphoreType.DMA((ring_z,)),
            pltpu.SemaphoreType.DMA((ring_z,)),
        ],
        compiler_params=pltpu.CompilerParams(collective_id=collective, has_side_effects=True),
    )(pieces)


def expert_kernel(single, x_ref, gate_ref, up_ref, down_ref, own_ref, other_ref, *scratch):
    acc_ref, rows_ref = (None,) + scratch if single else scratch
    step, last = pl.program_id(0), pl.num_programs(0) - 1

    @pl.when(step == 0)
    def _():
        rows_ref[...] = x_ref[...].reshape(rows_ref.shape)

    rows = rows_ref[...]
    gate_val = jnp.dot(rows, gate_ref[...], preferred_element_type=jnp.float32)
    up_val = jnp.dot(rows, up_ref[...], preferred_element_type=jnp.float32)
    hidden = (gate_val / (1.0 + jnp.exp(-gate_val)) * up_val).astype(jnp.bfloat16)
    term = jnp.dot(hidden, down_ref[...], preferred_element_type=jnp.float32)
    half = own_ref.shape[0]
    if acc_ref is None:
        own_ref[...] = term[:half]
        other_ref[...] = term[half:].astype(other_ref.dtype)
        return

    @pl.when(step == 0)
    def _():
        acc_ref[...] = term

    @pl.when((step > 0) & (step < last))
    def _():
        acc_ref[...] += term

    @pl.when(step == last)
    def _():
        total = acc_ref[...] + term
        own_ref[...] = total[:half]
        other_ref[...] = total[half:].astype(other_ref.dtype)


def expert(rows, gate_part, up_part, down_part, chunk=512):
    width = gate_part.shape[0]
    count = rows.size // width
    hidden = gate_part.shape[1]
    half = count // 2
    single = hidden == chunk
    accumulator = [] if single else [pltpu.VMEM((count, width), jnp.float32)]
    return pl.pallas_call(
        functools.partial(expert_kernel, single),
        out_shape=(
            jax.ShapeDtypeStruct((half, width), jnp.float32),
            jax.ShapeDtypeStruct((half, width), jnp.bfloat16),
        ),
        grid=(hidden // chunk,),
        in_specs=[
            pl.BlockSpec(rows.shape, lambda k: (0, 0, 0)),
            pl.BlockSpec((width, chunk), lambda k: (0, k)),
            pl.BlockSpec((width, chunk), lambda k: (0, k)),
            pl.BlockSpec((chunk, width), lambda k: (k, 0)),
        ],
        out_specs=(
            pl.BlockSpec((half, width), lambda k: (0, 0)),
            pl.BlockSpec((half, width), lambda k: (0, 0)),
        ),
        scratch_shapes=accumulator + [pltpu.VMEM((count, width), rows.dtype)],
        compiler_params=pltpu.CompilerParams(dimension_semantics=("arbitrary",)),
        cost_estimate=pl.CostEstimate(
            flops=6 * count * width * hidden,
            transcendentals=count * hidden,
            bytes_accessed=2 * (count * width + 3 * width * hidden) + 3 * half * width * 2,
        ),
    )(rows, gate_part, up_part, down_part)


def pair_barrier():
    me = lax.axis_index("shard")
    partner = (lax.axis_index("segment"), me + 1 - 2 * lax.rem(me, 2))
    barrier = pltpu.get_barrier_semaphore()
    pl.semaphore_signal(barrier, 1, device_id=partner, device_id_type=pl.DeviceIdType.MESH)
    pl.semaphore_wait(barrier, 1)
    return partner


def pair_gather_kernel(x_ref, o_ref, send_sem, recv_sem, local_sem):
    partner = pair_barrier()
    copy = pltpu.make_async_remote_copy(
        src_ref=x_ref,
        dst_ref=o_ref.at[1],
        send_sem=send_sem,
        recv_sem=recv_sem,
        device_id=partner,
        device_id_type=pl.DeviceIdType.MESH,
    )
    copy.start()
    local = pltpu.make_async_copy(x_ref, o_ref.at[0], local_sem)
    local.start()
    local.wait()
    copy.wait()


def pair_gather(value, collective):
    return pl.pallas_call(
        pair_gather_kernel,
        out_shape=jax.ShapeDtypeStruct((2,) + value.shape, value.dtype),
        in_specs=[pl.BlockSpec(memory_space=pltpu.VMEM)],
        out_specs=pl.BlockSpec(memory_space=pltpu.VMEM),
        scratch_shapes=[pltpu.SemaphoreType.DMA(()), pltpu.SemaphoreType.DMA(()), pltpu.SemaphoreType.DMA(())],
        compiler_params=pltpu.CompilerParams(collective_id=collective, has_side_effects=True),
    )(value)


def pair_send_kernel(x_ref, o_ref, send_sem, recv_sem):
    partner = pair_barrier()
    copy = pltpu.make_async_remote_copy(
        src_ref=x_ref,
        dst_ref=o_ref,
        send_sem=send_sem,
        recv_sem=recv_sem,
        device_id=partner,
        device_id_type=pl.DeviceIdType.MESH,
    )
    copy.start()
    copy.wait()


def pair_send(value, collective):
    return pl.pallas_call(
        pair_send_kernel,
        out_shape=jax.ShapeDtypeStruct(value.shape, value.dtype),
        in_specs=[pl.BlockSpec(memory_space=pltpu.VMEM)],
        out_specs=pl.BlockSpec(memory_space=pltpu.VMEM),
        scratch_shapes=[pltpu.SemaphoreType.DMA(()), pltpu.SemaphoreType.DMA(())],
        compiler_params=pltpu.CompilerParams(collective_id=collective, has_side_effects=True),
    )(value)


def shards(tokens, norm_gain, w_gate, w_up, w_down, block_counts, gate_prob):
    segment_index = lax.axis_index("segment")
    segment_count = lax.axis_size("segment")
    shard_count = lax.axis_size("shard")
    hidden_count = w_gate.shape[2]
    per_expert = FF // hidden_count
    zero_blocks = block_counts[0]
    row_gain = norm_gain[0]
    gate_part = w_gate[0]
    up_part = w_up[0]
    down_part = w_down[0]
    probs = gate_prob[0]
    local_rows = tokens.shape[1]
    width = tokens.shape[2]
    piece_rows = 2 * local_rows * width // LANES
    chips = shard_count // 2
    ring_z = 8
    ring_y = chips // ring_z
    carried = tokens
    stored = jnp.zeros_like(tokens)
    for tick in range(segment_count):
        normed = normalize(carried, row_gain)
        pieces = jnp.stack([normed[0:2], normed[1:3]]).reshape(2, piece_rows, LANES)
        block_rows = ring_gather(pieces, ring_y, ring_z, 0).reshape(shard_count, piece_rows, LANES)
        own_rows, other_rows = expert(block_rows, gate_part, up_part, down_part)
        chip_sum = (own_rows + pair_send(other_rows, 2).astype(jnp.float32)).astype(jnp.bfloat16)
        received = chip_exchange(chip_sum.reshape(chips, piece_rows, LANES), ring_y, ring_z, 0, 3)
        received = received.reshape(2, chips // 2, 2, local_rows, width)
        first = jnp.sum(received[0], axis=0, dtype=jnp.float32)
        second = jnp.sum(received[1], axis=0, dtype=jnp.float32)
        middle = jnp.where(zero_blocks >= 2, first[1], second[0])
        mixed = jnp.stack([first[0], middle, second[1]])
        updated = (carried.astype(jnp.float32) + probs[:, :, None] * mixed).astype(jnp.bfloat16)
        stored = jnp.where(segment_index == tick, updated, stored)
        if tick + 1 < segment_count:
            carried = shifted(updated, "segment", 1)
    return stored[None]


def solution(mesh):
    placed = (
        P(None, "shard", None),
        P("segment", None),
        P("segment", None, "shard"),
        P("segment", None, "shard"),
        P("segment", "shard", None),
        P("segment"),
        P("segment", None, "shard"),
    )
    return jax.shard_map(
        shards,
        mesh=mesh,
        in_specs=placed,
        out_specs=P("segment", None, "shard", None),
        check_vma=False,
    )
```

```python
import functools

import jax
import jax.numpy as jnp
from jax import lax
from jax.experimental import pallas as pl
from jax.experimental.pallas import tpu as pltpu
from jax.sharding import PartitionSpec as P

FF = 16384
LANES = 128


def shifted(value, axis, steps):
    count = lax.axis_size(axis)
    initial, last = (max(0, -steps), min(count, count - steps))
    return lax.ppermute(value, axis, [(source, source + steps) for source in range(initial, last)])


def normalize(rows, row_gain):
    values = rows.astype(jnp.float32)
    scale = lax.rsqrt(jnp.mean(values * values, axis=-1, keepdims=True) + 1e-05)
    return (values * scale * row_gain).astype(jnp.bfloat16)


def signed(index):
    return (index + 1) // 2 * (2 * lax.rem(index, 2) - 1)


def chip_exchange_kernel(ring_y, ring_z, per_expert, x_ref, o_ref, send_sem, recv_sem):
    me = lax.axis_index("shard")
    segment = lax.axis_index("segment")
    core = lax.rem(me, 2)
    chip = me // 2
    y, z = chip // ring_z, lax.rem(chip, ring_z)
    chips = ring_y * ring_z

    def peer(step, sign):
        z_index = lax.rem(step, ring_z)
        y_index = lax.rem(step // ring_z + z_index, ring_y)
        peer_y = lax.rem(y + sign * signed(y_index) + ring_y, ring_y)
        peer_z = lax.rem(z + sign * signed(z_index) + ring_z, ring_z)
        return peer_y * ring_z + peer_z

    def source(dest_chip):
        if per_expert:
            return x_ref.at[dest_chip // per_expert]
        return x_ref.at[lax.rem(dest_chip, ring_z) * ring_y + dest_chip // ring_z]

    def copy_of(dest_chip, slot):
        return pltpu.make_async_remote_copy(
            src_ref=source(dest_chip),
            dst_ref=o_ref.at[slot],
            send_sem=send_sem.at[dest_chip],
            recv_sem=recv_sem.at[slot],
            device_id=(segment, dest_chip * 2 + core),
            device_id_type=pl.DeviceIdType.MESH,
        )

    barrier = pltpu.get_barrier_semaphore()

    def greet(step, carry):
        dest = peer(step, 1) * 2 + core
        pl.semaphore_signal(barrier, 1, device_id=(segment, dest), device_id_type=pl.DeviceIdType.MESH)
        return carry

    lax.fori_loop(1, chips, greet, 0)
    pl.semaphore_wait(barrier, chips - 1)

    def start(step, carry):
        copy_of(peer(step, 1), chip).start()
        return carry

    lax.fori_loop(1, chips, start, 0)
    o_ref[chip] = source(chip)[...]

    def finish(step, carry):
        copy_of(peer(step, 1), chip).wait_send()
        origin = peer(step, -1)
        copy_of(origin, origin).wait_recv()
        return carry

    lax.fori_loop(1, chips, finish, 0)


def chip_exchange(pieces, ring_y, ring_z, per_expert, collective):
    rows, lanes = pieces.shape[1], pieces.shape[2]
    chips = ring_y * ring_z
    return pl.pallas_call(
        functools.partial(chip_exchange_kernel, ring_y, ring_z, per_expert),
        out_shape=jax.ShapeDtypeStruct((chips, rows, lanes), pieces.dtype),
        in_specs=[pl.BlockSpec(memory_space=pltpu.VMEM)],
        out_specs=pl.BlockSpec(memory_space=pltpu.VMEM),
        scratch_shapes=[pltpu.SemaphoreType.DMA((chips,)), pltpu.SemaphoreType.DMA((chips,))],
        compiler_params=pltpu.CompilerParams(collective_id=collective, has_side_effects=True),
    )(pieces)


def ring_gather_kernel(ring_y, ring_z, x_ref, o_ref, send_y, recv_y, send_up, send_down, recv_z, send_c, recv_c):
    me = lax.axis_index("shard")
    segment = lax.axis_index("segment")
    core = lax.rem(me, 2)
    chip = me // 2
    y, z = chip // ring_z, lax.rem(chip, ring_z)
    half_z = ring_z // 2

    def device(peer_y, peer_z):
        return (segment, (peer_y * ring_z + peer_z) * 2 + core)

    up_z, down_z = lax.rem(z + 1, ring_z), lax.rem(z + ring_z - 1, ring_z)
    partner = (segment, me + 1 - 2 * core)
    barrier = pltpu.get_barrier_semaphore()
    for step in range(1, ring_y):
        pl.semaphore_signal(barrier, 1, device_id=device(lax.rem(y + step, ring_y), z), device_id_type=pl.DeviceIdType.MESH)
    pl.semaphore_signal(barrier, 1, device_id=device(y, up_z), device_id_type=pl.DeviceIdType.MESH)
    pl.semaphore_signal(barrier, 1, device_id=device(y, down_z), device_id_type=pl.DeviceIdType.MESH)
    pl.semaphore_signal(barrier, 1, device_id=partner, device_id_type=pl.DeviceIdType.MESH)
    pl.semaphore_wait(barrier, ring_y + 2)

    def y_copy(peer_y, slot):
        return pltpu.make_async_remote_copy(
            src_ref=x_ref.at[peer_y * 2 // ring_y],
            dst_ref=o_ref.at[0, z, slot],
            send_sem=send_y.at[peer_y],
            recv_sem=recv_y.at[slot],
            device_id=device(peer_y, z),
            device_id_type=pl.DeviceIdType.MESH,
        )

    y_order = [ring_y // 2] + [step for step in range(1, ring_y) if step != ring_y // 2]
    for step in y_order:
        y_copy(lax.rem(y + step, ring_y), y).start()
    o_ref[0, z, y] = x_ref[y * 2 // ring_y]
    for step in range(1, ring_y):
        origin = lax.rem(y + ring_y - step, ring_y)
        y_copy(origin, origin).wait_recv()
        y_copy(lax.rem(y + step, ring_y), y).wait_send()

    def pair_copy(slot):
        return pltpu.make_async_remote_copy(
            src_ref=o_ref.at[0, slot],
            dst_ref=o_ref.at[1, slot],
            send_sem=send_c.at[slot],
            recv_sem=recv_c.at[slot],
            device_id=partner,
            device_id_type=pl.DeviceIdType.MESH,
        )

    pair_copy(z).start()

    def z_copy(slot, peer_z, sems, index):
        return pltpu.make_async_remote_copy(
            src_ref=o_ref.at[0, slot],
            dst_ref=o_ref.at[0, slot],
            send_sem=sems.at[index],
            recv_sem=recv_z.at[slot],
            device_id=device(y, peer_z),
            device_id_type=pl.DeviceIdType.MESH,
        )

    for step in range(half_z):
        up_slot = lax.rem(z + ring_z - step, ring_z)
        if step > 0:
            z_copy(up_slot, down_z, send_up, step).wait_recv()
            pair_copy(up_slot).start()
        z_copy(up_slot, up_z, send_up, step).start()
        if step < half_z - 1:
            down_slot = lax.rem(z + step, ring_z)
            if step > 0:
                z_copy(down_slot, up_z, send_down, step).wait_recv()
                pair_copy(down_slot).start()
            z_copy(down_slot, down_z, send_down, step).start()
    last_up = lax.rem(z + ring_z - half_z, ring_z)
    z_copy(last_up, down_z, send_up, 0).wait_recv()
    pair_copy(last_up).start()
    last_down = lax.rem(z + half_z - 1, ring_z)
    z_copy(last_down, up_z, send_down, 0).wait_recv()
    pair_copy(last_down).start()
    for step in range(half_z):
        z_copy(lax.rem(z + ring_z - step, ring_z), up_z, send_up, step).wait_send()
        if step < half_z - 1:
            z_copy(lax.rem(z + step, ring_z), down_z, send_down, step).wait_send()

    for slot in range(ring_z):
        pair_copy(slot).wait_send()
        pair_copy(slot).wait_recv()


def ring_gather(pieces, ring_y, ring_z, collective):
    rows, lanes = pieces.shape[1], pieces.shape[2]
    return pl.pallas_call(
        functools.partial(ring_gather_kernel, ring_y, ring_z),
        out_shape=jax.ShapeDtypeStruct((2, ring_z, ring_y, rows, lanes), pieces.dtype),
        in_specs=[pl.BlockSpec(memory_space=pltpu.VMEM)],
        out_specs=pl.BlockSpec(memory_space=pltpu.VMEM),
        scratch_shapes=[
            pltpu.SemaphoreType.DMA((ring_y,)),
            pltpu.SemaphoreType.DMA((ring_y,)),
            pltpu.SemaphoreType.DMA((ring_z // 2,)),
            pltpu.SemaphoreType.DMA((ring_z // 2,)),
            pltpu.SemaphoreType.DMA((ring_z,)),
            pltpu.SemaphoreType.DMA((ring_z,)),
            pltpu.SemaphoreType.DMA((ring_z,)),
        ],
        compiler_params=pltpu.CompilerParams(collective_id=collective, has_side_effects=True),
    )(pieces)


def expert_kernel(single, x_ref, gate_ref, up_ref, down_ref, own_ref, other_ref, *scratch):
    acc_ref, rows_ref = (None,) + scratch if single else scratch
    step, last = pl.program_id(0), pl.num_programs(0) - 1

    @pl.when(step == 0)
    def _():
        rows_ref[...] = x_ref[...].reshape(rows_ref.shape)

    rows = rows_ref[...]
    gate_val = jnp.dot(rows, gate_ref[...], preferred_element_type=jnp.float32)
    up_val = jnp.dot(rows, up_ref[...], preferred_element_type=jnp.float32)
    hidden = (gate_val / (1.0 + jnp.exp(-gate_val)) * up_val).astype(jnp.bfloat16)
    term = jnp.dot(hidden, down_ref[...], preferred_element_type=jnp.float32)
    half = own_ref.shape[0]
    if acc_ref is None:
        own_ref[...] = term[:half]
        other_ref[...] = term[half:].astype(other_ref.dtype)
        return

    @pl.when(step == 0)
    def _():
        acc_ref[...] = term

    @pl.when((step > 0) & (step < last))
    def _():
        acc_ref[...] += term

    @pl.when(step == last)
    def _():
        total = acc_ref[...] + term
        own_ref[...] = total[:half]
        other_ref[...] = total[half:].astype(other_ref.dtype)


def expert(rows, gate_part, up_part, down_part, chunk=512):
    width = gate_part.shape[0]
    count = rows.size // width
    hidden = gate_part.shape[1]
    half = count // 2
    single = hidden == chunk
    accumulator = [] if single else [pltpu.VMEM((count, width), jnp.float32)]
    return pl.pallas_call(
        functools.partial(expert_kernel, single),
        out_shape=(
            jax.ShapeDtypeStruct((half, width), jnp.float32),
            jax.ShapeDtypeStruct((half, width), jnp.bfloat16),
        ),
        grid=(hidden // chunk,),
        in_specs=[
            pl.BlockSpec(rows.shape, lambda k: (0, 0, 0)),
            pl.BlockSpec((width, chunk), lambda k: (0, k)),
            pl.BlockSpec((width, chunk), lambda k: (0, k)),
            pl.BlockSpec((chunk, width), lambda k: (k, 0)),
        ],
        out_specs=(
            pl.BlockSpec((half, width), lambda k: (0, 0)),
            pl.BlockSpec((half, width), lambda k: (0, 0)),
        ),
        scratch_shapes=accumulator + [pltpu.VMEM((count, width), rows.dtype)],
        compiler_params=pltpu.CompilerParams(dimension_semantics=("arbitrary",)),
        cost_estimate=pl.CostEstimate(
            flops=6 * count * width * hidden,
            transcendentals=count * hidden,
            bytes_accessed=2 * (count * width + 3 * width * hidden) + 3 * half * width * 2,
        ),
    )(rows, gate_part, up_part, down_part)


def pair_barrier():
    me = lax.axis_index("shard")
    partner = (lax.axis_index("segment"), me + 1 - 2 * lax.rem(me, 2))
    barrier = pltpu.get_barrier_semaphore()
    pl.semaphore_signal(barrier, 1, device_id=partner, device_id_type=pl.DeviceIdType.MESH)
    pl.semaphore_wait(barrier, 1)
    return partner


def pair_gather_kernel(x_ref, o_ref, send_sem, recv_sem, local_sem):
    partner = pair_barrier()
    copy = pltpu.make_async_remote_copy(
        src_ref=x_ref,
        dst_ref=o_ref.at[1],
        send_sem=send_sem,
        recv_sem=recv_sem,
        device_id=partner,
        device_id_type=pl.DeviceIdType.MESH,
    )
    copy.start()
    local = pltpu.make_async_copy(x_ref, o_ref.at[0], local_sem)
    local.start()
    local.wait()
    copy.wait()


def pair_gather(value, collective):
    return pl.pallas_call(
        pair_gather_kernel,
        out_shape=jax.ShapeDtypeStruct((2,) + value.shape, value.dtype),
        in_specs=[pl.BlockSpec(memory_space=pltpu.VMEM)],
        out_specs=pl.BlockSpec(memory_space=pltpu.VMEM),
        scratch_shapes=[pltpu.SemaphoreType.DMA(()), pltpu.SemaphoreType.DMA(()), pltpu.SemaphoreType.DMA(())],
        compiler_params=pltpu.CompilerParams(collective_id=collective, has_side_effects=True),
    )(value)


def pair_send_kernel(x_ref, o_ref, send_sem, recv_sem):
    partner = pair_barrier()
    copy = pltpu.make_async_remote_copy(
        src_ref=x_ref,
        dst_ref=o_ref,
        send_sem=send_sem,
        recv_sem=recv_sem,
        device_id=partner,
        device_id_type=pl.DeviceIdType.MESH,
    )
    copy.start()
    copy.wait()


def pair_send(value, collective):
    return pl.pallas_call(
        pair_send_kernel,
        out_shape=jax.ShapeDtypeStruct(value.shape, value.dtype),
        in_specs=[pl.BlockSpec(memory_space=pltpu.VMEM)],
        out_specs=pl.BlockSpec(memory_space=pltpu.VMEM),
        scratch_shapes=[pltpu.SemaphoreType.DMA(()), pltpu.SemaphoreType.DMA(())],
        compiler_params=pltpu.CompilerParams(collective_id=collective, has_side_effects=True),
    )(value)


def shards(tokens, norm_gain, w_gate, w_up, w_down, block_counts, gate_prob):
    segment_index = lax.axis_index("segment")
    segment_count = lax.axis_size("segment")
    shard_count = lax.axis_size("shard")
    hidden_count = w_gate.shape[2]
    per_expert = FF // hidden_count
    zero_blocks = block_counts[0]
    row_gain = norm_gain[0]
    gate_part = w_gate[0]
    up_part = w_up[0]
    down_part = w_down[0]
    probs = gate_prob[0]
    local_rows = tokens.shape[1]
    width = tokens.shape[2]
    piece_rows = 2 * local_rows * width // LANES
    chips = shard_count // 2
    ring_z = 8
    ring_y = chips // ring_z
    carried = tokens
    stored = jnp.zeros_like(tokens)
    for tick in range(segment_count):
        normed = normalize(carried, row_gain)
        pieces = jnp.stack([normed[0:2], normed[1:3]]).reshape(2, piece_rows, LANES)
        block_rows = ring_gather(pieces, ring_y, ring_z, 0).reshape(shard_count, piece_rows, LANES)
        own_rows, other_rows = expert(block_rows, gate_part, up_part, down_part)
        chip_sum = (own_rows + pair_send(other_rows, 2).astype(jnp.float32)).astype(jnp.bfloat16)
        received = chip_exchange(chip_sum.reshape(chips, piece_rows, LANES), ring_y, ring_z, 0, 3)
        received = received.reshape(2, chips // 2, 2, local_rows, width)
        first = jnp.sum(received[0], axis=0, dtype=jnp.float32)
        second = jnp.sum(received[1], axis=0, dtype=jnp.float32)
        middle = jnp.where(zero_blocks >= 2, first[1], second[0])
        mixed = jnp.stack([first[0], middle, second[1]])
        updated = (carried.astype(jnp.float32) + probs[:, :, None] * mixed).astype(jnp.bfloat16)
        stored = jnp.where(segment_index == tick, updated, stored)
        if tick + 1 < segment_count:
            carried = shifted(updated, "segment", 1)
    return stored[None]


def solution(mesh):
    placed = (
        P(None, "shard", None),
        P("segment", None),
        P("segment", None, "shard"),
        P("segment", None, "shard"),
        P("segment", "shard", None),
        P("segment"),
        P("segment", None, "shard"),
    )
    return jax.shard_map(
        shards,
        mesh=mesh,
        in_specs=placed,
        out_specs=P("segment", None, "shard", None),
        check_vma=False,
    )
```
